32 devices in a mesh: pipe: 4 (over z), ctx: 8 (over y, x, core).
Axes of the slice: x: 2, y: 2, z: 4, core: 2. Of those that a mesh axis runs over, the one named last changes fastest.
Arguments:
- queries: bfloat16 [4, 2048, 4096], P('pipe', 'ctx'), may hold values from -110 to 110
- keys: bfloat16 [4, 2048, 512], P('pipe', 'ctx'), may hold values from -4 to 4
- values: bfloat16 [4, 2048, 512], P('pipe', 'ctx'), may hold values from -6 to 6
- doc_ids: int32 [4, 8], P('pipe'), may hold values from 0 to 1, never falling along the last dimension, each value on 1 to 5 neighbouring positions
Outputs:
- handed: bfloat16 [4, 2048, 4096], P('pipe', 'ctx')
The draws below stay inside these ranges and needn't reach their ends.
Inputs may be any that keep to these rules, and one draw needn't show every extreme that they name: doc_ids never falls along a section's blocks; each document spans 1 to 5 blocks.
All inputs are finite; a program needn't handle non-finite values.
Results may differ from the reference program's by a relative error of at most 0.004.
Values may be sent and summed in bfloat16 or wider, within the bound.
A program may use at most 320 MiB of HBM per device.

```python
import math
import jax
import jax.numpy as jnp
import numpy as np
from jax import lax

HQ = 32
HK = 4
DH = 128
TOK_DEV = 256
SECTIONS = 4
SEQ = 2048
DOC_MOST = 5
DOC_COUNT = 2
N_CTX = 8


def key_field(key):
    field = jax.random.normal(jax.random.fold_in(key, 11), (SECTIONS, SEQ, HK * DH), jnp.float32)
    return jnp.clip(field, -4.0, 4.0)


def draw_keys(key, part):
    field = key_field(key)
    return field.astype(jnp.bfloat16)


def draw_queries(key, part):
    field = jax.random.normal(jax.random.fold_in(key, 23), (SECTIONS, SEQ, HQ * DH), jnp.float32)
    field = jnp.clip(field, -4.0, 4.0)
    return field.astype(jnp.bfloat16)


def block_scale(own_key, extent, split, smallest, top_value):
    factor_of = 1.0
    for axis_at, blocks in split:
        draws = jax.random.uniform(jax.random.fold_in(jax.random.fold_in(own_key, 6), axis_at), (blocks,), jnp.float32, smallest / len(split), top_value / len(split))
        factor_of = factor_of * jnp.repeat(jnp.exp(draws), extent[axis_at] // blocks).reshape((-1,) + (1,) * (len(extent) - 1 - axis_at))
    return factor_of


def profile(number_of, total, reach, skew):
    loads = [(1 << 20) // math.isqrt(grade ** skew) + 1 for grade in range(2, number_of + 1)]
    spare, given = total - reach - (number_of - 1), [1] * (number_of - 1)
    while spare > 0:
        candidates = [i for i in range(number_of - 1) if given[i] < reach]
        mass, budget = sum([loads[i] for i in candidates]), spare
        for i in candidates:
            more = min(reach - given[i], max(1, budget * loads[i] // mass), spare)
            given[i] = given[i] + more
            spare = spare - more
    return np.array([reach] + given)


def uneven(own_key, count, total, reach, slope):
    if count == 2:
        one = jax.random.randint(own_key, (), max(1, total - reach), min(reach, total - 1) + 1)
        return jnp.stack([one, total - one])
    tallies = jnp.asarray(profile(count, total, reach, slope), jnp.int32)
    couples = (count - 1) // 2
    giver, sink = tallies[1:1 + 2 * couples:2], tallies[2:2 + 2 * couples:2]
    room = jnp.minimum(giver - 1, reach - sink)
    shifted = jax.random.randint(jax.random.fold_in(own_key, 1), (couples,), 0, 1 << 20) % (room + 1)
    tallies = tallies.at[1:1 + 2 * couples:2].set(giver - shifted).at[2:2 + 2 * couples:2].set(sink + shifted)
    return tallies[jax.random.permutation(jax.random.fold_in(own_key, 2), count)]


def bell_draw(key, shape, width, most, pieces=(), held_as=jnp.bfloat16):
    gain = block_scale(key, shape, pieces, -0.22, 0.18) if pieces else 1.0
    values = jax.random.normal(key, shape, jnp.float32) * width * gain
    return jnp.minimum(jnp.maximum(values, -most), most).astype(held_as)


def setup_inputs(seed: int = 0) -> dict:
    key_list = jax.random.split(jax.random.key(seed), 5)
    return {
        "queries": draw_queries(jax.random.fold_in(key_list[4], 71), 0),
        "keys": draw_keys(jax.random.fold_in(key_list[4], 71), 0),
        "values": bell_draw(key_list[2], (SECTIONS, SEQ, HK * DH), 1.0, 6.0, ((0, 4), (1, 8))),
        "doc_ids": jax.vmap(lambda own: jnp.searchsorted(jnp.cumsum(uneven(own, DOC_COUNT, N_CTX, DOC_MOST, 0)), jnp.arange(N_CTX), side="right"))(jax.random.split(key_list[3], SECTIONS)).reshape((SECTIONS, N_CTX)).astype(jnp.int32),
    }


def reference(queries, keys, values, doc_ids):
    per_group = HQ // HK
    score_scale = 1.0 / math.sqrt(DH)

    def one_section(section_in):
        q_sec, k_sec, v_sec, doc_row = section_in
        key_heads = k_sec.astype(jnp.float32).reshape(SEQ, HK, DH)
        value_heads = v_sec.astype(jnp.float32).reshape(SEQ, HK, DH)
        key_pos = jnp.arange(SEQ, dtype=jnp.int32)
        key_doc = doc_row[(key_pos // TOK_DEV).astype(jnp.int32)]
        q_blocks = q_sec.reshape(N_CTX, TOK_DEV, HK, per_group, DH)

        def one_block(block_in):
            q_blk, blk_index = block_in
            query_pos = blk_index * TOK_DEV + jnp.arange(TOK_DEV, dtype=jnp.int32)
            scores = jnp.einsum('qhgd,khd->hgqk', q_blk.astype(jnp.float32), key_heads) * score_scale
            own_doc = doc_row[blk_index]
            visible = (key_doc[None, :] == own_doc) & (key_pos[None, :] <= query_pos[:, None])
            masked = jnp.where(visible, scores, -1e+30)
            row_top = lax.optimization_barrier(jnp.max(masked, axis=-1, keepdims=True))
            weights = jnp.where(visible, jnp.exp(masked - row_top), 0.0)
            row_total = lax.optimization_barrier(jnp.sum(weights, axis=-1, keepdims=True))
            rounded = lax.optimization_barrier(weights.astype(jnp.bfloat16))
            summed = jnp.einsum('hgqk,khd->hgqd', rounded.astype(jnp.float32), value_heads)
            attended = summed / row_total
            return attended.transpose(2, 0, 1, 3).reshape(TOK_DEV, HQ * DH).astype(jnp.bfloat16)
        blocks_out = lax.map(one_block, (q_blocks, jnp.arange(N_CTX, dtype=jnp.int32)))
        return blocks_out.reshape(SEQ, HQ * DH)
    attended_all = lax.map(one_section, (queries, keys, values, doc_ids))
    return jnp.roll(attended_all, 1, axis=0)
```

```python
import functools
import math

import jax
import jax.numpy as jnp
from jax import lax
from jax.experimental import pallas as pl
from jax.experimental.pallas import tpu as pltpu
from jax.sharding import PartitionSpec as P

HQ = 32
HK = 4
DH = 128
PER_GROUP = HQ // HK
STEP_HEADS = 2
SENT_STEPS = 2
HIDDEN = 1e30
MESH = pl.DeviceIdType.MESH


def kernel(
    n_pipe,
    n_ctx,
    window,
    rows,
    doc_hbm,
    q_ref,
    k_ref,
    v_ref,
    out_ref,
    qbuf,
    kbuf,
    vbuf,
    obuf,
    bias,
    doc_ref,
    doc_sem,
    q_sem,
    own_sem,
    kv_send,
    kv_recv,
    z_send,
    z_recv,
    o_send,
    o_recv,
    go_sem,
):
    pipe = lax.axis_index("pipe")
    ctx = lax.axis_index("ctx")
    right = lax.rem(pipe + 1, n_pipe)
    left = lax.rem(pipe + n_pipe - 1, n_pipe)
    moved = HK - 1
    group_cols = PER_GROUP * DH
    step_cols = STEP_HEADS * DH
    steps = HQ // STEP_HEADS
    group_steps = PER_GROUP // STEP_HEADS
    sent_steps = moved * group_steps
    sent_cols = SENT_STEPS * step_cols
    last = window - 1

    core = lax.rem(ctx, 2)
    odd_chip = lax.rem(ctx // 2, 2) == 1
    even_chip = lax.rem(ctx // 2, 2) == 0
    turn = 1 - 2 * core
    sibling = ctx + turn
    barrier = pltpu.get_barrier_semaphore()
    ends = pipe == n_pipe - 1
    guides = pipe == n_pipe - 2
    hall = jnp.where(ends, left, pipe)

    def greet(pipe_to, ctx_to):
        pl.semaphore_signal(barrier, inc=1, device_id=(pipe_to, ctx_to), device_id_type=MESH)

    greet(left, ctx)
    pl.when((core == 1) | (ctx >= 2))(lambda: greet(hall, sibling))
    pl.when(odd_chip)(lambda: greet(hall, lax.rem(ctx + n_ctx - 2, n_ctx)))
    pl.when(even_chip & (ctx >= 2))(lambda: greet(hall, lax.rem(ctx + 2, n_ctx)))
    met = jnp.where((core == 0) | (ctx >= 2), 1, 0)
    met = met + jnp.where(even_chip, 1, 0) + jnp.where(odd_chip & (ctx >= 4), 1, 0)
    for d in range(4, window, 2):
        pl.when(ctx >= d)(lambda d=d: greet(hall, lax.rem(ctx + n_ctx - d, n_ctx)))
        met = met + jnp.where(ctx + d < n_ctx, 1, 0)
    met = 1 + jnp.where(ends, 0, jnp.where(guides, 2 * met, met))

    def own_copies(g):
        cols = pl.ds(pl.multiple_of(g * DH, DH), DH)
        place = pl.ds(last * rows, rows)
        return (
            pltpu.make_async_copy(k_ref.at[:, cols], kbuf.at[g, place], own_sem.at[0, g]),
            pltpu.make_async_copy(v_ref.at[:, cols], vbuf.at[g, place], own_sem.at[1, g]),
        )

    def q_copy(g):
        cols = pl.ds(pl.multiple_of(g * group_cols, group_cols), group_cols)
        return pltpu.make_async_copy(q_ref.at[:, cols], qbuf.at[:, cols], q_sem.at[g])

    def kv_copies(g, source, target, ctx_to):
        from_rows = pl.ds(pl.multiple_of((last - source) * rows, rows), rows)
        to_rows = pl.ds(pl.multiple_of((last - target) * rows, rows), rows)
        return [
            pltpu.make_async_remote_copy(
                src_ref=buf.at[g, from_rows],
                dst_ref=buf.at[g, to_rows],
                send_sem=kv_send.at[which, g, target - 1],
                recv_sem=kv_recv.at[which, g, target - 1],
                device_id=(pipe, ctx_to),
                device_id_type=MESH,
            )
            for which, buf in ((0, kbuf), (1, vbuf))
        ]

    def direct(g, d):
        return kv_copies(g, 0, d, lax.rem(ctx + d, n_ctx))

    def relay(g, d):
        return kv_copies(g, d, d + turn, sibling)

    def forward(g, d):
        return kv_copies(g, d, d - 2, lax.rem(ctx + n_ctx - 2, n_ctx))

    def for_direct(do):
        for d in range(2, window, 2):
            fits = even_chip if d == 2 else ctx + d < n_ctx
            pl.when(fits)(functools.partial(do, d))

    def for_forward(do):
        pl.when(odd_chip & (ctx >= 4))(functools.partial(do, 4))

    def for_relay(do, late):
        for d in range(0, window, 2):
            if late and d != 2:
                continue
            if d == 0:
                fits = core == 0
            elif d == 2:
                fits = (even_chip if late else odd_chip) & (ctx >= d)
            else:
                fits = ctx >= d
            if d == last:
                fits = fits & (core == 1)
            pl.when(fits)(functools.partial(do, d))

    def start_all(make, g, d):
        for copy in make(g, d):
            copy.start()

    def end_send(make, g, d):
        for copy in make(g, d):
            copy.wait_send()

    def wait_block(g, d):
        for copy in kv_copies(g, 0, d, sibling):
            copy.wait_recv()

    def to_right(source, target, at):
        return pltpu.make_async_remote_copy(
            src_ref=source,
            dst_ref=target,
            send_sem=z_send.at[at],
            recv_sem=z_recv.at[at],
            device_id=(right, ctx),
            device_id_type=MESH,
        )

    def moved_copies():
        cols = pl.ds(moved * DH, DH)
        q_cols = pl.ds(moved * group_cols, group_cols)
        place = pl.ds(last * rows, rows)
        return (
            to_right(k_ref.at[:, cols], kbuf.at[moved, place], 0),
            to_right(v_ref.at[:, cols], vbuf.at[moved, place], 1),
            to_right(bias.at[0], bias.at[1], 2),
            to_right(q_ref.at[:, q_cols], qbuf.at[:, q_cols], 3),
        )

    def out_copy(step):
        cols = pl.ds(pl.multiple_of(step * sent_cols, sent_cols), sent_cols)
        return pltpu.make_async_remote_copy(
            src_ref=obuf.at[:, cols],
            dst_ref=out_ref.at[:, cols],
            send_sem=o_send.at[step],
            recv_sem=o_recv.at[step],
            device_id=(right, ctx),
            device_id_type=MESH,
        )

    def out_local(step):
        cols = pl.ds(pl.multiple_of(step * step_cols, step_cols), step_cols)
        return pltpu.make_async_copy(obuf.at[:, cols], out_ref.at[:, cols], o_send.at[step])

    doc_copy = pltpu.make_async_copy(doc_hbm, doc_ref, doc_sem)
    doc_copy.start()
    for g in range(moved):
        for copy in own_copies(g):
            copy.start()
        q_copy(g).start()

    pl.semaphore_wait(barrier, met)
    for at in (0, 1):
        moved_copies()[at].start()

    @pl.when(guides)
    def _():
        pl.semaphore_signal(go_sem, inc=1, device_id=(right, ctx), device_id_type=MESH)

    doc_copy.wait()
    bias[0] = jnp.zeros(bias.shape[1:], jnp.float32)
    own_doc = doc_ref[0, ctx]
    for d in range(window):
        block = jnp.maximum(ctx - d, 0)
        seen = (doc_ref[0, block] == own_doc) & (ctx >= d)
        bias[0, d : d + 1, :] = jnp.full((1, DH), jnp.where(seen, 0.0, HIDDEN), jnp.float32)

    for at in (2, 3):
        moved_copies()[at].start()

    @pl.when(ends)
    def _():
        pl.semaphore_wait(go_sem, 1)

    def start_direct(g):
        if g < moved:
            for copy in own_copies(g):
                copy.wait()
        else:
            for copy in moved_copies()[:3]:
                copy.wait_recv()
        for_direct(lambda d: start_all(direct, g, d))

    def pass_on(g):
        for d in range(2, window, 2):
            fits = odd_chip if d == 2 else ctx >= d
            pl.when(fits)(functools.partial(wait_block, g, d))
        for_forward(lambda d: start_all(forward, g, d))
        for_relay(lambda d: start_all(relay, g, d), False)

    def pass_late(g):
        pl.when(even_chip & (ctx >= 2))(functools.partial(wait_block, g, 2))
        for_relay(lambda d: start_all(relay, g, d), True)

    def end_gather(g):
        for d in range(1, window, 2):
            pl.when(ctx >= d)(functools.partial(wait_block, g, d))

    start_direct(0)
    for d in range(1, window):

        @pl.when(ctx < d)
        def _():
            place = pl.ds((last - d) * rows, rows)
            for g in range(HK):
                kbuf[g, place, :] = jnp.zeros((rows, DH), kbuf.dtype)
                vbuf[g, place, :] = jnp.zeros((rows, DH), vbuf.dtype)

    pass_on(0)
    start_direct(1)
    pass_late(0)
    pass_on(1)
    start_direct(2)
    factor = math.log2(math.e) / math.sqrt(DH)

    @pl.loop(0, steps)
    def _(step):
        g = step // group_steps

        @pl.when(lax.rem(step, group_steps) == 0)
        def _():
            @pl.when(g < moved)
            def _():
                q_copy(g).wait()

            @pl.when(g == moved)
            def _():
                moved_copies()[3].wait_recv()

            end_gather(g)

        @pl.when(step == 1)
        def _():
            pass_late(1)
            pass_on(2)
            start_direct(3)

        @pl.when(step == 3)
        def _():
            pass_late(2)
            pass_on(3)

        @pl.when(step == 5)
        def _():
            pass_late(3)

        which = jnp.where(g == moved, 1, 0)
        causal = lax.broadcasted_iota(jnp.int32, (rows, rows), 0) >= lax.broadcasted_iota(
            jnp.int32, (rows, rows), 1
        )
        for at in range(STEP_HEADS):
            cols = pl.ds(pl.multiple_of(step * step_cols + at * DH, DH), DH)
            query = qbuf[:, cols]
            scores = []
            top = None
            for d in range(window):
                place = pl.ds((last - d) * rows, rows)
                part = lax.dot_general(
                    query,
                    kbuf[g, place, :],
                    (((1,), (1,)), ((), ())),
                    preferred_element_type=jnp.float32,
                )
                if d == 0:
                    part = jnp.where(causal, part, -HIDDEN)
                scores.append(part)
                lanes = part[:, :DH]
                for c in range(1, rows // DH):
                    lanes = jnp.maximum(lanes, part[:, c * DH : (c + 1) * DH])
                if d > 0:
                    lanes = lanes - bias[which, d : d + 1, :]
                top = lanes if top is None else jnp.maximum(top, lanes)
            row_top = jnp.broadcast_to(jnp.max(top, axis=1, keepdims=True), (rows, DH))
            total = None
            acc = None
            for d in range(window):
                place = pl.ds((last - d) * rows, rows)
                offset = row_top
                if d > 0:
                    offset = row_top + bias[which, d : d + 1, :]
                rounded = []
                for c in range(rows // DH):
                    lanes = jnp.exp2((scores[d][:, c * DH : (c + 1) * DH] - offset) * factor)
                    total = lanes if total is None else total + lanes
                    rounded.append(lanes.astype(jnp.bfloat16))
                product = jnp.dot(
                    jnp.concatenate(rounded, axis=1),
                    vbuf[g, place, :],
                    preferred_element_type=jnp.float32,
                )
                acc = product if acc is None else acc + product
            row_total = jnp.sum(total, axis=1, keepdims=True)
            obuf[:, cols] = (acc / row_total).astype(obuf.dtype)

        @pl.when((g < moved) & (lax.rem(step, SENT_STEPS) == SENT_STEPS - 1))
        def _():
            out_copy(step // SENT_STEPS).start()

        @pl.when(g == moved)
        def _():
            out_local(step).start()

    for copy in moved_copies():
        copy.wait_send()

    @pl.loop(0, HK)
    def _(g):
        for_direct(lambda d: end_send(direct, g, d))
        for_forward(lambda d: end_send(forward, g, d))
        for_relay(lambda d: end_send(relay, g, d), False)
        for_relay(lambda d: end_send(relay, g, d), True)

    @pl.loop(sent_steps, steps)
    def _(step):
        out_local(step).wait()

    @pl.loop(0, sent_steps // SENT_STEPS)
    def _(step):
        out_copy(step).wait_send()
        out_copy(step).wait_recv()


def shards(n_pipe, n_ctx, queries, keys, values, doc_ids):
    rows = queries.shape[1]
    window = n_ctx // 2 + 1
    steps = HQ // STEP_HEADS
    bias_rows = (window + 7) // 8 * 8
    dma = pltpu.SemaphoreType.DMA
    anywhere = pl.BlockSpec(memory_space=pl.ANY)
    handed = pl.pallas_call(
        functools.partial(kernel, n_pipe, n_ctx, window, rows),
        out_shape=jax.ShapeDtypeStruct((rows, HQ * DH), jnp.bfloat16),
        in_specs=[pl.BlockSpec(memory_space=pltpu.HBM)] * 4,
        out_specs=anywhere,
        scratch_shapes=[
            pltpu.VMEM((rows, HQ * DH), jnp.bfloat16),
            pltpu.VMEM((HK, window * rows, DH), jnp.bfloat16),
            pltpu.VMEM((HK, window * rows, DH), jnp.bfloat16),
            pltpu.VMEM((rows, HQ * DH), jnp.bfloat16),
            pltpu.VMEM((2, bias_rows, DH), jnp.float32),
            pltpu.SMEM(doc_ids.shape, jnp.int32),
            dma,
            dma((HK,)),
            dma((2, HK)),
            dma((2, HK, window - 1)),
            dma((2, HK, window - 1)),
            dma((4,)),
            dma((4,)),
            dma((steps,)),
            dma((steps,)),
            pltpu.SemaphoreType.REGULAR,
        ],
        compiler_params=pltpu.CompilerParams(
            collective_id=0, has_side_effects=True, vmem_limit_bytes=48 * 1024 * 1024
        ),
        name="relay_attention",
    )(*(pltpu.with_memory_space_constraint(x, pltpu.HBM) for x in (doc_ids, queries[0], keys[0], values[0])))
    return handed[None]


def solution(mesh):
    placed = (
        P("pipe", "ctx", None),
        P("pipe", "ctx", None),
        P("pipe", "ctx", None),
        P("pipe", None),
    )
    return jax.shard_map(
        functools.partial(shards, mesh.shape["pipe"], mesh.shape["ctx"]),
        mesh=mesh,
        in_specs=placed,
        out_specs=P("pipe", "ctx", None),
        check_vma=False,
    )
```

```python
import functools
import math

import jax
import jax.numpy as jnp
from jax import lax
from jax.experimental import pallas as pl
from jax.experimental.pallas import tpu as pltpu
from jax.sharding import PartitionSpec as P

HQ = 32
HK = 4
DH = 128
PER_GROUP = HQ // HK
STEP_HEADS = 2
SPREAD_STEP = 4
SPREAD_LATER = 7
HELPERS = (1, 2, 4, 6)
HIDDEN = 1e30
MESH = pl.DeviceIdType.MESH


def kernel(
    n_pipe,
    n_ctx,
    window,
    rows,
    doc_hbm,
    q_ref,
    k_ref,
    v_ref,
    out_ref,
    qbuf,
    kbuf,
    vbuf,
    obuf,
    bias,
    doc_ref,
    doc_sem,
    q_sem,
    own_sem,
    kv_send,
    kv_recv,
    z_send,
    z_recv,
    o_send,
    o_recv,
    go_sem,
    spread,
    s_send,
    s_recv,
    h_send,
    h_recv,
):
    pipe = lax.axis_index("pipe")
    ctx = lax.axis_index("ctx")
    right = lax.rem(pipe + 1, n_pipe)
    left = lax.rem(pipe + n_pipe - 1, n_pipe)
    moved = HK - 1
    group_cols = PER_GROUP * DH
    step_cols = STEP_HEADS * DH
    steps = HQ // STEP_HEADS
    group_steps = PER_GROUP // STEP_HEADS
    sent_steps = moved * group_steps
    last = window - 1

    core = lax.rem(ctx, 2)
    odd_chip = lax.rem(ctx // 2, 2) == 1
    even_chip = lax.rem(ctx // 2, 2) == 0
    turn = 1 - 2 * core
    sibling = ctx + turn
    barrier = pltpu.get_barrier_semaphore()
    ends = pipe == n_pipe - 1
    guides = pipe == n_pipe - 2
    hall = jnp.where(ends, left, pipe)
    spreads = ends & (ctx == 0)
    gathers = (pipe == 0) & (ctx == 0)

    def greet(pipe_to, ctx_to):
        pl.semaphore_signal(barrier, inc=1, device_id=(pipe_to, ctx_to), device_id_type=MESH)

    greet(left, ctx)
    pl.when((core == 1) | (ctx >= 2))(lambda: greet(hall, sibling))
    pl.when(odd_chip)(lambda: greet(hall, lax.rem(ctx + n_ctx - 2, n_ctx)))
    pl.when(even_chip & (ctx >= 2))(lambda: greet(hall, lax.rem(ctx + 2, n_ctx)))
    met = jnp.where((core == 0) | (ctx >= 2), 1, 0)
    met = met + jnp.where(even_chip, 1, 0) + jnp.where(odd_chip & (ctx >= 4), 1, 0)
    for d in range(4, window, 2):
        pl.when(ctx >= d)(lambda d=d: greet(hall, lax.rem(ctx + n_ctx - d, n_ctx)))
        met = met + jnp.where(ctx + d < n_ctx, 1, 0)
    pl.when(ends & (ctx == 6))(lambda: greet(hall, 0))
    met = 1 + jnp.where(guides & (ctx == 0), 1, 0) + jnp.where(ends, 0, jnp.where(guides, 2 * met, met))

    def own_copies(g):
        cols = pl.ds(pl.multiple_of(g * DH, DH), DH)
        place = pl.ds(last * rows, rows)
        return (
            pltpu.make_async_copy(k_ref.at[:, cols], kbuf.at[g, place], own_sem.at[0, g]),
            pltpu.make_async_copy(v_ref.at[:, cols], vbuf.at[g, place], own_sem.at[1, g]),
        )

    def q_copy(g):
        cols = pl.ds(pl.multiple_of(g * group_cols, group_cols), group_cols)
        return pltpu.make_async_copy(q_ref.at[:, cols], qbuf.at[:, cols], q_sem.at[g])

    def kv_copies(g, source, target, ctx_to):
        from_rows = pl.ds(pl.multiple_of((last - source) * rows, rows), rows)
        to_rows = pl.ds(pl.multiple_of((last - target) * rows, rows), rows)
        return [
            pltpu.make_async_remote_copy(
                src_ref=buf.at[g, from_rows],
                dst_ref=buf.at[g, to_rows],
                send_sem=kv_send.at[which, g, target - 1],
                recv_sem=kv_recv.at[which, g, target - 1],
                device_id=(pipe, ctx_to),
                device_id_type=MESH,
            )
            for which, buf in ((0, kbuf), (1, vbuf))
        ]

    def direct(g, d):
        return kv_copies(g, 0, d, lax.rem(ctx + d, n_ctx))

    def relay(g, d):
        return kv_copies(g, d, d + turn, sibling)

    def forward(g, d):
        return kv_copies(g, d, d - 2, lax.rem(ctx + n_ctx - 2, n_ctx))

    def for_direct(do):
        for d in range(2, window, 2):
            fits = even_chip if d == 2 else ctx + d < n_ctx
            pl.when(fits)(functools.partial(do, d))

    def for_forward(do):
        pl.when(odd_chip & (ctx >= 4))(functools.partial(do, 4))

    def for_relay(do, late):
        for d in range(0, window, 2):
            if late and d != 2:
                continue
            if d == 0:
                fits = core == 0
            elif d == 2:
                fits = (even_chip if late else odd_chip) & (ctx >= d)
            else:
                fits = ctx >= d
            if d == last:
                fits = fits & (core == 1)
            pl.when(fits)(functools.partial(do, d))

    def start_all(make, g, d):
        for copy in make(g, d):
            copy.start()

    def end_send(make, g, d):
        for copy in make(g, d):
            copy.wait_send()

    def wait_block(g, d):
        for copy in kv_copies(g, 0, d, sibling):
            copy.wait_recv()

    def to_right(source, target, at):
        return pltpu.make_async_remote_copy(
            src_ref=source,
            dst_ref=target,
            send_sem=z_send.at[at],
            recv_sem=z_recv.at[at],
            device_id=(right, ctx),
            device_id_type=MESH,
        )

    def moved_copies():
        cols = pl.ds(moved * DH, DH)
        q_cols = pl.ds(moved * group_cols, group_cols)
        place = pl.ds(last * rows, rows)
        return (
            to_right(k_ref.at[:, cols], kbuf.at[moved, place], 0),
            to_right(v_ref.at[:, cols], vbuf.at[moved, place], 1),
            to_right(bias.at[0], bias.at[1], 2),
            to_right(q_ref.at[:, q_cols], qbuf.at[:, q_cols], 3),
        )

    def out_copy(step):
        cols = pl.ds(pl.multiple_of(step * step_cols, step_cols), step_cols)
        return pltpu.make_async_remote_copy(
            src_ref=obuf.at[:, cols],
            dst_ref=out_ref.at[:, cols],
            send_sem=o_send.at[step],
            recv_sem=o_recv.at[step],
            device_id=(right, ctx),
            device_id_type=MESH,
        )

    def piece(ref, at):
        part = rows // len(HELPERS)
        return ref.at[pl.ds(at * part, part), pl.ds(SPREAD_STEP * step_cols, step_cols)]

    def to_helper(at):
        return pltpu.make_async_remote_copy(
            src_ref=piece(obuf, at),
            dst_ref=spread,
            send_sem=s_send.at[at],
            recv_sem=h_recv,
            device_id=(pipe, HELPERS[at]),
            device_id_type=MESH,
        )

    def from_helper(at):
        return pltpu.make_async_remote_copy(
            src_ref=spread,
            dst_ref=piece(out_ref, at),
            send_sem=h_send,
            recv_sem=s_recv.at[at],
            device_id=(right, 0),
            device_id_type=MESH,
        )

    def out_local(step):
        cols = pl.ds(pl.multiple_of(step * step_cols, step_cols), step_cols)
        return pltpu.make_async_copy(obuf.at[:, cols], out_ref.at[:, cols], o_send.at[step])

    doc_copy = pltpu.make_async_copy(doc_hbm, doc_ref, doc_sem)
    doc_copy.start()

    def fetch_own():
        for g in range(moved):
            for copy in own_copies(g):
                copy.start()
            q_copy(g).start()

    def fill_bias():
        doc_copy.wait()
        bias[0] = jnp.zeros(bias.shape[1:], jnp.float32)
        own_doc = doc_ref[0, ctx]
        for d in range(window):
            block = jnp.maximum(ctx - d, 0)
            seen = (doc_ref[0, block] == own_doc) & (ctx >= d)
            bias[0, d : d + 1, :] = jnp.full((1, DH), jnp.where(seen, 0.0, HIDDEN), jnp.float32)

    @pl.when(jnp.logical_not(ends))
    def _():
        fetch_own()
        fill_bias()

    pl.semaphore_wait(barrier, met)
    for at in (0, 1):
        moved_copies()[at].start()

    @pl.when(guides)
    def _():
        pl.semaphore_signal(go_sem, inc=1, device_id=(right, ctx), device_id_type=MESH)

    pl.when(ends)(fill_bias)
    for at in (2, 3):
        moved_copies()[at].start()

    @pl.when(ends)
    def _():
        fetch_own()
        pl.semaphore_wait(go_sem, 1)

    def start_direct(g):
        if g < moved:
            for copy in own_copies(g):
                copy.wait()
        else:
            for copy in moved_copies()[:3]:
                copy.wait_recv()
        for_direct(lambda d: start_all(direct, g, d))

    def pass_on(g):
        def arrive_and_forward():
            for arrived, onward in zip(kv_copies(g, 0, 4, sibling), forward(g, 4)):
                arrived.wait_recv()
                onward.start()

        pl.when(odd_chip & (ctx >= 4))(arrive_and_forward)
        for d in range(2, window, 2):
            fits = odd_chip if d == 2 else ctx >= d
            if d == 4:
                fits = even_chip & (ctx >= d)
            pl.when(fits)(functools.partial(wait_block, g, d))
        for_relay(lambda d: start_all(relay, g, d), False)

    def pass_late(g):
        pl.when(even_chip & (ctx >= 2))(functools.partial(wait_block, g, 2))
        for_relay(lambda d: start_all(relay, g, d), True)

    def end_gather(g):
        for d in range(1, window, 2):
            pl.when(ctx >= d)(functools.partial(wait_block, g, d))

    start_direct(0)
    for d in range(1, window):

        @pl.when(ctx < d)
        def _():
            place = pl.ds((last - d) * rows, rows)
            for g in range(HK):
                kbuf[g, place, :] = jnp.zeros((rows, DH), kbuf.dtype)
                vbuf[g, place, :] = jnp.zeros((rows, DH), vbuf.dtype)

    pass_on(0)
    start_direct(1)
    pass_late(0)
    pass_on(1)
    start_direct(2)
    factor = math.log2(math.e) / math.sqrt(DH)

    @pl.loop(0, steps)
    def _(step):
        g = step // group_steps

        @pl.when(lax.rem(step, group_steps) == 0)
        def _():
            @pl.when(g < moved)
            def _():
                q_copy(g).wait()

            @pl.when(g == moved)
            def _():
                moved_copies()[3].wait_recv()

            end_gather(g)

        @pl.when(step == 1)
        def _():
            pass_late(1)
            pass_on(2)
            start_direct(3)

        @pl.when(step == 3)
        def _():
            pass_late(2)
            pass_on(3)

        @pl.when(step == 5)
        def _():
            pass_late(3)

        which = jnp.where(g == moved, 1, 0)
        causal = lax.broadcasted_iota(jnp.int32, (rows, rows), 0) >= lax.broadcasted_iota(
            jnp.int32, (rows, rows), 1
        )
        for at in range(STEP_HEADS):
            cols = pl.ds(pl.multiple_of(step * step_cols + at * DH, DH), DH)
            query = qbuf[:, cols]
            scores = []
            top = None
            for d in range(window):
                place = pl.ds((last - d) * rows, rows)
                part = lax.dot_general(
                    query,
                    kbuf[g, place, :],
                    (((1,), (1,)), ((), ())),
                    preferred_element_type=jnp.float32,
                )
                if d == 0:
                    part = jnp.where(causal, part, -HIDDEN)
                scores.append(part)
                lanes = part[:, :DH]
                for c in range(1, rows // DH):
                    lanes = jnp.maximum(lanes, part[:, c * DH : (c + 1) * DH])
                if d > 0:
                    lanes = lanes - bias[which, d : d + 1, :]
                top = lanes if top is None else jnp.maximum(top, lanes)
            row_top = jnp.broadcast_to(jnp.max(top, axis=1, keepdims=True), (rows, DH))
            total = None
            acc = None
            for d in range(window):
                place = pl.ds((last - d) * rows, rows)
                offset = row_top
                if d > 0:
                    offset = row_top + bias[which, d : d + 1, :]
                rounded = []
                for c in range(rows // DH):
                    lanes = jnp.exp2((scores[d][:, c * DH : (c + 1) * DH] - offset) * factor)
                    total = lanes if total is None else total + lanes
                    rounded.append(lanes.astype(jnp.bfloat16))
                product = jnp.dot(
                    jnp.concatenate(rounded, axis=1),
                    vbuf[g, place, :],
                    preferred_element_type=jnp.float32,
                )
                acc = product if acc is None else acc + product
            row_total = jnp.sum(total, axis=1, keepdims=True)
            obuf[:, cols] = (acc / row_total).astype(obuf.dtype)

        @pl.when((g < moved) & jnp.logical_not(spreads & (step == SPREAD_STEP)))
        def _():
            out_copy(step).start()

        @pl.when(spreads & (step == SPREAD_STEP))
        def _():
            for at in range(len(HELPERS)):
                to_helper(at).start()

        for at, helper in enumerate(HELPERS):

            @pl.when(ends & (ctx == helper) & (step == SPREAD_LATER))
            def _(at=at):
                to_helper(at).wait_recv()
                from_helper(at).start()

        @pl.when(g == moved)
        def _():
            out_local(step).start()

    for copy in moved_copies():
        copy.wait_send()

    @pl.loop(0, HK)
    def _(g):
        for_direct(lambda d: end_send(direct, g, d))
        for_forward(lambda d: end_send(forward, g, d))
        for_relay(lambda d: end_send(relay, g, d), False)
        for_relay(lambda d: end_send(relay, g, d), True)

    @pl.loop(sent_steps, steps)
    def _(step):
        out_local(step).wait()

    for at, helper in enumerate(HELPERS):

        @pl.when(spreads)
        def _(at=at):
            to_helper(at).wait_send()

        @pl.when(ends & (ctx == helper))
        def _(at=at):
            from_helper(at).wait_send()

    @pl.loop(0, sent_steps)
    def _(step):
        @pl.when(jnp.logical_not(spreads & (step == SPREAD_STEP)))
        def _():
            out_copy(step).wait_send()

        @pl.when(jnp.logical_not(gathers & (step == SPREAD_STEP)))
        def _():
            out_copy(step).wait_recv()

    for at in range(len(HELPERS)):

        @pl.when(gathers)
        def _(at=at):
            from_helper(at).wait_recv()


def shards(n_pipe, n_ctx, queries, keys, values, doc_ids):
    rows = queries.shape[1]
    window = n_ctx // 2 + 1
    steps = HQ // STEP_HEADS
    bias_rows = (window + 7) // 8 * 8
    dma = pltpu.SemaphoreType.DMA
    anywhere = pl.BlockSpec(memory_space=pl.ANY)
    handed = pl.pallas_call(
        functools.partial(kernel, n_pipe, n_ctx, window, rows),
        out_shape=jax.ShapeDtypeStruct((rows, HQ * DH), jnp.bfloat16),
        in_specs=[pl.BlockSpec(memory_space=pltpu.HBM)] * 4,
        out_specs=anywhere,
        scratch_shapes=[
            pltpu.VMEM((rows, HQ * DH), jnp.bfloat16),
            pltpu.VMEM((HK, window * rows, DH), jnp.bfloat16),
            pltpu.VMEM((HK, window * rows, DH), jnp.bfloat16),
            pltpu.VMEM((rows, HQ * DH), jnp.bfloat16),
            pltpu.VMEM((2, bias_rows, DH), jnp.float32),
            pltpu.SMEM(doc_ids.shape, jnp.int32),
            dma,
            dma((HK,)),
            dma((2, HK)),
            dma((2, HK, window - 1)),
            dma((2, HK, window - 1)),
            dma((4,)),
            dma((4,)),
            dma((steps,)),
            dma((steps,)),
            pltpu.SemaphoreType.REGULAR,
            pltpu.VMEM((rows // len(HELPERS), STEP_HEADS * DH), jnp.bfloat16),
            dma((len(HELPERS),)),
            dma((len(HELPERS),)),
            dma,
            dma,
        ],
        compiler_params=pltpu.CompilerParams(
            collective_id=0, has_side_effects=True, vmem_limit_bytes=48 * 1024 * 1024
        ),
        name="relay_attention",
    )(*(pltpu.with_memory_space_constraint(x, pltpu.HBM) for x in (doc_ids, queries[0], keys[0], values[0])))
    return handed[None]


def solution(mesh):
    placed = (
        P("pipe", "ctx", None),
        P("pipe", "ctx", None),
        P("pipe", "ctx", None),
        P("pipe", None),
    )
    return jax.shard_map(
        functools.partial(shards, mesh.shape["pipe"], mesh.shape["ctx"]),
        mesh=mesh,
        in_specs=placed,
        out_specs=P("pipe", "ctx", None),
        check_vma=False,
    )
```

```python
import functools
import math

import jax
import jax.numpy as jnp
from jax import lax
from jax.experimental import pallas as pl
from jax.experimental.pallas import tpu as pltpu
from jax.sharding import PartitionSpec as P

HQ = 32
HK = 4
DH = 128
PER_GROUP = HQ // HK
STEP_HEADS = 2
SPREAD_STEP = 4
SPREAD_LATER = 7
HELPERS = (1, 2, 4, 6)
HIDDEN = 1e30
MESH = pl.DeviceIdType.MESH


def kernel(
    n_pipe,
    n_ctx,
    window,
    rows,
    doc_hbm,
    q_ref,
    k_ref,
    v_ref,
    out_ref,
    qbuf,
    kvbuf,
    obuf,
    bias,
    doc_ref,
    spread,
    doc_sem,
    q_sem,
    own_sem,
    kv_send,
    kv_recv,
    z_send,
    z_recv,
    o_send,
    o_recv,
    o_local,
    h_send,
    h_recv,
    go_sem,
):
    pipe = lax.axis_index("pipe")
    ctx = lax.axis_index("ctx")
    right = lax.rem(pipe + 1, n_pipe)
    left = lax.rem(pipe + n_pipe - 1, n_pipe)
    moved = HK - 1
    group_cols = PER_GROUP * DH
    step_cols = STEP_HEADS * DH
    steps = HQ // STEP_HEADS
    group_steps = PER_GROUP // STEP_HEADS
    last = window - 1
    own_rows = pl.ds(last * rows, rows)
    sent_cols = pl.ds(0, moved * group_cols)
    moved_cols = pl.ds(moved * group_cols, group_cols)

    core = lax.rem(ctx, 2)
    turn = 1 - 2 * core
    sibling = ctx + turn
    barrier = pltpu.get_barrier_semaphore()
    ends = pipe == n_pipe - 1
    guides = pipe == n_pipe - 2
    hall = jnp.where(ends, left, pipe)
    spreads = ends & (ctx == 0)

    def greet(pipe_to, ctx_to):
        pl.semaphore_signal(barrier, inc=1, device_id=(pipe_to, ctx_to), device_id_type=MESH)

    greet(left, ctx)
    pl.when((core == 1) | (ctx >= 2))(lambda: greet(hall, sibling))
    met = jnp.where((core == 0) | (ctx >= 2), 1, 0)
    for d in range(2, window, 2):
        pl.when(ctx >= d)(lambda d=d: greet(hall, lax.rem(ctx + n_ctx - d, n_ctx)))
        met = met + jnp.where(ctx + d < n_ctx, 1, 0)
    pl.when(ends & (ctx == HELPERS[-1]))(lambda: greet(hall, 0))
    met = 1 + jnp.where(guides & (ctx == 0), 1, 0) + jnp.where(ends, 0, jnp.where(guides, 2 * met, met))

    def own_copies(g):
        cols = pl.ds(g * DH, DH)
        return (
            pltpu.make_async_copy(k_ref.at[:, cols], kvbuf.at[g, 0, own_rows], own_sem.at[g]),
            pltpu.make_async_copy(v_ref.at[:, cols], kvbuf.at[g, 1, own_rows], own_sem.at[g]),
        )

    def both_own(g):
        block = kvbuf.at[g, :, own_rows]
        return pltpu.make_async_copy(block, block, own_sem.at[g])

    q_copy = pltpu.make_async_copy(q_ref.at[:, sent_cols], qbuf.at[:, sent_cols], q_sem)

    def kv_copy(g, source, target, ctx_to):
        from_rows = pl.ds(pl.multiple_of((last - source) * rows, rows), rows)
        to_rows = pl.ds(pl.multiple_of((last - target) * rows, rows), rows)
        return pltpu.make_async_remote_copy(
            src_ref=kvbuf.at[g, :, from_rows],
            dst_ref=kvbuf.at[g, :, to_rows],
            send_sem=kv_send.at[g],
            recv_sem=kv_recv.at[g, target - 1],
            device_id=(pipe, ctx_to),
            device_id_type=MESH,
        )

    def wait_block(g, d):
        kv_copy(g, 0, d, sibling).wait_recv()

    def relays(d):
        fits = core == 0 if d == 0 else ctx >= d
        return fits & (core == 1) if d == last else fits

    sends = jnp.int32(0)
    for d in range(0, window, 2):
        sends = sends + jnp.where(relays(d), 1, 0)
        if d > 0:
            sends = sends + jnp.where(ctx + d < n_ctx, 1, 0)

    def to_right(source, target, at):
        return pltpu.make_async_remote_copy(
            src_ref=source,
            dst_ref=target,
            send_sem=z_send.at[at],
            recv_sem=z_recv.at[at],
            device_id=(right, ctx),
            device_id_type=MESH,
        )

    def moved_kv():
        cols = pl.ds(moved * DH, DH)
        return (
            to_right(k_ref.at[:, cols], kvbuf.at[moved, 0, own_rows], 0),
            to_right(v_ref.at[:, cols], kvbuf.at[moved, 1, own_rows], 0),
        )

    def both_moved():
        return to_right(kvbuf.at[moved, :, own_rows], kvbuf.at[moved, :, own_rows], 0)

    def moved_bias():
        return to_right(bias.at[0], bias.at[1], 1)

    def moved_q():
        return to_right(q_ref.at[:, moved_cols], qbuf.at[:, moved_cols], 2)

    def out_copy(cols):
        return pltpu.make_async_remote_copy(
            src_ref=obuf.at[:, cols],
            dst_ref=out_ref.at[:, cols],
            send_sem=o_send,
            recv_sem=o_recv,
            device_id=(right, ctx),
            device_id_type=MESH,
        )

    def out_local(cols):
        return pltpu.make_async_copy(obuf.at[:, cols], out_ref.at[:, cols], o_local)

    def piece(ref, at):
        part = rows // len(HELPERS)
        return ref.at[pl.ds(at * part, part), pl.ds(SPREAD_STEP * step_cols, step_cols)]

    def to_helper(at):
        return pltpu.make_async_remote_copy(
            src_ref=piece(obuf, at),
            dst_ref=spread,
            send_sem=o_send,
            recv_sem=h_recv,
            device_id=(pipe, HELPERS[at]),
            device_id_type=MESH,
        )

    def from_helper(at):
        return pltpu.make_async_remote_copy(
            src_ref=spread,
            dst_ref=piece(out_ref, at),
            send_sem=h_send,
            recv_sem=o_recv,
            device_id=(right, 0),
            device_id_type=MESH,
        )

    doc_copy = pltpu.make_async_copy(doc_hbm, doc_ref, doc_sem)
    doc_copy.start()

    def fetch_own():
        for g in range(moved):
            for copy in own_copies(g):
                copy.start()
        q_copy.start()

    def fill_bias():
        doc_copy.wait()
        bias[0] = jnp.zeros(bias.shape[1:], jnp.float32)
        own_doc = doc_ref[0, ctx]
        for d in range(window):
            block = jnp.maximum(ctx - d, 0)
            seen = (doc_ref[0, block] == own_doc) & (ctx >= d)
            bias[0, d : d + 1, :] = jnp.full((1, DH), jnp.where(seen, 0.0, HIDDEN), jnp.float32)

    @pl.when(jnp.logical_not(ends))
    def _():
        fetch_own()
        fill_bias()

    pl.semaphore_wait(barrier, met)
    for copy in moved_kv():
        copy.start()

    @pl.when(guides)
    def _():
        pl.semaphore_signal(go_sem, inc=1, device_id=(right, ctx), device_id_type=MESH)

    pl.when(ends)(fill_bias)
    moved_bias().start()
    moved_q().start()

    @pl.when(ends)
    def _():
        fetch_own()
        pl.semaphore_wait(go_sem, 1)

    def start_direct(g):
        if g < moved:
            both_own(g).wait()
        else:
            both_moved().wait_recv()
            moved_bias().wait_recv()
        for d in range(2, window, 2):
            pl.when(ctx + d < n_ctx)(lambda d=d: kv_copy(g, 0, d, lax.rem(ctx + d, n_ctx)).start())

    def pass_on(g):
        pl.when(relays(0))(lambda: kv_copy(g, 0, 1, sibling).start())
        for d in range(2, window, 2):
            pl.when(ctx >= d)(functools.partial(wait_block, g, d))
            pl.when(relays(d))(lambda d=d: kv_copy(g, d, d + turn, sibling).start())

    def end_gather(g):
        for d in range(1, window, 2):
            pl.when(ctx >= d)(functools.partial(wait_block, g, d))

    start_direct(0)
    for d in range(1, window):

        @pl.when(ctx < d)
        def _():
            place = pl.ds((last - d) * rows, rows)
            for g in range(HK):
                for which in range(2):
                    kvbuf[g, which, place, :] = jnp.zeros((rows, DH), kvbuf.dtype)

    pass_on(0)
    start_direct(1)
    q_copy.wait()
    factor = math.log2(math.e) / math.sqrt(DH)

    @pl.loop(0, steps)
    def _(step):
        g = step // group_steps

        @pl.when(lax.rem(step, group_steps) == 0)
        def _():
            pl.when(g == moved)(lambda: moved_q().wait_recv())
            end_gather(g)

        @pl.when(step == 3)
        def _():
            pass_on(1)
            start_direct(2)

        @pl.when(step == 7)
        def _():
            pass_on(2)
            start_direct(3)

        @pl.when(step == 11)
        def _():
            pass_on(3)

        which = jnp.where(g == moved, 1, 0)
        causal = lax.broadcasted_iota(jnp.int32, (rows, rows), 0) >= lax.broadcasted_iota(
            jnp.int32, (rows, rows), 1
        )
        for at in range(STEP_HEADS):
            cols = pl.ds(pl.multiple_of(step * step_cols + at * DH, DH), DH)
            query = qbuf[:, cols]
            scores = []
            top = None
            for d in range(window):
                place = pl.ds((last - d) * rows, rows)
                part = lax.dot_general(
                    query,
                    kvbuf[g, 0, place, :],
                    (((1,), (1,)), ((), ())),
                    preferred_element_type=jnp.float32,
                )
                if d == 0:
                    part = jnp.where(causal, part, -HIDDEN)
                scores.append(part)
                lanes = part[:, :DH]
                for c in range(1, rows // DH):
                    lanes = jnp.maximum(lanes, part[:, c * DH : (c + 1) * DH])
                if d > 0:
                    lanes = lanes - bias[which, d : d + 1, :]
                top = lanes if top is None else jnp.maximum(top, lanes)
            row_top = jnp.broadcast_to(jnp.max(top, axis=1, keepdims=True), (rows, DH))
            total = None
            acc = None
            for d in range(window):
                place = pl.ds((last - d) * rows, rows)
                offset = row_top
                if d > 0:
                    offset = row_top + bias[which, d : d + 1, :]
                rounded = []
                for c in range(rows // DH):
                    lanes = jnp.exp2((scores[d][:, c * DH : (c + 1) * DH] - offset) * factor)
                    total = lanes if total is None else total + lanes
                    rounded.append(lanes.astype(jnp.bfloat16))
                product = jnp.dot(
                    jnp.concatenate(rounded, axis=1),
                    kvbuf[g, 1, place, :],
                    preferred_element_type=jnp.float32,
                )
                acc = product if acc is None else acc + product
            row_total = jnp.sum(total, axis=1, keepdims=True)
            obuf[:, cols] = (acc / row_total).astype(obuf.dtype)

        done = pl.ds(pl.multiple_of(step * step_cols, step_cols), step_cols)

        @pl.when((g < moved) & jnp.logical_not(spreads & (step == SPREAD_STEP)))
        def _():
            out_copy(done).start()

        @pl.when(spreads & (step == SPREAD_STEP))
        def _():
            for at in range(len(HELPERS)):
                to_helper(at).start()

        for at, helper in enumerate(HELPERS):

            @pl.when(ends & (ctx == helper) & (step == SPREAD_LATER))
            def _(at=at):
                to_helper(at).wait_recv()
                from_helper(at).start()

        @pl.when(g == moved)
        def _():
            out_local(done).start()

    both_moved().wait_send()
    moved_bias().wait_send()
    moved_q().wait_send()

    for count in range(1, window + 1):

        @pl.when(sends == count)
        def _(count=count):
            for g in range(HK):
                blocks = kvbuf.at[g, :, pl.ds(0, count * rows)]
                pltpu.make_async_copy(blocks, blocks, kv_send.at[g]).wait()

    for at, helper in enumerate(HELPERS):
        pl.when(ends & (ctx == helper))(lambda at=at: from_helper(at).wait_send())
    out_local(moved_cols).wait()
    out_copy(sent_cols).wait_send()
    out_copy(sent_cols).wait_recv()


def shards(n_pipe, n_ctx, queries, keys, values, doc_ids):
    rows = queries.shape[1]
    window = n_ctx // 2 + 1
    bias_rows = (window + 7) // 8 * 8
    dma = pltpu.SemaphoreType.DMA
    anywhere = pl.BlockSpec(memory_space=pl.ANY)
    handed = pl.pallas_call(
        functools.partial(kernel, n_pipe, n_ctx, window, rows),
        out_shape=jax.ShapeDtypeStruct((rows, HQ * DH), jnp.bfloat16),
        in_specs=[pl.BlockSpec(memory_space=pltpu.HBM)] * 4,
        out_specs=anywhere,
        scratch_shapes=[
            pltpu.VMEM((rows, HQ * DH), jnp.bfloat16),
            pltpu.VMEM((HK, 2, window * rows, DH), jnp.bfloat16),
            pltpu.VMEM((rows, HQ * DH), jnp.bfloat16),
            pltpu.VMEM((2, bias_rows, DH), jnp.float32),
            pltpu.SMEM(doc_ids.shape, jnp.int32),
            pltpu.VMEM((rows // len(HELPERS), STEP_HEADS * DH), jnp.bfloat16),
            dma,
            dma,
            dma((HK - 1,)),
            dma((HK,)),
            dma((HK, window - 1)),
            dma((3,)),
            dma((3,)),
            dma,
            dma,
            dma,
            dma,
            dma,
            pltpu.SemaphoreType.REGULAR,
        ],
        compiler_params=pltpu.CompilerParams(
            collective_id=0, has_side_effects=True, vmem_limit_bytes=48 * 1024 * 1024
        ),
        name="relay_attention",
    )(*(pltpu.with_memory_space_constraint(x, pltpu.HBM) for x in (doc_ids, queries[0], keys[0], values[0])))
    return handed[None]


def solution(mesh):
    placed = (
        P("pipe", "ctx", None),
        P("pipe", "ctx", None),
        P("pipe", "ctx", None),
        P("pipe", None),
    )
    return jax.shard_map(
        functools.partial(shards, mesh.shape["pipe"], mesh.shape["ctx"]),
        mesh=mesh,
        in_specs=placed,
        out_specs=P("pipe", "ctx", None),
        check_vma=False,
    )
```

```python
import functools
import math

import jax
import jax.numpy as jnp
from jax import lax
from jax.experimental import pallas as pl
from jax.experimental.pallas import tpu as pltpu
from jax.sharding import PartitionSpec as P

HQ = 32
HK = 4
DH = 128
PER_GROUP = HQ // HK
STEP_HEADS = 2
SPREAD_STEP = 2
SPREAD_LATER = 5
HELPERS = (1, 2, 4, 6)
SIXTEENTHS = (4, 3, 3, 3)
HIDDEN = 1e30
MESH = pl.DeviceIdType.MESH


def kernel(
    n_pipe,
    n_ctx,
    window,
    rows,
    doc_hbm,
    q_ref,
    k_ref,
    v_ref,
    out_ref,
    qbuf,
    kvbuf,
    obuf,
    bias,
    doc_ref,
    spread,
    lent,
    doc_sem,
    q_sem,
    own_sem,
    kv_send,
    kv_recv,
    z_send,
    z_recv,
    o_send,
    o_recv,
    h_send,
    h_recv,
    go_sem,
):
    pipe = lax.axis_index("pipe")
    ctx = lax.axis_index("ctx")
    right = lax.rem(pipe + 1, n_pipe)
    left = lax.rem(pipe + n_pipe - 1, n_pipe)
    moved = HK - 1
    group_cols = PER_GROUP * DH
    step_cols = STEP_HEADS * DH
    steps = HQ // STEP_HEADS
    group_steps = PER_GROUP // STEP_HEADS
    last = window - 1
    own_rows = pl.ds(last * rows, rows)
    sent_cols = pl.ds(0, moved * group_cols)
    moved_cols = pl.ds(moved * group_cols, group_cols)

    core = lax.rem(ctx, 2)
    turn = 1 - 2 * core
    sibling = ctx + turn
    barrier = pltpu.get_barrier_semaphore()
    ends = pipe == n_pipe - 1
    guides = pipe == n_pipe - 2
    hall = jnp.where(ends, left, pipe)
    spreads = ends & (ctx == 0)

    def greet(pipe_to, ctx_to):
        pl.semaphore_signal(barrier, inc=1, device_id=(pipe_to, ctx_to), device_id_type=MESH)

    greet(left, ctx)
    pl.when((core == 1) | (ctx >= 2))(lambda: greet(hall, sibling))
    met = jnp.where((core == 0) | (ctx >= 2), 1, 0)
    for d in range(2, window, 2):
        pl.when(ctx >= d)(lambda d=d: greet(hall, lax.rem(ctx + n_ctx - d, n_ctx)))
        met = met + jnp.where(ctx + d < n_ctx, 1, 0)
    pl.when(ends & (ctx == HELPERS[-1]))(lambda: greet(hall, 0))
    met = 1 + jnp.where(guides & (ctx == 0), 1, 0) + jnp.where(ends, 0, jnp.where(guides, 2 * met, met))

    def own_copies(g):
        cols = pl.ds(g * DH, DH)
        place = lent if g == moved else kvbuf.at[g, :, own_rows]
        return (
            pltpu.make_async_copy(k_ref.at[:, cols], place.at[0], own_sem),
            pltpu.make_async_copy(v_ref.at[:, cols], place.at[1], own_sem),
        )

    def all_own():
        blocks = kvbuf.at[:, :, own_rows]
        return pltpu.make_async_copy(blocks, blocks, own_sem)

    q_copy = pltpu.make_async_copy(q_ref.at[:, sent_cols], qbuf.at[:, sent_cols], q_sem)

    def kv_copy(g, source, target, ctx_to):
        from_rows = pl.ds(pl.multiple_of((last - source) * rows, rows), rows)
        to_rows = pl.ds(pl.multiple_of((last - target) * rows, rows), rows)
        return pltpu.make_async_remote_copy(
            src_ref=kvbuf.at[g, :, from_rows],
            dst_ref=kvbuf.at[g, :, to_rows],
            send_sem=kv_send.at[g],
            recv_sem=kv_recv.at[g, target - 1],
            device_id=(pipe, ctx_to),
            device_id_type=MESH,
        )

    def wait_block(g, d):
        kv_copy(g, 0, d, sibling).wait_recv()

    def relays(d):
        fits = core == 0 if d == 0 else ctx >= d
        return fits & (core == 1) if d == last else fits

    sends = jnp.int32(0)
    for d in range(0, window, 2):
        sends = sends + jnp.where(relays(d), 1, 0)
        if d > 0:
            sends = sends + jnp.where(ctx + d < n_ctx, 1, 0)

    def to_right(source, target, at):
        return pltpu.make_async_remote_copy(
            src_ref=source,
            dst_ref=target,
            send_sem=o_send if at == 2 else z_send.at[at],
            recv_sem=z_recv.at[at],
            device_id=(right, ctx),
            device_id_type=MESH,
        )

    def moved_kv():
        return to_right(lent, kvbuf.at[moved, :, own_rows], 0)

    def moved_bias():
        return to_right(bias.at[0], bias.at[1], 1)

    def moved_q():
        return to_right(q_ref.at[:, moved_cols], qbuf.at[:, moved_cols], 2)

    def out_copy(cols):
        return pltpu.make_async_remote_copy(
            src_ref=obuf.at[:, cols],
            dst_ref=out_ref.at[:, cols],
            send_sem=o_send,
            recv_sem=o_recv,
            device_id=(right, ctx),
            device_id_type=MESH,
        )

    def out_local(cols):
        return pltpu.make_async_copy(obuf.at[:, cols], out_ref.at[:, cols], o_recv)

    def piece(ref, at):
        first = sum(SIXTEENTHS[:at]) * rows // 16
        count = SIXTEENTHS[at] * rows // 16 if at < len(HELPERS) else rows - first
        return ref.at[pl.ds(first, count), pl.ds(SPREAD_STEP * step_cols, step_cols)]

    def landing(at):
        return spread.at[pl.ds(0, SIXTEENTHS[at] * rows // 16)]

    def rest_copy():
        return pltpu.make_async_remote_copy(
            src_ref=piece(obuf, len(HELPERS)),
            dst_ref=piece(out_ref, len(HELPERS)),
            send_sem=o_send,
            recv_sem=o_recv,
            device_id=(right, ctx),
            device_id_type=MESH,
        )

    def to_helper(at):
        return pltpu.make_async_remote_copy(
            src_ref=piece(obuf, at),
            dst_ref=landing(at),
            send_sem=o_send,
            recv_sem=h_recv,
            device_id=(pipe, HELPERS[at]),
            device_id_type=MESH,
        )

    def from_helper(at):
        return pltpu.make_async_remote_copy(
            src_ref=landing(at),
            dst_ref=piece(out_ref, at),
            send_sem=h_send,
            recv_sem=o_recv,
            device_id=(right, 0),
            device_id_type=MESH,
        )

    doc_copy = pltpu.make_async_copy(doc_hbm, doc_ref, doc_sem)
    doc_copy.start()

    def fetch_own():
        for g in range(HK):
            for copy in own_copies(g):
                copy.start()
        q_copy.start()

    def fill_bias():
        doc_copy.wait()
        bias[0] = jnp.zeros(bias.shape[1:], jnp.float32)
        own_doc = doc_ref[0, ctx]
        for d in range(window):
            block = jnp.maximum(ctx - d, 0)
            seen = (doc_ref[0, block] == own_doc) & (ctx >= d)
            bias[0, d : d + 1, :] = jnp.full((1, DH), jnp.where(seen, 0.0, HIDDEN), jnp.float32)

    @pl.when(jnp.logical_not(ends))
    def _():
        fetch_own()
        fill_bias()

    pl.semaphore_wait(barrier, met)
    moved_q().start()

    @pl.when(guides)
    def _():
        pl.semaphore_signal(go_sem, inc=1, device_id=(right, ctx), device_id_type=MESH)

    @pl.when(ends)
    def _():
        fetch_own()
        fill_bias()

    all_own().wait()
    moved_kv().start()
    moved_bias().start()
    pl.when(ends)(lambda: pl.semaphore_wait(go_sem, 1))

    def start_direct(g):
        if g == moved:
            moved_kv().wait_recv()
            moved_bias().wait_recv()
        for d in range(2, window, 2):
            pl.when(ctx + d < n_ctx)(lambda d=d: kv_copy(g, 0, d, lax.rem(ctx + d, n_ctx)).start())

    def pass_on(g):
        pl.when(relays(0))(lambda: kv_copy(g, 0, 1, sibling).start())
        for d in range(2, window, 2):
            pl.when(ctx >= d)(functools.partial(wait_block, g, d))
            pl.when(relays(d))(lambda d=d: kv_copy(g, d, d + turn, sibling).start())

    def end_gather(g):
        for d in range(1, window, 2):
            pl.when(ctx >= d)(functools.partial(wait_block, g, d))

    start_direct(0)
    for d in range(1, window):

        @pl.when(ctx < d)
        def _():
            place = pl.ds((last - d) * rows, rows)
            for g in range(HK):
                for which in range(2):
                    kvbuf[g, which, place, :] = jnp.zeros((rows, DH), kvbuf.dtype)

    pass_on(0)
    start_direct(1)
    q_copy.wait()
    factor = math.log2(math.e) / math.sqrt(DH)

    @pl.loop(0, steps)
    def _(step):
        g = step // group_steps

        @pl.when(lax.rem(step, group_steps) == 0)
        def _():
            pl.when(g == moved)(lambda: moved_q().wait_recv())
            end_gather(g)

        @pl.when(step == 3)
        def _():
            pass_on(1)
            start_direct(2)

        @pl.when(step == 7)
        def _():
            pass_on(2)
            start_direct(3)

        @pl.when(step == 11)
        def _():
            pass_on(3)

        which = jnp.where(g == moved, 1, 0)
        causal = lax.broadcasted_iota(jnp.int32, (rows, rows), 0) >= lax.broadcasted_iota(
            jnp.int32, (rows, rows), 1
        )
        for at in range(STEP_HEADS):
            cols = pl.ds(pl.multiple_of(step * step_cols + at * DH, DH), DH)
            query = qbuf[:, cols]
            scores = []
            top = None
            for d in range(window):
                place = pl.ds((last - d) * rows, rows)
                part = lax.dot_general(
                    query,
                    kvbuf[g, 0, place, :],
                    (((1,), (1,)), ((), ())),
                    preferred_element_type=jnp.float32,
                )
                if d == 0:
                    part = jnp.where(causal, part, -HIDDEN)
                scores.append(part)
                lanes = part[:, :DH]
                for c in range(1, rows // DH):
                    lanes = jnp.maximum(lanes, part[:, c * DH : (c + 1) * DH])
                if d > 0:
                    lanes = lanes - bias[which, d : d + 1, :]
                top = lanes if top is None else jnp.maximum(top, lanes)
            row_top = jnp.broadcast_to(jnp.max(top, axis=1, keepdims=True), (rows, DH))
            total = None
            acc = None
            for d in range(window):
                place = pl.ds((last - d) * rows, rows)
                offset = row_top
                if d > 0:
                    offset = row_top + bias[which, d : d + 1, :]
                rounded = []
                for c in range(rows // DH):
                    lanes = jnp.exp2((scores[d][:, c * DH : (c + 1) * DH] - offset) * factor)
                    total = lanes if total is None else total + lanes
                    rounded.append(lanes.astype(jnp.bfloat16))
                product = jnp.dot(
                    jnp.concatenate(rounded, axis=1),
                    kvbuf[g, 1, place, :],
                    preferred_element_type=jnp.float32,
                )
                acc = product if acc is None else acc + product
            row_total = jnp.sum(total, axis=1, keepdims=True)
            obuf[:, cols] = (acc / row_total).astype(obuf.dtype)

        done = pl.ds(pl.multiple_of(step * step_cols, step_cols), step_cols)

        @pl.when((step < group_steps) & jnp.logical_not(spreads & (step == SPREAD_STEP)))
        def _():
            out_copy(done).start()

        @pl.when((step >= group_steps) & (g < moved) & (lax.rem(step, 2) == 1))
        def _():
            pair = pl.ds(pl.multiple_of((step - 1) * step_cols, 2 * step_cols), 2 * step_cols)
            out_copy(pair).start()

        @pl.when(spreads & (step == SPREAD_STEP))
        def _():
            for at in range(len(HELPERS)):
                to_helper(at).start()
            rest_copy().start()

        for at, helper in enumerate(HELPERS):

            @pl.when(ends & (ctx == helper) & (step == SPREAD_LATER))
            def _(at=at):
                to_helper(at).wait_recv()
                from_helper(at).start()

        @pl.when(g == moved)
        def _():
            out_local(done).start()

    moved_kv().wait_send()
    moved_bias().wait_send()

    for count in range(1, window + 1):

        @pl.when(sends == count)
        def _(count=count):
            for g in range(HK):
                blocks = kvbuf.at[g, :, pl.ds(0, count * rows)]
                pltpu.make_async_copy(blocks, blocks, kv_send.at[g]).wait()

    for at, helper in enumerate(HELPERS):
        pl.when(ends & (ctx == helper))(lambda at=at: from_helper(at).wait_send())
    whole = pl.ds(0, HQ * DH)
    out_copy(whole).wait_send()
    out_copy(whole).wait_recv()


def shards(n_pipe, n_ctx, queries, keys, values, doc_ids):
    rows = queries.shape[1]
    window = n_ctx // 2 + 1
    bias_rows = (window + 7) // 8 * 8
    dma = pltpu.SemaphoreType.DMA
    anywhere = pl.BlockSpec(memory_space=pl.ANY)
    handed = pl.pallas_call(
        functools.partial(kernel, n_pipe, n_ctx, window, rows),
        out_shape=jax.ShapeDtypeStruct((rows, HQ * DH), jnp.bfloat16),
        in_specs=[pl.BlockSpec(memory_space=pltpu.HBM)] * 4,
        out_specs=anywhere,
        scratch_shapes=[
            pltpu.VMEM((rows, HQ * DH), jnp.bfloat16),
            pltpu.VMEM((HK, 2, window * rows, DH), jnp.bfloat16),
            pltpu.VMEM((rows, HQ * DH), jnp.bfloat16),
            pltpu.VMEM((2, bias_rows, DH), jnp.float32),
            pltpu.SMEM(doc_ids.shape, jnp.int32),
            pltpu.VMEM((max(SIXTEENTHS) * rows // 16, STEP_HEADS * DH), jnp.bfloat16),
            pltpu.VMEM((2, rows, DH), jnp.bfloat16),
            dma,
            dma,
            dma,
            dma((HK,)),
            dma((HK, window - 1)),
            dma((2,)),
            dma((3,)),
            dma,
            dma,
            dma,
            dma,
            pltpu.SemaphoreType.REGULAR,
        ],
        compiler_params=pltpu.CompilerParams(
            collective_id=0, has_side_effects=True, vmem_limit_bytes=48 * 1024 * 1024
        ),
        name="relay_attention",
    )(*(pltpu.with_memory_space_constraint(x, pltpu.HBM) for x in (doc_ids, queries[0], keys[0], values[0])))
    return handed[None]


def solution(mesh):
    placed = (
        P("pipe", "ctx", None),
        P("pipe", "ctx", None),
        P("pipe", "ctx", None),
        P("pipe", None),
    )
    return jax.shard_map(
        functools.partial(shards, mesh.shape["pipe"], mesh.shape["ctx"]),
        mesh=mesh,
        in_specs=placed,
        out_specs=P("pipe", "ctx", None),
        check_vma=False,
    )
```

```python
import functools
import math

import jax
import jax.numpy as jnp
from jax import lax
from jax.experimental import pallas as pl
from jax.experimental.pallas import tpu as pltpu
from jax.sharding import PartitionSpec as P

HQ = 32
HK = 4
DH = 128
PER_GROUP = HQ // HK
STEP_HEADS = 2
SPREAD_STEP = 2
SPREAD_LATER = 9
HELPED = ((2, 0), (4, 1), (6, 0))
SPREAD_ROWS = 128
TOP = 128
HIDDEN = 1e30
MESH = pl.DeviceIdType.MESH


def kernel(
    n_pipe,
    n_ctx,
    window,
    rows,
    doc_hbm,
    q_ref,
    k_ref,
    v_ref,
    out_ref,
    qbuf,
    kvbuf,
    obuf,
    bias,
    doc_ref,
    spread,
    lent,
    weights,
    sums,
    tile,
    packed,
    facts,
    vtop,
    top,
    doc_sem,
    q_sem,
    own_sem,
    kv_send,
    kv_recv,
    z_send,
    z_recv,
    o_send,
    o_recv,
    h_send,
    h_recv,
    y_send,
    y_recv,
    f_send,
    f_recv,
    v_send,
    v_recv,
    t_sem,
    go_sem,
):
    pipe = lax.axis_index("pipe")
    ctx = lax.axis_index("ctx")
    right = lax.rem(pipe + 1, n_pipe)
    left = lax.rem(pipe + n_pipe - 1, n_pipe)
    moved = HK - 1
    group_cols = PER_GROUP * DH
    step_cols = STEP_HEADS * DH
    steps = HQ // STEP_HEADS
    group_steps = PER_GROUP // STEP_HEADS
    last = window - 1
    own_rows = pl.ds(last * rows, rows)
    sent_cols = pl.ds(0, moved * group_cols)
    moved_cols = pl.ds(moved * group_cols, group_cols)

    core = lax.rem(ctx, 2)
    turn = 1 - 2 * core
    sibling = ctx + turn
    barrier = pltpu.get_barrier_semaphore()
    ends = pipe == n_pipe - 1
    guides = pipe == n_pipe - 2
    hall = jnp.where(ends, left, pipe)
    packs = ends & (ctx == 0)
    unpacks = (pipe == 0) & (ctx == 0)
    spreads = ends & functools.reduce(jnp.logical_or, [ctx == helped for helped, _ in HELPED])

    def greet(pipe_to, ctx_to):
        pl.semaphore_signal(barrier, inc=1, device_id=(pipe_to, ctx_to), device_id_type=MESH)

    greet(left, ctx)
    pl.when((core == 1) | (ctx >= 2))(lambda: greet(hall, sibling))
    met = jnp.where((core == 0) | (ctx >= 2), 1, 0)
    for d in range(2, window, 2):
        pl.when(ctx >= d)(lambda d=d: greet(hall, lax.rem(ctx + n_ctx - d, n_ctx)))
        met = met + jnp.where(ctx + d < n_ctx, 1, 0)
    met = 1 + jnp.where(ends, 0, jnp.where(guides, 2 * met, met))
    for helped, helper in HELPED:
        pl.when(ends & (ctx == helper))(lambda helped=helped: greet(hall, helped))
        met = met + jnp.where(guides & (ctx == helped), 1, 0)

    def own_copies(g):
        cols = pl.ds(g * DH, DH)
        place = lent if g == moved else kvbuf.at[g, :, own_rows]
        return (
            pltpu.make_async_copy(k_ref.at[:, cols], place.at[0], own_sem),
            pltpu.make_async_copy(v_ref.at[:, cols], place.at[1], own_sem),
        )

    def all_own():
        blocks = kvbuf.at[:, :, own_rows]
        return pltpu.make_async_copy(blocks, blocks, own_sem)

    q_copy = pltpu.make_async_copy(q_ref.at[:, sent_cols], qbuf.at[:, sent_cols], q_sem)

    def kv_copy(g, source, target, ctx_to):
        from_rows = pl.ds(pl.multiple_of((last - source) * rows, rows), rows)
        to_rows = pl.ds(pl.multiple_of((last - target) * rows, rows), rows)
        return pltpu.make_async_remote_copy(
            src_ref=kvbuf.at[g, :, from_rows],
            dst_ref=kvbuf.at[g, :, to_rows],
            send_sem=kv_send.at[g],
            recv_sem=kv_recv.at[g, target - 1],
            device_id=(pipe, ctx_to),
            device_id_type=MESH,
        )

    def wait_block(g, d):
        kv_copy(g, 0, d, sibling).wait_recv()

    def relays(d):
        fits = core == 0 if d == 0 else ctx >= d
        return fits & (core == 1) if d == last else fits

    sends = jnp.int32(0)
    for d in range(0, window, 2):
        sends = sends + jnp.where(relays(d), 1, 0)
        if d > 0:
            sends = sends + jnp.where(ctx + d < n_ctx, 1, 0)

    def to_right(source, target, at):
        return pltpu.make_async_remote_copy(
            src_ref=source,
            dst_ref=target,
            send_sem=o_send if at == 2 else z_send.at[at],
            recv_sem=z_recv.at[at],
            device_id=(right, ctx),
            device_id_type=MESH,
        )

    def moved_kv():
        return to_right(lent, kvbuf.at[moved, :, own_rows], 0)

    def moved_bias():
        return to_right(bias.at[0], bias.at[1], 1)

    def moved_q():
        return to_right(q_ref.at[:, moved_cols], qbuf.at[:, moved_cols], 2)

    def out_copy(cols):
        return pltpu.make_async_remote_copy(
            src_ref=obuf.at[:, cols],
            dst_ref=out_ref.at[:, cols],
            send_sem=o_send,
            recv_sem=o_recv,
            device_id=(right, ctx),
            device_id_type=MESH,
        )

    def out_local(cols):
        return pltpu.make_async_copy(obuf.at[:, cols], out_ref.at[:, cols], o_recv)

    def half_copy(cols):
        low = pl.ds(TOP, rows - TOP)
        return pltpu.make_async_remote_copy(
            src_ref=obuf.at[low, cols],
            dst_ref=out_ref.at[low, cols],
            send_sem=o_send,
            recv_sem=o_recv,
            device_id=(right, ctx),
            device_id_type=MESH,
        )

    def to_top(source, target, send_sem, recv_sem):
        return pltpu.make_async_remote_copy(
            src_ref=source,
            dst_ref=target,
            send_sem=send_sem,
            recv_sem=recv_sem,
            device_id=(right, ctx),
            device_id_type=MESH,
        )

    def packed_copy(g):
        tiles = packed.at[pl.ds(g * group_steps, group_steps)]
        return to_top(tiles, tiles, y_send, y_recv.at[g])

    def facts_copy(g):
        lines = facts.at[g, pl.ds(0, 16)]
        return to_top(lines, lines, f_send, f_recv.at[g])

    def vtop_copy():
        return to_top(kvbuf.at[pl.ds(0, moved), 1, pl.ds(last * rows, TOP)], vtop, v_send, v_recv)

    def top_copy(g):
        cols = pl.ds(pl.multiple_of(g * group_cols, group_cols), group_cols)
        return pltpu.make_async_copy(top.at[:, cols], out_ref.at[pl.ds(0, TOP), cols], t_sem)

    def piece(ref):
        return ref.at[pl.ds(0, SPREAD_ROWS), pl.ds(SPREAD_STEP * step_cols, step_cols)]

    def rest_copy():
        lower = pl.ds(SPREAD_ROWS, rows - SPREAD_ROWS)
        cols = pl.ds(SPREAD_STEP * step_cols, step_cols)
        return to_top(obuf.at[lower, cols], out_ref.at[lower, cols], o_send, o_recv)

    def to_helper(slot):
        return pltpu.make_async_remote_copy(
            src_ref=piece(obuf),
            dst_ref=spread.at[slot],
            send_sem=o_send,
            recv_sem=h_recv.at[slot],
            device_id=(pipe, HELPED[slot][1]),
            device_id_type=MESH,
        )

    def from_helper(slot):
        return pltpu.make_async_remote_copy(
            src_ref=spread.at[slot],
            dst_ref=piece(out_ref),
            send_sem=h_send.at[slot],
            recv_sem=o_recv,
            device_id=(right, HELPED[slot][0]),
            device_id_type=MESH,
        )

    row = lax.broadcasted_iota(jnp.int32, (TOP, TOP), 0)
    lane = lax.broadcasted_iota(jnp.int32, (TOP, TOP), 1)

    def pack(step):
        first, second = weights[0], weights[1]
        packed[step] = jnp.where(row >= lane, first, second.T).astype(packed.dtype)
        diagonal = jnp.sum(jnp.where(row == lane, second, 0.0), axis=1, keepdims=True)
        at = 3 * lax.rem(step, group_steps)
        known = jnp.where(lane == at, sums[0], tile[...])
        known = jnp.where(lane == at + 1, sums[1], known)
        tile[...] = jnp.where(lane == at + 2, diagonal, known)

    def unpack(g):
        known = facts[g].T
        for k in range(group_steps):
            pair = packed[g * group_steps + k].astype(jnp.float32)
            diagonal = known[:, 3 * k + 2 : 3 * k + 3]
            first = jnp.where(row >= lane, pair, 0.0)
            second = jnp.where(row > lane, pair.T, jnp.where(row == lane, diagonal, 0.0))
            for at, part in ((0, first), (1, second)):
                product = jnp.dot(
                    part.astype(jnp.bfloat16), vtop[g], preferred_element_type=jnp.float32
                )
                start = pl.multiple_of(g * group_cols, group_cols) + (2 * k + at) * DH
                cols = pl.ds(pl.multiple_of(start, DH), DH)
                top[:, cols] = (product / known[:, 3 * k + at : 3 * k + at + 1]).astype(top.dtype)

    doc_copy = pltpu.make_async_copy(doc_hbm, doc_ref, doc_sem)
    doc_copy.start()

    def fetch_own():
        for g in range(HK):
            for copy in own_copies(g):
                copy.start()
        q_copy.start()

    def fill_bias():
        doc_copy.wait()
        bias[0] = jnp.zeros(bias.shape[1:], jnp.float32)
        own_doc = doc_ref[0, ctx]
        for d in range(window):
            block = jnp.maximum(ctx - d, 0)
            seen = (doc_ref[0, block] == own_doc) & (ctx >= d)
            bias[0, d : d + 1, :] = jnp.full((1, DH), jnp.where(seen, 0.0, HIDDEN), jnp.float32)

    @pl.when(jnp.logical_not(ends))
    def _():
        fetch_own()
        fill_bias()

    pl.semaphore_wait(barrier, met)
    moved_q().start()

    @pl.when(guides)
    def _():
        pl.semaphore_signal(go_sem, inc=1, device_id=(right, ctx), device_id_type=MESH)

    @pl.when(ends)
    def _():
        fetch_own()
        fill_bias()

    all_own().wait()
    moved_kv().start()
    moved_bias().start()
    pl.when(packs)(lambda: vtop_copy().start())
    pl.when(ends)(lambda: pl.semaphore_wait(go_sem, 1))

    def start_direct(g):
        if g == moved:
            moved_kv().wait_recv()
            moved_bias().wait_recv()
        for d in range(2, window, 2):
            pl.when(ctx + d < n_ctx)(lambda d=d: kv_copy(g, 0, d, lax.rem(ctx + d, n_ctx)).start())

    def pass_on(g):
        pl.when(relays(0))(lambda: kv_copy(g, 0, 1, sibling).start())
        for d in range(2, window, 2):
            pl.when(ctx >= d)(functools.partial(wait_block, g, d))
            pl.when(relays(d))(lambda d=d: kv_copy(g, d, d + turn, sibling).start())

    def end_gather(g):
        for d in range(1, window, 2):
            pl.when(ctx >= d)(functools.partial(wait_block, g, d))

    start_direct(0)
    for d in range(1, window):

        @pl.when(ctx < d)
        def _():
            place = pl.ds((last - d) * rows, rows)
            for g in range(HK):
                for which in range(2):
                    kvbuf[g, which, place, :] = jnp.zeros((rows, DH), kvbuf.dtype)

    pass_on(0)
    start_direct(1)
    q_copy.wait()
    factor = math.log2(math.e) / math.sqrt(DH)

    @pl.loop(0, steps)
    def _(step):
        g = step // group_steps

        @pl.when(lax.rem(step, group_steps) == 0)
        def _():
            pl.when(g == moved)(lambda: moved_q().wait_recv())
            end_gather(g)

        @pl.when(step == 3)
        def _():
            pass_on(1)
            start_direct(2)

        @pl.when(step == 7)
        def _():
            pass_on(2)
            start_direct(3)

        @pl.when(step == 11)
        def _():
            pass_on(3)

        which = jnp.where(g == moved, 1, 0)
        causal = lax.broadcasted_iota(jnp.int32, (rows, rows), 0) >= lax.broadcasted_iota(
            jnp.int32, (rows, rows), 1
        )
        for at in range(STEP_HEADS):
            cols = pl.ds(pl.multiple_of(step * step_cols + at * DH, DH), DH)
            query = qbuf[:, cols]
            scores = []
            top = None
            for d in range(window):
                place = pl.ds((last - d) * rows, rows)
                part = lax.dot_general(
                    query,
                    kvbuf[g, 0, place, :],
                    (((1,), (1,)), ((), ())),
                    preferred_element_type=jnp.float32,
                )
                if d == 0:
                    part = jnp.where(causal, part, -HIDDEN)
                scores.append(part)
                lanes = part[:, :DH]
                for c in range(1, rows // DH):
                    lanes = jnp.maximum(lanes, part[:, c * DH : (c + 1) * DH])
                if d > 0:
                    lanes = lanes - bias[which, d : d + 1, :]
                top = lanes if top is None else jnp.maximum(top, lanes)
            row_top = jnp.broadcast_to(jnp.max(top, axis=1, keepdims=True), (rows, DH))
            total = None
            acc = None
            for d in range(window):
                place = pl.ds((last - d) * rows, rows)
                offset = row_top
                if d > 0:
                    offset = row_top + bias[which, d : d + 1, :]
                rounded = []
                for c in range(rows // DH):
                    lanes = jnp.exp2((scores[d][:, c * DH : (c + 1) * DH] - offset) * factor)
                    total = lanes if total is None else total + lanes
                    if d == 0 and c == 0:
                        weights[at] = lanes[:TOP]
                    rounded.append(lanes.astype(jnp.bfloat16))
                product = jnp.dot(
                    jnp.concatenate(rounded, axis=1),
                    kvbuf[g, 1, place, :],
                    preferred_element_type=jnp.float32,
                )
                acc = product if acc is None else acc + product
            row_total = jnp.sum(total, axis=1, keepdims=True)
            sums[at] = jnp.broadcast_to(row_total[:TOP], (TOP, TOP))
            obuf[:, cols] = (acc / row_total).astype(obuf.dtype)

        done = pl.ds(pl.multiple_of(step * step_cols, step_cols), step_cols)

        later = lax.rem(step, 2) == 1
        pair = pl.ds(pl.multiple_of((step - lax.rem(step, 2)) * step_cols, 2 * step_cols), 2 * step_cols)

        @pl.when((step < group_steps) & jnp.logical_not(packs | (spreads & (step == SPREAD_STEP))))
        def _():
            out_copy(done).start()

        @pl.when((step >= group_steps) & (g < moved) & later & jnp.logical_not(packs))
        def _():
            out_copy(pair).start()

        @pl.when((g < moved) & packs)
        def _():
            pack(step)
            pl.when(step < group_steps)(lambda: half_copy(done).start())
            pl.when((step >= group_steps) & later)(lambda: half_copy(pair).start())

            @pl.when(lax.rem(step, group_steps) == group_steps - 1)
            def _():
                facts[g] = tile[...].T
                packed_copy(g).start()
                facts_copy(g).start()

        @pl.when(spreads & (step == SPREAD_STEP))
        def _():
            for slot, (helped, _) in enumerate(HELPED):
                pl.when(ctx == helped)(lambda slot=slot: to_helper(slot).start())
            rest_copy().start()

        for slot, (_, helper) in enumerate(HELPED):

            @pl.when(ends & (ctx == helper) & (step == SPREAD_LATER))
            def _(slot=slot):
                to_helper(slot).wait_recv()
                from_helper(slot).start()

        @pl.when(g == moved)
        def _():
            out_local(done).start()

    moved_kv().wait_send()
    moved_bias().wait_send()

    for count in range(1, window + 1):

        @pl.when(sends == count)
        def _(count=count):
            for g in range(HK):
                blocks = kvbuf.at[g, :, pl.ds(0, count * rows)]
                pltpu.make_async_copy(blocks, blocks, kv_send.at[g]).wait()

    for slot, (_, helper) in enumerate(HELPED):
        pl.when(ends & (ctx == helper))(lambda slot=slot: from_helper(slot).wait_send())

    @pl.when(unpacks)
    def _():
        vtop_copy().wait_recv()

        @pl.loop(0, moved)
        def _(g):
            packed_copy(g).wait_recv()
            facts_copy(g).wait_recv()
            unpack(g)
            top_copy(g).start()

        everything = pl.ds(0, moved * group_cols)
        pltpu.make_async_copy(top.at[:, everything], out_ref.at[pl.ds(0, TOP), everything], t_sem).wait()

    @pl.when(packs)
    def _():
        vtop_copy().wait_send()
        to_top(packed, packed, y_send, y_recv.at[0]).wait_send()
        sent = facts.at[:, pl.ds(0, 16)]
        to_top(sent, sent, f_send, f_recv.at[0]).wait_send()

    whole = pl.ds(0, HQ * DH)
    lower = pl.ds(0, group_cols + moved * group_cols * (rows - TOP) // rows)
    pl.when(packs)(lambda: out_copy(lower).wait_send())
    pl.when(jnp.logical_not(packs))(lambda: out_copy(whole).wait_send())
    pl.when(unpacks)(lambda: out_copy(lower).wait_recv())
    pl.when(jnp.logical_not(unpacks))(lambda: out_copy(whole).wait_recv())


def shards(n_pipe, n_ctx, queries, keys, values, doc_ids):
    rows = queries.shape[1]
    window = n_ctx // 2 + 1
    bias_rows = (window + 7) // 8 * 8
    dma = pltpu.SemaphoreType.DMA
    anywhere = pl.BlockSpec(memory_space=pl.ANY)
    handed = pl.pallas_call(
        functools.partial(kernel, n_pipe, n_ctx, window, rows),
        out_shape=jax.ShapeDtypeStruct((rows, HQ * DH), jnp.bfloat16),
        in_specs=[pl.BlockSpec(memory_space=pltpu.HBM)] * 4,
        out_specs=anywhere,
        scratch_shapes=[
            pltpu.VMEM((rows, HQ * DH), jnp.bfloat16),
            pltpu.VMEM((HK, 2, window * rows, DH), jnp.bfloat16),
            pltpu.VMEM((rows, HQ * DH), jnp.bfloat16),
            pltpu.VMEM((2, bias_rows, DH), jnp.float32),
            pltpu.SMEM(doc_ids.shape, jnp.int32),
            pltpu.VMEM((len(HELPED), SPREAD_ROWS, STEP_HEADS * DH), jnp.bfloat16),
            pltpu.VMEM((2, rows, DH), jnp.bfloat16),
            pltpu.VMEM((STEP_HEADS, TOP, TOP), jnp.float32),
            pltpu.VMEM((STEP_HEADS, TOP, TOP), jnp.float32),
            pltpu.VMEM((TOP, TOP), jnp.float32),
            pltpu.VMEM(((HK - 1) * PER_GROUP // STEP_HEADS, TOP, TOP), jnp.bfloat16),
            pltpu.VMEM((HK - 1, TOP, TOP), jnp.float32),
            pltpu.VMEM((HK - 1, TOP, DH), jnp.bfloat16),
            pltpu.VMEM((TOP, (HK - 1) * PER_GROUP * DH), jnp.bfloat16),
            dma,
            dma,
            dma,
            dma((HK,)),
            dma((HK, window - 1)),
            dma((2,)),
            dma((3,)),
            dma,
            dma,
            dma((len(HELPED),)),
            dma((len(HELPED),)),
            dma,
            dma((HK - 1,)),
            dma,
            dma((HK - 1,)),
            dma,
            dma,
            dma,
            pltpu.SemaphoreType.REGULAR,
        ],
        compiler_params=pltpu.CompilerParams(
            collective_id=0, has_side_effects=True, vmem_limit_bytes=48 * 1024 * 1024
        ),
        name="relay_attention",
    )(*(pltpu.with_memory_space_constraint(x, pltpu.HBM) for x in (doc_ids, queries[0], keys[0], values[0])))
    return handed[None]


def solution(mesh):
    placed = (
        P("pipe", "ctx", None),
        P("pipe", "ctx", None),
        P("pipe", "ctx", None),
        P("pipe", None),
    )
    return jax.shard_map(
        functools.partial(shards, mesh.shape["pipe"], mesh.shape["ctx"]),
        mesh=mesh,
        in_specs=placed,
        out_specs=P("pipe", "ctx", None),
        check_vma=False,
    )
```

```python
import functools
import math

import jax
import jax.numpy as jnp
from jax import lax
from jax.experimental import pallas as pl
from jax.experimental.pallas import tpu as pltpu
from jax.sharding import PartitionSpec as P

HQ = 32
HK = 4
DH = 128
PER_GROUP = HQ // HK
STEP_HEADS = 2
SPREAD_STEP = 2
SPREAD_LATER = 9
HELPED = ((2, 0), (4, 1), (6, 0))
SPREAD_ROWS = 160
TOP = 128
HIDDEN = 1e30
MESH = pl.DeviceIdType.MESH


def kernel(
    n_pipe,
    n_ctx,
    window,
    rows,
    doc_hbm,
    q_ref,
    k_ref,
    v_ref,
    out_ref,
    qbuf,
    kvbuf,
    obuf,
    bias,
    doc_ref,
    spread,
    lent,
    weights,
    sums,
    tile,
    packed,
    facts,
    vtop,
    qtop,
    top,
    doc_sem,
    q_sem,
    own_sem,
    kv_send,
    kv_recv,
    z_send,
    z_recv,
    o_send,
    o_recv,
    h_send,
    h_recv,
    y_recv,
    f_recv,
    v_recv,
    t_sem,
    go_sem,
):
    pipe = lax.axis_index("pipe")
    ctx = lax.axis_index("ctx")
    right = lax.rem(pipe + 1, n_pipe)
    left = lax.rem(pipe + n_pipe - 1, n_pipe)
    moved = HK - 1
    group_cols = PER_GROUP * DH
    step_cols = STEP_HEADS * DH
    steps = HQ // STEP_HEADS
    group_steps = PER_GROUP // STEP_HEADS
    last = window - 1
    factor = math.log2(math.e) / math.sqrt(DH)
    own_rows = pl.ds(last * rows, rows)
    low = pl.ds(TOP, rows - TOP)
    sent_cols = pl.ds(0, moved * group_cols)
    moved_cols = pl.ds(moved * group_cols, group_cols)

    core = lax.rem(ctx, 2)
    turn = 1 - 2 * core
    sibling = ctx + turn
    barrier = pltpu.get_barrier_semaphore()
    ends = pipe == n_pipe - 1
    guides = pipe == n_pipe - 2
    hall = jnp.where(ends, left, pipe)
    packs = ends & (ctx == 0)
    unpacks = (pipe == 0) & (ctx == 0)
    spreads = ends & functools.reduce(jnp.logical_or, [ctx == helped for helped, _ in HELPED])

    def greet(pipe_to, ctx_to):
        pl.semaphore_signal(barrier, inc=1, device_id=(pipe_to, ctx_to), device_id_type=MESH)

    greet(left, ctx)
    pl.when((core == 1) | (ctx >= 2))(lambda: greet(hall, sibling))
    met = jnp.where((core == 0) | (ctx >= 2), 1, 0)
    for d in range(2, window, 2):
        pl.when(ctx >= d)(lambda d=d: greet(hall, lax.rem(ctx + n_ctx - d, n_ctx)))
        met = met + jnp.where(ctx + d < n_ctx, 1, 0)
    met = 1 + jnp.where(ends, 0, jnp.where(guides, 2 * met, met))
    for helped, helper in HELPED:
        pl.when(ends & (ctx == helper))(lambda helped=helped: greet(hall, helped))
        met = met + jnp.where(guides & (ctx == helped), 1, 0)

    def own_copies(g):
        cols = pl.ds(g * DH, DH)
        place = lent if g == moved else kvbuf.at[g, :, own_rows]
        return (
            pltpu.make_async_copy(k_ref.at[:, cols], place.at[0], own_sem),
            pltpu.make_async_copy(v_ref.at[:, cols], place.at[1], own_sem),
        )

    def all_own():
        blocks = kvbuf.at[:, :, own_rows]
        return pltpu.make_async_copy(blocks, blocks, own_sem)

    q_copy = pltpu.make_async_copy(q_ref.at[:, sent_cols], qbuf.at[:, sent_cols], q_sem)

    def kv_copy(g, source, target, ctx_to):
        from_rows = pl.ds(pl.multiple_of((last - source) * rows, rows), rows)
        to_rows = pl.ds(pl.multiple_of((last - target) * rows, rows), rows)
        return pltpu.make_async_remote_copy(
            src_ref=kvbuf.at[g, :, from_rows],
            dst_ref=kvbuf.at[g, :, to_rows],
            send_sem=kv_send,
            recv_sem=kv_recv.at[g, target - 1],
            device_id=(pipe, ctx_to),
            device_id_type=MESH,
        )

    def wait_block(g, d):
        kv_copy(g, 0, d, sibling).wait_recv()

    def relays(d):
        fits = core == 0 if d == 0 else ctx >= d
        return fits & (core == 1) if d == last else fits

    sends = jnp.int32(0)
    for d in range(0, window, 2):
        sends = sends + jnp.where(relays(d), 1, 0)
        if d > 0:
            sends = sends + jnp.where(ctx + d < n_ctx, 1, 0)

    def to_right(source, target, at):
        return pltpu.make_async_remote_copy(
            src_ref=source,
            dst_ref=target,
            send_sem=o_send if at == 2 else z_send.at[at],
            recv_sem=z_recv.at[at],
            device_id=(right, ctx),
            device_id_type=MESH,
        )

    def moved_kv():
        return to_right(lent, kvbuf.at[moved, :, own_rows], 0)

    def moved_bias():
        return to_right(bias.at[0], bias.at[1], 1)

    def moved_q():
        return to_right(q_ref.at[:, moved_cols], qbuf.at[:, moved_cols], 2)

    def moved_low_q():
        return to_right(q_ref.at[low, moved_cols], qbuf.at[low, moved_cols], 2)

    def out_copy(cols):
        return pltpu.make_async_remote_copy(
            src_ref=obuf.at[:, cols],
            dst_ref=out_ref.at[:, cols],
            send_sem=o_send,
            recv_sem=o_recv,
            device_id=(right, ctx),
            device_id_type=MESH,
        )

    def out_local(cols):
        return pltpu.make_async_copy(obuf.at[:, cols], out_ref.at[:, cols], o_recv)

    def half_local(cols):
        return pltpu.make_async_copy(obuf.at[low, cols], out_ref.at[low, cols], o_recv)

    qtop_copy = pltpu.make_async_copy(q_ref.at[pl.ds(0, TOP), moved_cols], qtop, t_sem)

    def half_copy(cols):
        return pltpu.make_async_remote_copy(
            src_ref=obuf.at[low, cols],
            dst_ref=out_ref.at[low, cols],
            send_sem=o_send,
            recv_sem=o_recv,
            device_id=(right, ctx),
            device_id_type=MESH,
        )

    def to_top(source, target, send_sem, recv_sem):
        return pltpu.make_async_remote_copy(
            src_ref=source,
            dst_ref=target,
            send_sem=send_sem,
            recv_sem=recv_sem,
            device_id=(right, ctx),
            device_id_type=MESH,
        )

    def packed_copy(g):
        tiles = packed.at[pl.ds(g * group_steps, group_steps)]
        return to_top(tiles, tiles, q_sem, y_recv.at[g])

    def facts_copy(g):
        lines = facts.at[g, pl.ds(0, 16)]
        return to_top(lines, lines, doc_sem, f_recv.at[g])

    def vtop_copy():
        sent = pl.ds(0, moved)
        return to_top(
            kvbuf.at[sent, 1, pl.ds(last * rows, TOP)], vtop.at[sent], own_sem, v_recv
        )

    def top_copy(g):
        cols = pl.ds(pl.multiple_of(g * group_cols, group_cols), group_cols)
        return pltpu.make_async_copy(top.at[:, cols], out_ref.at[pl.ds(0, TOP), cols], t_sem)

    def piece(ref):
        return ref.at[pl.ds(0, SPREAD_ROWS), pl.ds(SPREAD_STEP * step_cols, step_cols)]

    def rest_copy():
        lower = pl.ds(SPREAD_ROWS, rows - SPREAD_ROWS)
        cols = pl.ds(SPREAD_STEP * step_cols, step_cols)
        return to_top(obuf.at[lower, cols], out_ref.at[lower, cols], o_send, o_recv)

    def to_helper(slot):
        return pltpu.make_async_remote_copy(
            src_ref=piece(obuf),
            dst_ref=spread.at[slot],
            send_sem=o_send,
            recv_sem=h_recv.at[slot],
            device_id=(pipe, HELPED[slot][1]),
            device_id_type=MESH,
        )

    def from_helper(slot):
        return pltpu.make_async_remote_copy(
            src_ref=spread.at[slot],
            dst_ref=piece(out_ref),
            send_sem=h_send.at[slot],
            recv_sem=o_recv,
            device_id=(right, HELPED[slot][0]),
            device_id_type=MESH,
        )

    row = lax.broadcasted_iota(jnp.int32, (TOP, TOP), 0)
    lane = lax.broadcasted_iota(jnp.int32, (TOP, TOP), 1)

    def pack(step):
        first, second = weights[0], weights[1]
        packed[step] = jnp.where(row >= lane, first, second.T).astype(packed.dtype)
        diagonal = jnp.sum(jnp.where(row == lane, second, 0.0), axis=1, keepdims=True)
        at = 3 * lax.rem(step, group_steps)
        known = jnp.where(lane == at, sums[0], tile[...])
        known = jnp.where(lane == at + 1, sums[1], known)
        tile[...] = jnp.where(lane == at + 2, diagonal, known)

    def pack_moved(k):
        for at in range(STEP_HEADS):
            cols = pl.ds(pl.multiple_of(k * step_cols + at * DH, DH), DH)
            scores = lax.dot_general(
                qtop[:, cols],
                lent[0, :TOP, :],
                (((1,), (1,)), ((), ())),
                preferred_element_type=jnp.float32,
            )
            scores = jnp.where(row >= lane, scores, -HIDDEN)
            row_top = jnp.max(scores, axis=1, keepdims=True)
            seen = jnp.exp2((scores - row_top) * factor)
            weights[at] = seen
            sums[at] = jnp.broadcast_to(jnp.sum(seen, axis=1, keepdims=True), (TOP, TOP))
        pack(moved * group_steps + k)

    def hand_packed(g):
        facts[g] = tile[...].T
        packed_copy(g).start()
        facts_copy(g).start()

    def unpack(g):
        known = facts[g].T
        for k in range(group_steps):
            pair = packed[g * group_steps + k].astype(jnp.float32)
            diagonal = known[:, 3 * k + 2 : 3 * k + 3]
            first = jnp.where(row >= lane, pair, 0.0)
            second = jnp.where(row > lane, pair.T, jnp.where(row == lane, diagonal, 0.0))
            for at, part in ((0, first), (1, second)):
                product = jnp.dot(
                    part.astype(jnp.bfloat16), vtop[g], preferred_element_type=jnp.float32
                )
                start = pl.multiple_of(g * group_cols, group_cols) + (2 * k + at) * DH
                cols = pl.ds(pl.multiple_of(start, DH), DH)
                top[:, cols] = (product / known[:, 3 * k + at : 3 * k + at + 1]).astype(top.dtype)

    doc_copy = pltpu.make_async_copy(doc_hbm, doc_ref, doc_sem)
    doc_copy.start()

    def fetch_own():
        for g in range(HK):
            for copy in own_copies(g):
                copy.start()
        q_copy.start()

    def fill_bias():
        doc_copy.wait()
        bias[0] = jnp.zeros(bias.shape[1:], jnp.float32)
        own_doc = doc_ref[0, ctx]
        for d in range(window):
            block = jnp.maximum(ctx - d, 0)
            seen = (doc_ref[0, block] == own_doc) & (ctx >= d)
            bias[0, d : d + 1, :] = jnp.full((1, DH), jnp.where(seen, 0.0, HIDDEN), jnp.float32)

    @pl.when(jnp.logical_not(ends))
    def _():
        fetch_own()
        fill_bias()

    pl.semaphore_wait(barrier, met)
    pl.when(packs)(lambda: moved_low_q().start())
    pl.when(jnp.logical_not(packs))(lambda: moved_q().start())
    pl.when(packs)(qtop_copy.start)

    @pl.when(guides)
    def _():
        pl.semaphore_signal(go_sem, inc=1, device_id=(right, ctx), device_id_type=MESH)

    @pl.when(ends)
    def _():
        fetch_own()
        fill_bias()

    all_own().wait()
    moved_kv().start()
    moved_bias().start()
    pl.when(packs)(lambda: vtop_copy().start())
    pl.when(ends)(lambda: pl.semaphore_wait(go_sem, 1))

    def start_direct(g):
        if g == moved:
            moved_kv().wait_recv()
            moved_bias().wait_recv()
        for d in range(2, window, 2):
            pl.when(ctx + d < n_ctx)(lambda d=d: kv_copy(g, 0, d, lax.rem(ctx + d, n_ctx)).start())

    def pass_on(g):
        pl.when(relays(0))(lambda: kv_copy(g, 0, 1, sibling).start())
        for d in range(2, window, 2):
            pl.when(ctx >= d)(functools.partial(wait_block, g, d))
            pl.when(relays(d))(lambda d=d: kv_copy(g, d, d + turn, sibling).start())

    def end_gather(g):
        for d in range(1, window, 2):
            pl.when(ctx >= d)(functools.partial(wait_block, g, d))

    start_direct(0)

    @pl.when(unpacks)
    def _():
        qbuf[:TOP, moved_cols] = jnp.zeros((TOP, group_cols), qbuf.dtype)

    for d in range(1, window):

        @pl.when(ctx < d)
        def _():
            place = pl.ds((last - d) * rows, rows)
            for g in range(HK):
                for which in range(2):
                    kvbuf[g, which, place, :] = jnp.zeros((rows, DH), kvbuf.dtype)

    pass_on(0)
    start_direct(1)
    q_copy.wait()

    @pl.loop(0, steps)
    def _(step):
        g = step // group_steps

        @pl.when(lax.rem(step, group_steps) == 0)
        def _():
            pl.when((g == moved) & unpacks)(lambda: moved_low_q().wait_recv())
            pl.when((g == moved) & jnp.logical_not(unpacks))(lambda: moved_q().wait_recv())
            end_gather(g)

        @pl.when(step == 3)
        def _():
            pass_on(1)
            start_direct(2)

        @pl.when(step == 7)
        def _():
            pass_on(2)
            start_direct(3)

        @pl.when(step == 11)
        def _():
            pass_on(3)

        which = jnp.where(g == moved, 1, 0)
        causal = lax.broadcasted_iota(jnp.int32, (rows, rows), 0) >= lax.broadcasted_iota(
            jnp.int32, (rows, rows), 1
        )
        for at in range(STEP_HEADS):
            cols = pl.ds(pl.multiple_of(step * step_cols + at * DH, DH), DH)
            query = qbuf[:, cols]
            scores = []
            top = None
            for d in range(window):
                place = pl.ds((last - d) * rows, rows)
                part = lax.dot_general(
                    query,
                    kvbuf[g, 0, place, :],
                    (((1,), (1,)), ((), ())),
                    preferred_element_type=jnp.float32,
                )
                if d == 0:
                    part = jnp.where(causal, part, -HIDDEN)
                scores.append(part)
                lanes = part[:, :DH]
                for c in range(1, rows // DH):
                    lanes = jnp.maximum(lanes, part[:, c * DH : (c + 1) * DH])
                if d > 0:
                    lanes = lanes - bias[which, d : d + 1, :]
                top = lanes if top is None else jnp.maximum(top, lanes)
            row_top = jnp.broadcast_to(jnp.max(top, axis=1, keepdims=True), (rows, DH))
            total = None
            acc = None
            for d in range(window):
                place = pl.ds((last - d) * rows, rows)
                offset = row_top
                if d > 0:
                    offset = row_top + bias[which, d : d + 1, :]
                rounded = []
                for c in range(rows // DH):
                    lanes = jnp.exp2((scores[d][:, c * DH : (c + 1) * DH] - offset) * factor)
                    total = lanes if total is None else total + lanes
                    if d == 0 and c == 0:
                        weights[at] = lanes[:TOP]
                    rounded.append(lanes.astype(jnp.bfloat16))
                product = jnp.dot(
                    jnp.concatenate(rounded, axis=1),
                    kvbuf[g, 1, place, :],
                    preferred_element_type=jnp.float32,
                )
                acc = product if acc is None else acc + product
            row_total = jnp.sum(total, axis=1, keepdims=True)
            sums[at] = jnp.broadcast_to(row_total[:TOP], (TOP, TOP))
            obuf[:, cols] = (acc / row_total).astype(obuf.dtype)

        done = pl.ds(pl.multiple_of(step * step_cols, step_cols), step_cols)

        later = lax.rem(step, 2) == 1
        pair = pl.ds(pl.multiple_of((step - lax.rem(step, 2)) * step_cols, 2 * step_cols), 2 * step_cols)

        @pl.when((step < group_steps) & jnp.logical_not(packs | (spreads & (step == SPREAD_STEP))))
        def _():
            out_copy(done).start()

        @pl.when((step >= group_steps) & (g < moved) & later & jnp.logical_not(packs))
        def _():
            out_copy(pair).start()

        @pl.when((g < moved) & packs)
        def _():
            pack(step)
            pl.when(step < group_steps)(lambda: half_copy(done).start())
            pl.when((step >= group_steps) & later)(lambda: half_copy(pair).start())

            @pl.when(lax.rem(step, group_steps) == group_steps - 1)
            def _():
                hand_packed(g)

            @pl.when(step == group_steps - 1)
            def _():
                qtop_copy.wait()

                @pl.loop(0, group_steps)
                def _(k):
                    pack_moved(k)

                hand_packed(moved)

        @pl.when(spreads & (step == SPREAD_STEP))
        def _():
            for slot, (helped, _) in enumerate(HELPED):
                pl.when(ctx == helped)(lambda slot=slot: to_helper(slot).start())
            rest_copy().start()

        for slot, (_, helper) in enumerate(HELPED):

            @pl.when(ends & (ctx == helper) & (step == SPREAD_LATER))
            def _(slot=slot):
                to_helper(slot).wait_recv()
                from_helper(slot).start()

        pl.when((g == moved) & unpacks)(lambda: half_local(done).start())
        pl.when((g == moved) & jnp.logical_not(unpacks))(lambda: out_local(done).start())

    moved_kv().wait_send()
    moved_bias().wait_send()

    for count in range(1, window + 1):

        @pl.when(sends == count)
        def _(count=count):
            blocks = kvbuf.at[:, :, pl.ds(0, count * rows)]
            pltpu.make_async_copy(blocks, blocks, kv_send).wait()

    for slot, (_, helper) in enumerate(HELPED):
        pl.when(ends & (ctx == helper))(lambda slot=slot: from_helper(slot).wait_send())

    @pl.when(unpacks)
    def _():
        vtop_copy().wait_recv()
        vtop[moved] = kvbuf[moved, 1, pl.ds(last * rows, TOP), :]

        @pl.loop(0, HK)
        def _(g):
            packed_copy(g).wait_recv()
            facts_copy(g).wait_recv()
            unpack(g)
            top_copy(g).start()

        pltpu.make_async_copy(top, out_ref.at[pl.ds(0, TOP)], t_sem).wait()

    @pl.when(packs)
    def _():
        vtop_copy().wait_send()
        to_top(packed, packed, q_sem, y_recv.at[0]).wait_send()
        sent = facts.at[:, pl.ds(0, 16)]
        to_top(sent, sent, doc_sem, f_recv.at[0]).wait_send()

    whole = pl.ds(0, HQ * DH)
    lower = pl.ds(0, HQ * DH * (rows - TOP) // rows)
    pl.when(packs)(lambda: out_copy(lower).wait_send())
    pl.when(jnp.logical_not(packs))(lambda: out_copy(whole).wait_send())
    pl.when(unpacks)(lambda: out_copy(lower).wait_recv())
    pl.when(jnp.logical_not(unpacks))(lambda: out_copy(whole).wait_recv())


def shards(n_pipe, n_ctx, queries, keys, values, doc_ids):
    rows = queries.shape[1]
    window = n_ctx // 2 + 1
    bias_rows = (window + 7) // 8 * 8
    dma = pltpu.SemaphoreType.DMA
    anywhere = pl.BlockSpec(memory_space=pl.ANY)
    handed = pl.pallas_call(
        functools.partial(kernel, n_pipe, n_ctx, window, rows),
        out_shape=jax.ShapeDtypeStruct((rows, HQ * DH), jnp.bfloat16),
        in_specs=[pl.BlockSpec(memory_space=pltpu.HBM)] * 4,
        out_specs=anywhere,
        scratch_shapes=[
            pltpu.VMEM((rows, HQ * DH), jnp.bfloat16),
            pltpu.VMEM((HK, 2, window * rows, DH), jnp.bfloat16),
            pltpu.VMEM((rows, HQ * DH), jnp.bfloat16),
            pltpu.VMEM((2, bias_rows, DH), jnp.float32),
            pltpu.SMEM(doc_ids.shape, jnp.int32),
            pltpu.VMEM((len(HELPED), SPREAD_ROWS, STEP_HEADS * DH), jnp.bfloat16),
            pltpu.VMEM((2, rows, DH), jnp.bfloat16),
            pltpu.VMEM((STEP_HEADS, TOP, TOP), jnp.float32),
            pltpu.VMEM((STEP_HEADS, TOP, TOP), jnp.float32),
            pltpu.VMEM((TOP, TOP), jnp.float32),
            pltpu.VMEM((HQ // STEP_HEADS, TOP, TOP), jnp.bfloat16),
            pltpu.VMEM((HK, TOP, TOP), jnp.float32),
            pltpu.VMEM((HK, TOP, DH), jnp.bfloat16),
            pltpu.VMEM((TOP, PER_GROUP * DH), jnp.bfloat16),
            pltpu.VMEM((TOP, HQ * DH), jnp.bfloat16),
            dma,
            dma,
            dma,
            dma,
            dma((HK, window - 1)),
            dma((2,)),
            dma((3,)),
            dma,
            dma,
            dma((len(HELPED),)),
            dma((len(HELPED),)),
            dma((HK,)),
            dma((HK,)),
            dma,
            dma,
            pltpu.SemaphoreType.REGULAR,
        ],
        compiler_params=pltpu.CompilerParams(
            collective_id=0, has_side_effects=True, vmem_limit_bytes=48 * 1024 * 1024
        ),
        name="relay_attention",
    )(*(pltpu.with_memory_space_constraint(x, pltpu.HBM) for x in (doc_ids, queries[0], keys[0], values[0])))
    return handed[None]


def solution(mesh):
    placed = (
        P("pipe", "ctx", None),
        P("pipe", "ctx", None),
        P("pipe", "ctx", None),
        P("pipe", None),
    )
    return jax.shard_map(
        functools.partial(shards, mesh.shape["pipe"], mesh.shape["ctx"]),
        mesh=mesh,
        in_specs=placed,
        out_specs=P("pipe", "ctx", None),
        check_vma=False,
    )
```

```python
import functools
import math

import jax
import jax.numpy as jnp
from jax import lax
from jax.experimental import pallas as pl
from jax.experimental.pallas import tpu as pltpu
from jax.sharding import PartitionSpec as P

HQ = 32
HK = 4
DH = 128
PER_GROUP = HQ // HK
STEP_HEADS = 2
SPREAD_STEP = 2
SPREAD_LATER = 13
HELPED = ((2, 0, 0), (4, 1, 0), (6, 0, 1))
SPREAD_ROWS = 208
TOP = 128
HIDDEN = 1e30
MESH = pl.DeviceIdType.MESH


def kernel(
    n_pipe,
    n_ctx,
    window,
    rows,
    doc_hbm,
    q_ref,
    k_ref,
    v_ref,
    out_ref,
    qbuf,
    kvbuf,
    obuf,
    bias,
    doc_ref,
    spread,
    lent,
    weights,
    sums,
    tile,
    packed,
    facts,
    tiles_in,
    facts_in,
    vtop,
    qtop,
    top,
    doc_sem,
    q_sem,
    own_sem,
    kv_send,
    kv_recv,
    z_send,
    z_recv,
    o_send,
    o_recv,
    h_send,
    h_recv,
    y_recv,
    t_sem,
    go_sem,
):
    pipe = lax.axis_index("pipe")
    ctx = lax.axis_index("ctx")
    right = lax.rem(pipe + 1, n_pipe)
    left = lax.rem(pipe + n_pipe - 1, n_pipe)
    moved = HK - 1
    group_cols = PER_GROUP * DH
    step_cols = STEP_HEADS * DH
    steps = HQ // STEP_HEADS
    group_steps = PER_GROUP // STEP_HEADS
    last = window - 1
    factor = math.log2(math.e) / math.sqrt(DH)
    own_rows = pl.ds(last * rows, rows)
    low = pl.ds(TOP, rows - TOP)
    sent_cols = pl.ds(0, moved * group_cols)
    moved_cols = pl.ds(moved * group_cols, group_cols)

    core = lax.rem(ctx, 2)
    turn = 1 - 2 * core
    sibling = ctx + turn
    barrier = pltpu.get_barrier_semaphore()
    ends = pipe == n_pipe - 1
    guides = pipe == n_pipe - 2
    hall = jnp.where(ends, left, pipe)
    packs = ctx == 0
    spreads = functools.reduce(jnp.logical_or, [ctx == helped for helped, _, _ in HELPED])

    def greet(pipe_to, ctx_to):
        pl.semaphore_signal(barrier, inc=1, device_id=(pipe_to, ctx_to), device_id_type=MESH)

    greet(left, ctx)
    pl.when((core == 1) | (ctx >= 2))(lambda: greet(hall, sibling))
    met = jnp.where((core == 0) | (ctx >= 2), 1, 0)
    for d in range(2, window, 2):
        pl.when(ctx >= d)(lambda d=d: greet(hall, lax.rem(ctx + n_ctx - d, n_ctx)))
        met = met + jnp.where(ctx + d < n_ctx, 1, 0)
    for helped, helper, _ in HELPED:
        pl.when(ctx == helper)(lambda helped=helped: greet(hall, helped))
        met = met + jnp.where(ctx == helped, 1, 0)
    met = 1 + jnp.where(ends, 0, jnp.where(guides, 2 * met, met))

    def own_copies(g):
        cols = pl.ds(g * DH, DH)
        place = lent if g == moved else kvbuf.at[g, :, own_rows]
        return (
            pltpu.make_async_copy(k_ref.at[:, cols], place.at[0], own_sem),
            pltpu.make_async_copy(v_ref.at[:, cols], place.at[1], own_sem),
        )

    def all_own():
        blocks = kvbuf.at[:, :, own_rows]
        return pltpu.make_async_copy(blocks, blocks, own_sem)

    q_copy = pltpu.make_async_copy(q_ref.at[:, sent_cols], qbuf.at[:, sent_cols], q_sem)

    def kv_copy(g, source, target, ctx_to, slot):
        from_rows = pl.ds(pl.multiple_of((last - source) * rows, rows), rows)
        to_rows = pl.ds(pl.multiple_of((last - target) * rows, rows), rows)
        return pltpu.make_async_remote_copy(
            src_ref=kvbuf.at[g, :, from_rows],
            dst_ref=kvbuf.at[g, :, to_rows],
            send_sem=kv_send,
            recv_sem=kv_recv.at[g, slot],
            device_id=(pipe, ctx_to),
            device_id_type=MESH,
        )

    def wait_block(g, d):
        kv_copy(g, 0, d, sibling, d // 2).wait_recv()

    def relays(d):
        fits = core == 0 if d == 0 else ctx >= d
        return fits & (core == 1) if d == last else fits

    sends = jnp.int32(0)
    for d in range(0, window, 2):
        sends = sends + jnp.where(relays(d), 1, 0)
        if d > 0:
            sends = sends + jnp.where(ctx + d < n_ctx, 1, 0)

    def to_right(source, target, at):
        return pltpu.make_async_remote_copy(
            src_ref=source,
            dst_ref=target,
            send_sem=o_send if at == 1 else z_send,
            recv_sem=z_recv.at[at],
            device_id=(right, ctx),
            device_id_type=MESH,
        )

    def moved_kv():
        return to_right(lent, kvbuf.at[moved, :, own_rows], 0)

    def moved_bias():
        return to_right(bias.at[0], bias.at[1], 0)

    lent_rows = kvbuf.at[0, 0, pl.ds(0, 2 * rows + 2 * bias.shape[1])]

    def moved_q():
        return to_right(q_ref.at[:, moved_cols], qbuf.at[:, moved_cols], 1)

    def moved_low_q():
        return to_right(q_ref.at[low, moved_cols], qbuf.at[low, moved_cols], 1)

    def out_copy(cols):
        return pltpu.make_async_remote_copy(
            src_ref=obuf.at[:, cols],
            dst_ref=out_ref.at[:, cols],
            send_sem=o_send,
            recv_sem=o_recv,
            device_id=(right, ctx),
            device_id_type=MESH,
        )

    def out_local(cols):
        return pltpu.make_async_copy(obuf.at[:, cols], out_ref.at[:, cols], o_recv)

    def half_local(cols):
        return pltpu.make_async_copy(obuf.at[low, cols], out_ref.at[low, cols], o_recv)

    qtop_copy = pltpu.make_async_copy(q_ref.at[pl.ds(0, TOP), moved_cols], qtop, t_sem)

    def half_copy(cols):
        return pltpu.make_async_remote_copy(
            src_ref=obuf.at[low, cols],
            dst_ref=out_ref.at[low, cols],
            send_sem=o_send,
            recv_sem=o_recv,
            device_id=(right, ctx),
            device_id_type=MESH,
        )

    def to_top(source, target, send_sem, recv_sem):
        return pltpu.make_async_remote_copy(
            src_ref=source,
            dst_ref=target,
            send_sem=send_sem,
            recv_sem=recv_sem,
            device_id=(right, ctx),
            device_id_type=MESH,
        )

    def packed_copy(g):
        tiles = pl.ds(g * group_steps, group_steps)
        return to_top(packed.at[tiles], tiles_in.at[tiles], q_sem, y_recv.at[g])

    def facts_copy(g):
        lines = pl.ds(0, 16)
        return to_top(facts.at[g, lines], facts_in.at[g, lines], doc_sem, y_recv.at[g])

    def vtop_copy():
        sent = pl.ds(0, moved)
        return to_top(
            kvbuf.at[sent, 1, pl.ds(last * rows, TOP)], vtop.at[sent], own_sem, y_recv.at[0]
        )

    def top_copy(g):
        cols = pl.ds(pl.multiple_of(g * group_cols, group_cols), group_cols)
        return pltpu.make_async_copy(top.at[:, cols], out_ref.at[pl.ds(0, TOP), cols], t_sem)

    def piece(ref):
        return ref.at[pl.ds(0, SPREAD_ROWS), pl.ds(SPREAD_STEP * step_cols, step_cols)]

    def rest_copy():
        lower = pl.ds(SPREAD_ROWS, rows - SPREAD_ROWS)
        cols = pl.ds(SPREAD_STEP * step_cols, step_cols)
        return to_top(obuf.at[lower, cols], out_ref.at[lower, cols], o_send, o_recv)

    def to_helper(helper, slot):
        return pltpu.make_async_remote_copy(
            src_ref=piece(obuf),
            dst_ref=spread.at[slot],
            send_sem=o_send,
            recv_sem=h_recv.at[slot],
            device_id=(pipe, helper),
            device_id_type=MESH,
        )

    def from_helper(helped, slot):
        return pltpu.make_async_remote_copy(
            src_ref=spread.at[slot],
            dst_ref=piece(out_ref),
            send_sem=h_send.at[slot],
            recv_sem=o_recv,
            device_id=(right, helped),
            device_id_type=MESH,
        )

    row = lax.broadcasted_iota(jnp.int32, (TOP, TOP), 0)
    lane = lax.broadcasted_iota(jnp.int32, (TOP, TOP), 1)

    def pack(step):
        first, second = weights[0], weights[1]
        packed[step] = jnp.where(row >= lane, first, second.T).astype(packed.dtype)
        diagonal = jnp.sum(jnp.where(row == lane, second, 0.0), axis=1, keepdims=True)
        at = 3 * lax.rem(step, group_steps)
        known = jnp.where(lane == at, sums[0], tile[...])
        known = jnp.where(lane == at + 1, sums[1], known)
        tile[...] = jnp.where(lane == at + 2, diagonal, known)

    def pack_moved(k):
        for at in range(STEP_HEADS):
            cols = pl.ds(pl.multiple_of(k * step_cols + at * DH, DH), DH)
            scores = lax.dot_general(
                qtop[:, cols],
                lent[0, :TOP, :],
                (((1,), (1,)), ((), ())),
                preferred_element_type=jnp.float32,
            )
            scores = jnp.where(row >= lane, scores, -HIDDEN)
            row_top = jnp.max(scores, axis=1, keepdims=True)
            seen = jnp.exp2((scores - row_top) * factor)
            weights[at] = seen
            sums[at] = jnp.broadcast_to(jnp.sum(seen, axis=1, keepdims=True), (TOP, TOP))
        pack(moved * group_steps + k)

    def hand_packed(g):
        facts[g] = tile[...].T
        packed_copy(g).start()
        facts_copy(g).start()

    def unpack(g):
        known = facts_in[g].T
        for k in range(group_steps):
            pair = tiles_in[g * group_steps + k].astype(jnp.float32)
            diagonal = known[:, 3 * k + 2 : 3 * k + 3]
            first = jnp.where(row >= lane, pair, 0.0)
            second = jnp.where(row > lane, pair.T, jnp.where(row == lane, diagonal, 0.0))
            for at, part in ((0, first), (1, second)):
                product = jnp.dot(
                    part.astype(jnp.bfloat16), vtop[g], preferred_element_type=jnp.float32
                )
                start = pl.multiple_of(g * group_cols, group_cols) + (2 * k + at) * DH
                cols = pl.ds(pl.multiple_of(start, DH), DH)
                top[:, cols] = (product / known[:, 3 * k + at : 3 * k + at + 1]).astype(top.dtype)

    doc_copy = pltpu.make_async_copy(doc_hbm, doc_ref, doc_sem)
    doc_copy.start()

    def fetch_own():
        for g in range(HK):
            for copy in own_copies(g):
                copy.start()
        q_copy.start()

    def fill_bias():
        doc_copy.wait()
        bias[0] = jnp.zeros(bias.shape[1:], jnp.float32)
        own_doc = doc_ref[0, ctx]
        for d in range(window):
            block = jnp.maximum(ctx - d, 0)
            seen = (doc_ref[0, block] == own_doc) & (ctx >= d)
            bias[0, d : d + 1, :] = jnp.full((1, DH), jnp.where(seen, 0.0, HIDDEN), jnp.float32)

    @pl.when(jnp.logical_not(ends))
    def _():
        fetch_own()
        fill_bias()

    pl.semaphore_wait(barrier, met)
    pl.when(packs)(lambda: moved_low_q().start())
    pl.when(jnp.logical_not(packs))(lambda: moved_q().start())
    pl.when(packs)(qtop_copy.start)

    @pl.when(guides)
    def _():
        pl.semaphore_signal(go_sem, inc=1, device_id=(right, ctx), device_id_type=MESH)

    @pl.when(ends)
    def _():
        fetch_own()
        fill_bias()

    all_own().wait()
    moved_kv().start()
    moved_bias().start()
    pl.when(packs)(lambda: vtop_copy().start())
    pl.when(ends)(lambda: pl.semaphore_wait(go_sem, 1))

    def start_direct(g):
        if g == moved:
            to_right(lent_rows, lent_rows, 0).wait_recv()
        for d in range(2, window, 2):
            pl.when(ctx + d < n_ctx)(lambda d=d: kv_copy(g, 0, d, lax.rem(ctx + d, n_ctx), d // 2).start())

    def pass_on(g):
        pl.when(relays(0))(lambda: kv_copy(g, 0, 1, sibling, 0).start())
        for d in range(2, window, 2):
            pl.when(ctx >= d)(functools.partial(wait_block, g, d))
            pl.when(relays(d))(lambda d=d: kv_copy(g, d, d + turn, sibling, 0).start())

    def end_gather(g):
        for d in range(1, window, 2):
            fits = (ctx >= d) & (ctx < d + 2) if d + 2 < window else ctx >= d

            @pl.when(fits)
            def _(d=d):
                blocks = kvbuf.at[g, :, pl.ds(0, (d + 1) // 2 * rows)]
                pltpu.make_async_copy(blocks, blocks, kv_recv.at[g, 0]).wait()

    start_direct(0)

    @pl.when(packs)
    def _():
        qbuf[:TOP, moved_cols] = jnp.zeros((TOP, group_cols), qbuf.dtype)

    for d in range(1, window):

        @pl.when(ctx < d)
        def _():
            place = pl.ds((last - d) * rows, rows)
            for g in range(HK):
                for which in range(2):
                    kvbuf[g, which, place, :] = jnp.zeros((rows, DH), kvbuf.dtype)

    pass_on(0)
    start_direct(1)
    q_copy.wait()

    @pl.loop(0, steps)
    def _(step):
        g = step // group_steps

        @pl.when(lax.rem(step, group_steps) == 0)
        def _():
            pl.when((g == moved) & packs)(lambda: moved_low_q().wait_recv())
            pl.when((g == moved) & jnp.logical_not(packs))(lambda: moved_q().wait_recv())
            end_gather(g)

        @pl.when(step == 3)
        def _():
            pass_on(1)
            start_direct(2)

        @pl.when(step == 7)
        def _():
            pass_on(2)
            start_direct(3)

        @pl.when(step == 11)
        def _():
            pass_on(3)

        which = jnp.where(g == moved, 1, 0)
        causal = lax.broadcasted_iota(jnp.int32, (rows, rows), 0) >= lax.broadcasted_iota(
            jnp.int32, (rows, rows), 1
        )
        for at in range(STEP_HEADS):
            cols = pl.ds(pl.multiple_of(step * step_cols + at * DH, DH), DH)
            query = qbuf[:, cols]
            scores = []
            top = None
            for d in range(window):
                place = pl.ds((last - d) * rows, rows)
                part = lax.dot_general(
                    query,
                    kvbuf[g, 0, place, :],
                    (((1,), (1,)), ((), ())),
                    preferred_element_type=jnp.float32,
                )
                if d == 0:
                    part = jnp.where(causal, part, -HIDDEN)
                scores.append(part)
                lanes = part[:, :DH]
                for c in range(1, rows // DH):
                    lanes = jnp.maximum(lanes, part[:, c * DH : (c + 1) * DH])
                if d > 0:
                    lanes = lanes - bias[which, d : d + 1, :]
                top = lanes if top is None else jnp.maximum(top, lanes)
            row_top = jnp.broadcast_to(jnp.max(top, axis=1, keepdims=True), (rows, DH))
            total = None
            acc = None
            for d in range(window):
                place = pl.ds((last - d) * rows, rows)
                offset = row_top
                if d > 0:
                    offset = row_top + bias[which, d : d + 1, :]
                rounded = []
                for c in range(rows // DH):
                    lanes = jnp.exp2((scores[d][:, c * DH : (c + 1) * DH] - offset) * factor)
                    total = lanes if total is None else total + lanes
                    if d == 0 and c == 0:
                        weights[at] = lanes[:TOP]
                    rounded.append(lanes.astype(jnp.bfloat16))
                product = jnp.dot(
                    jnp.concatenate(rounded, axis=1),
                    kvbuf[g, 1, place, :],
                    preferred_element_type=jnp.float32,
                )
                acc = product if acc is None else acc + product
            row_total = jnp.sum(total, axis=1, keepdims=True)
            sums[at] = jnp.broadcast_to(row_total[:TOP], (TOP, TOP))
            obuf[:, cols] = (acc / row_total).astype(obuf.dtype)

        done = pl.ds(pl.multiple_of(step * step_cols, step_cols), step_cols)

        later = lax.rem(step, 2) == 1
        pair = pl.ds(pl.multiple_of((step - lax.rem(step, 2)) * step_cols, 2 * step_cols), 2 * step_cols)

        @pl.when((step < group_steps) & jnp.logical_not(packs | (spreads & (step == SPREAD_STEP))))
        def _():
            out_copy(done).start()

        @pl.when((step >= group_steps) & (g < moved) & later & jnp.logical_not(packs))
        def _():
            out_copy(pair).start()

        @pl.when((g < moved) & packs)
        def _():
            pack(step)
            pl.when(step < group_steps)(lambda: half_copy(done).start())
            pl.when((step >= group_steps) & later)(lambda: half_copy(pair).start())

            @pl.when(lax.rem(step, group_steps) == group_steps - 1)
            def _():
                hand_packed(g)

            @pl.when(step == group_steps - 1)
            def _():
                qtop_copy.wait()

                @pl.loop(0, group_steps)
                def _(k):
                    pack_moved(k)

                hand_packed(moved)

        @pl.when(spreads & (step == SPREAD_STEP))
        def _():
            for helped, helper, slot in HELPED:
                pl.when(ctx == helped)(lambda to=(helper, slot): to_helper(*to).start())
            rest_copy().start()

        for helped, helper, slot in HELPED:

            @pl.when((ctx == helper) & (step == SPREAD_LATER))
            def _(helped=helped, helper=helper, slot=slot):
                to_helper(helper, slot).wait_recv()
                from_helper(helped, slot).start()

        pl.when((g == moved) & packs)(lambda: half_local(done).start())
        pl.when((g == moved) & jnp.logical_not(packs))(lambda: out_local(done).start())

    to_right(lent_rows, lent_rows, 0).wait_send()

    for count in range(1, window + 1):

        @pl.when(sends == count)
        def _(count=count):
            blocks = kvbuf.at[:, :, pl.ds(0, count * rows)]
            pltpu.make_async_copy(blocks, blocks, kv_send).wait()

    for helped, helper, slot in HELPED:
        pl.when(ctx == helper)(lambda by=(helped, slot): from_helper(*by).wait_send())

    @pl.when(packs)
    def _():
        vtop[moved] = kvbuf[moved, 1, pl.ds(last * rows, TOP), :]
        lines = group_steps * TOP + 32

        @pl.loop(0, HK)
        def _(g):
            for first, count in ((True, lines + moved * TOP), (False, lines)):

                @pl.when((g == 0) == first)
                def _(count=count):
                    arrived = kvbuf.at[0, 0, pl.ds(0, count)]
                    pltpu.make_async_copy(arrived, arrived, y_recv.at[g]).wait()

            unpack(g)
            top_copy(g).start()

        pltpu.make_async_copy(top, out_ref.at[pl.ds(0, TOP)], t_sem).wait()

    @pl.when(packs)
    def _():
        vtop_copy().wait_send()
        to_top(packed, tiles_in, q_sem, y_recv.at[0]).wait_send()
        sent = facts.at[:, pl.ds(0, 16)]
        to_top(sent, sent, doc_sem, y_recv.at[0]).wait_send()

    whole = pl.ds(0, HQ * DH)
    lower = pl.ds(0, HQ * DH * (rows - TOP) // rows)
    pl.when(packs)(lambda: out_copy(lower).wait_send())
    pl.when(jnp.logical_not(packs))(lambda: out_copy(whole).wait_send())
    pl.when(packs)(lambda: out_copy(lower).wait_recv())
    pl.when(jnp.logical_not(packs))(lambda: out_copy(whole).wait_recv())


def shards(n_pipe, n_ctx, queries, keys, values, doc_ids):
    rows = queries.shape[1]
    window = n_ctx // 2 + 1
    bias_rows = (window + 7) // 8 * 8
    dma = pltpu.SemaphoreType.DMA
    anywhere = pl.BlockSpec(memory_space=pl.ANY)
    handed = pl.pallas_call(
        functools.partial(kernel, n_pipe, n_ctx, window, rows),
        out_shape=jax.ShapeDtypeStruct((rows, HQ * DH), jnp.bfloat16),
        in_specs=[pl.BlockSpec(memory_space=pltpu.HBM)] * 4,
        out_specs=anywhere,
        scratch_shapes=[
            pltpu.VMEM((rows, HQ * DH), jnp.bfloat16),
            pltpu.VMEM((HK, 2, window * rows, DH), jnp.bfloat16),
            pltpu.VMEM((rows, HQ * DH), jnp.bfloat16),
            pltpu.VMEM((2, bias_rows, DH), jnp.float32),
            pltpu.SMEM(doc_ids.shape, jnp.int32),
            pltpu.VMEM((2, SPREAD_ROWS, STEP_HEADS * DH), jnp.bfloat16),
            pltpu.VMEM((2, rows, DH), jnp.bfloat16),
            pltpu.VMEM((STEP_HEADS, TOP, TOP), jnp.float32),
            pltpu.VMEM((STEP_HEADS, TOP, TOP), jnp.float32),
            pltpu.VMEM((TOP, TOP), jnp.float32),
            pltpu.VMEM((HQ // STEP_HEADS, TOP, TOP), jnp.bfloat16),
            pltpu.VMEM((HK, TOP, TOP), jnp.float32),
            pltpu.VMEM((HQ // STEP_HEADS, TOP, TOP), jnp.bfloat16),
            pltpu.VMEM((HK, TOP, TOP), jnp.float32),
            pltpu.VMEM((HK, TOP, DH), jnp.bfloat16),
            pltpu.VMEM((TOP, PER_GROUP * DH), jnp.bfloat16),
            pltpu.VMEM((TOP, HQ * DH), jnp.bfloat16),
            dma,
            dma,
            dma,
            dma,
            dma((HK, 1 + (window - 1) // 2)),
            dma,
            dma((2,)),
            dma,
            dma,
            dma((2,)),
            dma((2,)),
            dma((HK,)),
            dma,
            pltpu.SemaphoreType.REGULAR,
        ],
        compiler_params=pltpu.CompilerParams(
            collective_id=0, has_side_effects=True, vmem_limit_bytes=48 * 1024 * 1024
        ),
        name="relay_attention",
    )(*(pltpu.with_memory_space_constraint(x, pltpu.HBM) for x in (doc_ids, queries[0], keys[0], values[0])))
    return handed[None]


def solution(mesh):
    placed = (
        P("pipe", "ctx", None),
        P("pipe", "ctx", None),
        P("pipe", "ctx", None),
        P("pipe", None),
    )
    return jax.shard_map(
        functools.partial(shards, mesh.shape["pipe"], mesh.shape["ctx"]),
        mesh=mesh,
        in_specs=placed,
        out_specs=P("pipe", "ctx", None),
        check_vma=False,
    )
```

```python
import functools
import math

import jax
import jax.numpy as jnp
from jax import lax
from jax.experimental import pallas as pl
from jax.experimental.pallas import tpu as pltpu
from jax.sharding import PartitionSpec as P

HQ = 32
HK = 4
DH = 128
PER_GROUP = HQ // HK
STEP_HEADS = 2
SPREAD_STEP = 2
SPREAD_LATER = 13
HELPED = ((2, 0, 0), (4, 1, 0), (6, 0, 1))
SPREAD_ROWS = 208
TOP = 128
HIDDEN = 1e30
MESH = pl.DeviceIdType.MESH


def kernel(
    n_pipe,
    n_ctx,
    window,
    rows,
    doc_hbm,
    q_ref,
    k_ref,
    v_ref,
    out_ref,
    qbuf,
    kvbuf,
    obuf,
    bias,
    doc_ref,
    spread,
    lent,
    weights,
    sums,
    tile,
    packed,
    facts,
    tiles_in,
    facts_in,
    vtop,
    qtop,
    top,
    doc_sem,
    q_sem,
    own_sem,
    kv_send,
    kv_recv,
    z_send,
    z_recv,
    o_send,
    o_recv,
    h_send,
    h_recv,
    y_recv,
    t_sem,
    go_sem,
):
    pipe = lax.axis_index("pipe")
    ctx = lax.axis_index("ctx")
    right = lax.rem(pipe + 1, n_pipe)
    left = lax.rem(pipe + n_pipe - 1, n_pipe)
    moved = HK - 1
    group_cols = PER_GROUP * DH
    step_cols = STEP_HEADS * DH
    steps = HQ // STEP_HEADS
    group_steps = PER_GROUP // STEP_HEADS
    last = window - 1
    factor = math.log2(math.e) / math.sqrt(DH)
    own_rows = pl.ds(last * rows, rows)
    low = pl.ds(TOP, rows - TOP)
    sent_cols = pl.ds(0, moved * group_cols)
    moved_cols = pl.ds(moved * group_cols, group_cols)

    core = lax.rem(ctx, 2)
    turn = 1 - 2 * core
    sibling = ctx + turn
    barrier = pltpu.get_barrier_semaphore()
    ends = pipe == n_pipe - 1
    guides = pipe == n_pipe - 2
    hall = jnp.where(ends, left, pipe)
    packs = ctx == 0
    spreads = functools.reduce(jnp.logical_or, [ctx == helped for helped, _, _ in HELPED])

    def greet(pipe_to, ctx_to):
        pl.semaphore_signal(barrier, inc=1, device_id=(pipe_to, ctx_to), device_id_type=MESH)

    greet(left, ctx)

    def own_copies(g):
        cols = pl.ds(g * DH, DH)
        place = lent if g == moved else kvbuf.at[g, :, own_rows]
        return (
            pltpu.make_async_copy(k_ref.at[:, cols], place.at[0], own_sem),
            pltpu.make_async_copy(v_ref.at[:, cols], place.at[1], own_sem),
        )

    def all_own():
        blocks = kvbuf.at[:, :, own_rows]
        return pltpu.make_async_copy(blocks, blocks, own_sem)

    q_copy = pltpu.make_async_copy(q_ref.at[:, sent_cols], qbuf.at[:, sent_cols], q_sem)

    def kv_copy(g, source, target, ctx_to, slot):
        from_rows = pl.ds(pl.multiple_of((last - source) * rows, rows), rows)
        to_rows = pl.ds(pl.multiple_of((last - target) * rows, rows), rows)
        return pltpu.make_async_remote_copy(
            src_ref=kvbuf.at[g, :, from_rows],
            dst_ref=kvbuf.at[g, :, to_rows],
            send_sem=kv_send,
            recv_sem=kv_recv.at[g, slot],
            device_id=(pipe, ctx_to),
            device_id_type=MESH,
        )

    def wait_block(g, d):
        kv_copy(g, 0, d, sibling, d // 2).wait_recv()

    def relays(d):
        fits = core == 0 if d == 0 else ctx >= d
        return fits & (core == 1) if d == last else fits

    sends = jnp.int32(0)
    for d in range(0, window, 2):
        sends = sends + jnp.where(relays(d), 1, 0)
        if d > 0:
            sends = sends + jnp.where(ctx + d < n_ctx, 1, 0)

    def to_right(source, target, at):
        return pltpu.make_async_remote_copy(
            src_ref=source,
            dst_ref=target,
            send_sem=o_send if at == 1 else z_send,
            recv_sem=z_recv.at[at],
            device_id=(right, ctx),
            device_id_type=MESH,
        )

    def moved_kv():
        return to_right(lent, kvbuf.at[moved, :, own_rows], 0)

    def moved_bias():
        return to_right(bias.at[0], bias.at[1], 0)

    lent_rows = kvbuf.at[0, 0, pl.ds(0, 2 * rows + 2 * bias.shape[1])]

    def moved_q():
        return to_right(q_ref.at[:, moved_cols], qbuf.at[:, moved_cols], 1)

    def moved_low_q():
        return to_right(q_ref.at[low, moved_cols], qbuf.at[low, moved_cols], 1)

    def out_copy(cols):
        return pltpu.make_async_remote_copy(
            src_ref=obuf.at[:, cols],
            dst_ref=out_ref.at[:, cols],
            send_sem=o_send,
            recv_sem=o_recv,
            device_id=(right, ctx),
            device_id_type=MESH,
        )

    def out_local(cols):
        return pltpu.make_async_copy(obuf.at[:, cols], out_ref.at[:, cols], o_recv)

    def half_local(cols):
        return pltpu.make_async_copy(obuf.at[low, cols], out_ref.at[low, cols], o_recv)

    qtop_copy = pltpu.make_async_copy(q_ref.at[pl.ds(0, TOP), moved_cols], qtop, t_sem)

    def half_copy(cols):
        return pltpu.make_async_remote_copy(
            src_ref=obuf.at[low, cols],
            dst_ref=out_ref.at[low, cols],
            send_sem=o_send,
            recv_sem=o_recv,
            device_id=(right, ctx),
            device_id_type=MESH,
        )

    def to_top(source, target, send_sem, recv_sem):
        return pltpu.make_async_remote_copy(
            src_ref=source,
            dst_ref=target,
            send_sem=send_sem,
            recv_sem=recv_sem,
            device_id=(right, ctx),
            device_id_type=MESH,
        )

    def packed_copy(g):
        tiles = pl.ds(g * group_steps, group_steps)
        return to_top(packed.at[tiles], tiles_in.at[tiles], q_sem, y_recv.at[g])

    def facts_copy(g):
        lines = pl.ds(0, 16)
        return to_top(facts.at[g, lines], facts_in.at[g, lines], doc_sem, y_recv.at[g])

    def vtop_copy():
        sent = pl.ds(0, moved)
        return to_top(
            kvbuf.at[sent, 1, pl.ds(last * rows, TOP)], vtop.at[sent], own_sem, y_recv.at[0]
        )

    def top_copy(g):
        cols = pl.ds(pl.multiple_of(g * group_cols, group_cols), group_cols)
        return pltpu.make_async_copy(top.at[:, cols], out_ref.at[pl.ds(0, TOP), cols], t_sem)

    def piece(ref):
        return ref.at[pl.ds(0, SPREAD_ROWS), pl.ds(SPREAD_STEP * step_cols, step_cols)]

    def rest_copy():
        lower = pl.ds(SPREAD_ROWS, rows - SPREAD_ROWS)
        cols = pl.ds(SPREAD_STEP * step_cols, step_cols)
        return to_top(obuf.at[lower, cols], out_ref.at[lower, cols], o_send, o_recv)

    def to_helper(helper, slot):
        return pltpu.make_async_remote_copy(
            src_ref=piece(obuf),
            dst_ref=spread.at[slot],
            send_sem=o_send,
            recv_sem=h_recv.at[slot],
            device_id=(pipe, helper),
            device_id_type=MESH,
        )

    def from_helper(helped, slot):
        return pltpu.make_async_remote_copy(
            src_ref=spread.at[slot],
            dst_ref=piece(out_ref),
            send_sem=h_send.at[slot],
            recv_sem=o_recv,
            device_id=(right, helped),
            device_id_type=MESH,
        )

    row = lax.broadcasted_iota(jnp.int32, (TOP, TOP), 0)
    lane = lax.broadcasted_iota(jnp.int32, (TOP, TOP), 1)

    def pack(step):
        first, second = weights[0], weights[1]
        packed[step] = jnp.where(row >= lane, first, second.T).astype(packed.dtype)
        diagonal = jnp.sum(jnp.where(row == lane, second, 0.0), axis=1, keepdims=True)
        at = 3 * lax.rem(step, group_steps)
        known = jnp.where(lane == at, sums[0], tile[...])
        known = jnp.where(lane == at + 1, sums[1], known)
        tile[...] = jnp.where(lane == at + 2, diagonal, known)

    def pack_moved(k):
        for at in range(STEP_HEADS):
            cols = pl.ds(pl.multiple_of(k * step_cols + at * DH, DH), DH)
            scores = lax.dot_general(
                qtop[:, cols],
                lent[0, :TOP, :],
                (((1,), (1,)), ((), ())),
                preferred_element_type=jnp.float32,
            )
            scores = jnp.where(row >= lane, scores, -HIDDEN)
            row_top = jnp.max(scores, axis=1, keepdims=True)
            seen = jnp.exp2((scores - row_top) * factor)
            weights[at] = seen
            sums[at] = jnp.broadcast_to(jnp.sum(seen, axis=1, keepdims=True), (TOP, TOP))
        pack(moved * group_steps + k)

    def hand_packed(g):
        facts[g] = tile[...].T
        packed_copy(g).start()
        facts_copy(g).start()

    def unpack(g):
        known = facts_in[g].T
        for k in range(group_steps):
            pair = tiles_in[g * group_steps + k].astype(jnp.float32)
            diagonal = known[:, 3 * k + 2 : 3 * k + 3]
            first = jnp.where(row >= lane, pair, 0.0)
            second = jnp.where(row > lane, pair.T, jnp.where(row == lane, diagonal, 0.0))
            for at, part in ((0, first), (1, second)):
                product = jnp.dot(
                    part.astype(jnp.bfloat16), vtop[g], preferred_element_type=jnp.float32
                )
                start = pl.multiple_of(g * group_cols, group_cols) + (2 * k + at) * DH
                cols = pl.ds(pl.multiple_of(start, DH), DH)
                top[:, cols] = (product / known[:, 3 * k + at : 3 * k + at + 1]).astype(top.dtype)

    def send_q():
        pl.when(packs)(lambda: moved_low_q().start())
        pl.when(jnp.logical_not(packs))(lambda: moved_q().start())

    @pl.when(ends)
    def _():
        pl.semaphore_wait(barrier, 1)
        send_q()

    pl.when((core == 1) | (ctx >= 2))(lambda: greet(hall, sibling))
    met = jnp.where((core == 0) | (ctx >= 2), 1, 0)
    for d in range(2, window, 2):
        pl.when(ctx >= d)(lambda d=d: greet(hall, lax.rem(ctx + n_ctx - d, n_ctx)))
        met = met + jnp.where(ctx + d < n_ctx, 1, 0)
    for helped, helper, _ in HELPED:
        pl.when(ctx == helper)(lambda helped=helped: greet(hall, helped))
        met = met + jnp.where(ctx == helped, 1, 0)
    met = 1 + jnp.where(guides, 2 * met, met)
    doc_copy = pltpu.make_async_copy(doc_hbm, doc_ref, doc_sem)
    doc_copy.start()

    def fetch_own():
        for g in range(HK):
            for copy in own_copies(g):
                copy.start()
        q_copy.start()

    def fill_bias():
        doc_copy.wait()
        bias[0] = jnp.zeros(bias.shape[1:], jnp.float32)
        own_doc = doc_ref[0, ctx]
        for d in range(window):
            block = jnp.maximum(ctx - d, 0)
            seen = (doc_ref[0, block] == own_doc) & (ctx >= d)
            bias[0, d : d + 1, :] = jnp.full((1, DH), jnp.where(seen, 0.0, HIDDEN), jnp.float32)

    @pl.when(jnp.logical_not(ends))
    def _():
        fetch_own()
        fill_bias()

    @pl.when(jnp.logical_not(ends))
    def _():
        pl.semaphore_wait(barrier, met)
        send_q()

    pl.when(packs)(qtop_copy.start)

    @pl.when(guides)
    def _():
        pl.semaphore_signal(go_sem, inc=1, device_id=(right, ctx), device_id_type=MESH)

    @pl.when(ends)
    def _():
        fetch_own()
        fill_bias()

    all_own().wait()
    moved_kv().start()
    moved_bias().start()
    pl.when(packs)(lambda: vtop_copy().start())
    pl.when(ends)(lambda: pl.semaphore_wait(go_sem, 1))

    def start_direct(g):
        if g == moved:
            to_right(lent_rows, lent_rows, 0).wait_recv()
        for d in range(2, window, 2):
            pl.when(ctx + d < n_ctx)(lambda d=d: kv_copy(g, 0, d, lax.rem(ctx + d, n_ctx), d // 2).start())

    def pass_on(g):
        pl.when(relays(0))(lambda: kv_copy(g, 0, 1, sibling, 0).start())
        for d in range(2, window, 2):
            pl.when(ctx >= d)(functools.partial(wait_block, g, d))
            pl.when(relays(d))(lambda d=d: kv_copy(g, d, d + turn, sibling, 0).start())

    def end_gather(g):
        for d in range(1, window, 2):
            fits = (ctx >= d) & (ctx < d + 2) if d + 2 < window else ctx >= d

            @pl.when(fits)
            def _(d=d):
                blocks = kvbuf.at[g, :, pl.ds(0, (d + 1) // 2 * rows)]
                pltpu.make_async_copy(blocks, blocks, kv_recv.at[g, 0]).wait()

    start_direct(0)

    @pl.when(packs)
    def _():
        qbuf[:TOP, moved_cols] = jnp.zeros((TOP, group_cols), qbuf.dtype)

    for d in range(1, window):

        @pl.when(ctx < d)
        def _():
            place = pl.ds((last - d) * rows, rows)
            for g in range(HK):
                for which in range(2):
                    kvbuf[g, which, place, :] = jnp.zeros((rows, DH), kvbuf.dtype)

    pass_on(0)
    start_direct(1)
    q_copy.wait()

    @pl.loop(0, steps)
    def _(step):
        g = step // group_steps

        @pl.when(lax.rem(step, group_steps) == 0)
        def _():
            pl.when((g == moved) & packs)(lambda: moved_low_q().wait_recv())
            pl.when((g == moved) & jnp.logical_not(packs))(lambda: moved_q().wait_recv())
            end_gather(g)

        @pl.when(step == 3)
        def _():
            pass_on(1)
            start_direct(2)

        @pl.when(step == 7)
        def _():
            pass_on(2)
            start_direct(3)

        @pl.when(step == 11)
        def _():
            pass_on(3)

        which = jnp.where(g == moved, 1, 0)
        causal = lax.broadcasted_iota(jnp.int32, (rows, rows), 0) >= lax.broadcasted_iota(
            jnp.int32, (rows, rows), 1
        )
        for at in range(STEP_HEADS):
            cols = pl.ds(pl.multiple_of(step * step_cols + at * DH, DH), DH)
            query = qbuf[:, cols]
            scores = []
            top = None
            for d in range(window):
                place = pl.ds((last - d) * rows, rows)
                part = lax.dot_general(
                    query,
                    kvbuf[g, 0, place, :],
                    (((1,), (1,)), ((), ())),
                    preferred_element_type=jnp.float32,
                )
                if d == 0:
                    part = jnp.where(causal, part, -HIDDEN)
                scores.append(part)
                lanes = part[:, :DH]
                for c in range(1, rows // DH):
                    lanes = jnp.maximum(lanes, part[:, c * DH : (c + 1) * DH])
                if d > 0:
                    lanes = lanes - bias[which, d : d + 1, :]
                top = lanes if top is None else jnp.maximum(top, lanes)
            row_top = jnp.broadcast_to(jnp.max(top, axis=1, keepdims=True), (rows, DH))
            total = None
            acc = None
            for d in range(window):
                place = pl.ds((last - d) * rows, rows)
                offset = row_top
                if d > 0:
                    offset = row_top + bias[which, d : d + 1, :]
                rounded = []
                for c in range(rows // DH):
                    lanes = jnp.exp2((scores[d][:, c * DH : (c + 1) * DH] - offset) * factor)
                    total = lanes if total is None else total + lanes
                    if d == 0 and c == 0:
                        weights[at] = lanes[:TOP]
                    rounded.append(lanes.astype(jnp.bfloat16))
                product = jnp.dot(
                    jnp.concatenate(rounded, axis=1),
                    kvbuf[g, 1, place, :],
                    preferred_element_type=jnp.float32,
                )
                acc = product if acc is None else acc + product
            row_total = jnp.sum(total, axis=1, keepdims=True)
            sums[at] = jnp.broadcast_to(row_total[:TOP], (TOP, TOP))
            obuf[:, cols] = (acc / row_total).astype(obuf.dtype)

        done = pl.ds(pl.multiple_of(step * step_cols, step_cols), step_cols)

        later = lax.rem(step, 2) == 1
        pair = pl.ds(pl.multiple_of((step - lax.rem(step, 2)) * step_cols, 2 * step_cols), 2 * step_cols)

        @pl.when((step < group_steps) & jnp.logical_not(packs | (spreads & (step == SPREAD_STEP))))
        def _():
            out_copy(done).start()

        @pl.when((step >= group_steps) & (g < moved) & later & jnp.logical_not(packs))
        def _():
            out_copy(pair).start()

        @pl.when((g < moved) & packs)
        def _():
            pack(step)
            pl.when(step < group_steps)(lambda: half_copy(done).start())
            pl.when((step >= group_steps) & later)(lambda: half_copy(pair).start())

            @pl.when(lax.rem(step, group_steps) == group_steps - 1)
            def _():
                hand_packed(g)

            @pl.when(step == group_steps - 1)
            def _():
                qtop_copy.wait()

                @pl.loop(0, group_steps)
                def _(k):
                    pack_moved(k)

                hand_packed(moved)

        @pl.when(spreads & (step == SPREAD_STEP))
        def _():
            for helped, helper, slot in HELPED:
                pl.when(ctx == helped)(lambda to=(helper, slot): to_helper(*to).start())
            rest_copy().start()

        for helped, helper, slot in HELPED:

            @pl.when((ctx == helper) & (step == SPREAD_LATER))
            def _(helped=helped, helper=helper, slot=slot):
                to_helper(helper, slot).wait_recv()
                from_helper(helped, slot).start()

        pl.when((g == moved) & packs)(lambda: half_local(done).start())
        pl.when((g == moved) & jnp.logical_not(packs))(lambda: out_local(done).start())

    to_right(lent_rows, lent_rows, 0).wait_send()

    for count in range(1, window + 1):

        @pl.when(sends == count)
        def _(count=count):
            blocks = kvbuf.at[:, :, pl.ds(0, count * rows)]
            pltpu.make_async_copy(blocks, blocks, kv_send).wait()

    for helped, helper, slot in HELPED:
        pl.when(ctx == helper)(lambda by=(helped, slot): from_helper(*by).wait_send())

    @pl.when(packs)
    def _():
        vtop[moved] = kvbuf[moved, 1, pl.ds(last * rows, TOP), :]
        lines = group_steps * TOP + 32

        @pl.loop(0, HK)
        def _(g):
            for first, count in ((True, lines + moved * TOP), (False, lines)):

                @pl.when((g == 0) == first)
                def _(count=count):
                    arrived = kvbuf.at[0, 0, pl.ds(0, count)]
                    pltpu.make_async_copy(arrived, arrived, y_recv.at[g]).wait()

            unpack(g)
            top_copy(g).start()

        pltpu.make_async_copy(top, out_ref.at[pl.ds(0, TOP)], t_sem).wait()

    @pl.when(packs)
    def _():
        vtop_copy().wait_send()
        to_top(packed, tiles_in, q_sem, y_recv.at[0]).wait_send()
        sent = facts.at[:, pl.ds(0, 16)]
        to_top(sent, sent, doc_sem, y_recv.at[0]).wait_send()

    whole = pl.ds(0, HQ * DH)
    lower = pl.ds(0, HQ * DH * (rows - TOP) // rows)
    pl.when(packs)(lambda: out_copy(lower).wait_send())
    pl.when(jnp.logical_not(packs))(lambda: out_copy(whole).wait_send())
    pl.when(packs)(lambda: out_copy(lower).wait_recv())
    pl.when(jnp.logical_not(packs))(lambda: out_copy(whole).wait_recv())


def shards(n_pipe, n_ctx, queries, keys, values, doc_ids):
    rows = queries.shape[1]
    window = n_ctx // 2 + 1
    bias_rows = (window + 7) // 8 * 8
    dma = pltpu.SemaphoreType.DMA
    anywhere = pl.BlockSpec(memory_space=pl.ANY)
    handed = pl.pallas_call(
        functools.partial(kernel, n_pipe, n_ctx, window, rows),
        out_shape=jax.ShapeDtypeStruct((rows, HQ * DH), jnp.bfloat16),
        in_specs=[pl.BlockSpec(memory_space=pltpu.HBM)] * 4,
        out_specs=anywhere,
        scratch_shapes=[
            pltpu.VMEM((rows, HQ * DH), jnp.bfloat16),
            pltpu.VMEM((HK, 2, window * rows, DH), jnp.bfloat16),
            pltpu.VMEM((rows, HQ * DH), jnp.bfloat16),
            pltpu.VMEM((2, bias_rows, DH), jnp.float32),
            pltpu.SMEM(doc_ids.shape, jnp.int32),
            pltpu.VMEM((2, SPREAD_ROWS, STEP_HEADS * DH), jnp.bfloat16),
            pltpu.VMEM((2, rows, DH), jnp.bfloat16),
            pltpu.VMEM((STEP_HEADS, TOP, TOP), jnp.float32),
            pltpu.VMEM((STEP_HEADS, TOP, TOP), jnp.float32),
            pltpu.VMEM((TOP, TOP), jnp.float32),
            pltpu.VMEM((HQ // STEP_HEADS, TOP, TOP), jnp.bfloat16),
            pltpu.VMEM((HK, TOP, TOP), jnp.float32),
            pltpu.VMEM((HQ // STEP_HEADS, TOP, TOP), jnp.bfloat16),
            pltpu.VMEM((HK, TOP, TOP), jnp.float32),
            pltpu.VMEM((HK, TOP, DH), jnp.bfloat16),
            pltpu.VMEM((TOP, PER_GROUP * DH), jnp.bfloat16),
            pltpu.VMEM((TOP, HQ * DH), jnp.bfloat16),
            dma,
            dma,
            dma,
            dma,
            dma((HK, 1 + (window - 1) // 2)),
            dma,
            dma((2,)),
            dma,
            dma,
            dma((2,)),
            dma((2,)),
            dma((HK,)),
            dma,
            pltpu.SemaphoreType.REGULAR,
        ],
        compiler_params=pltpu.CompilerParams(
            collective_id=0, has_side_effects=True, vmem_limit_bytes=48 * 1024 * 1024
        ),
        name="relay_attention",
    )(*(pltpu.with_memory_space_constraint(x, pltpu.HBM) for x in (doc_ids, queries[0], keys[0], values[0])))
    return handed[None]


def solution(mesh):
    placed = (
        P("pipe", "ctx", None),
        P("pipe", "ctx", None),
        P("pipe", "ctx", None),
        P("pipe", None),
    )
    return jax.shard_map(
        functools.partial(shards, mesh.shape["pipe"], mesh.shape["ctx"]),
        mesh=mesh,
        in_specs=placed,
        out_specs=P("pipe", "ctx", None),
        check_vma=False,
    )
```

```python
import functools
import math

import jax
import jax.numpy as jnp
from jax import lax
from jax.experimental import pallas as pl
from jax.experimental.pallas import tpu as pltpu
from jax.sharding import PartitionSpec as P

HQ = 32
HK = 4
DH = 128
PER_GROUP = HQ // HK
STEP_HEADS = 2
SPREAD_STEP = 2
SPREAD_LATER = 13
HELPED = ((2, 0, 0), (4, 0, 1), (6, 1, 0))
SPREAD_ROWS = 208
TOP = 128
HIDDEN = 1e30
MESH = pl.DeviceIdType.MESH


def kernel(
    n_pipe,
    n_ctx,
    window,
    rows,
    doc_hbm,
    q_ref,
    k_ref,
    v_ref,
    out_ref,
    qbuf,
    kvbuf,
    obuf,
    bias,
    doc_ref,
    spread,
    lent,
    weights,
    sums,
    tile,
    packed,
    facts,
    tiles_in,
    facts_in,
    vtop,
    qtop,
    top,
    doc_sem,
    q_sem,
    own_sem,
    kv_send,
    kv_recv,
    z_send,
    z_recv,
    o_send,
    o_recv,
    h_send,
    h_recv,
    y_recv,
    t_sem,
    go_sem,
):
    pipe = lax.axis_index("pipe")
    ctx = lax.axis_index("ctx")
    right = lax.rem(pipe + 1, n_pipe)
    left = lax.rem(pipe + n_pipe - 1, n_pipe)
    moved = HK - 1
    group_cols = PER_GROUP * DH
    step_cols = STEP_HEADS * DH
    steps = HQ // STEP_HEADS
    group_steps = PER_GROUP // STEP_HEADS
    last = window - 1
    factor = math.log2(math.e) / math.sqrt(DH)
    own_rows = pl.ds(last * rows, rows)
    low = pl.ds(TOP, rows - TOP)
    sent_cols = pl.ds(0, moved * group_cols)
    moved_cols = pl.ds(moved * group_cols, group_cols)

    core = lax.rem(ctx, 2)
    turn = 1 - 2 * core
    sibling = ctx + turn
    barrier = pltpu.get_barrier_semaphore()
    ends = pipe == n_pipe - 1
    guides = pipe == n_pipe - 2
    hall = jnp.where(ends, left, pipe)
    packs = ctx == 0
    spreads = functools.reduce(jnp.logical_or, [ctx == helped for helped, _, _ in HELPED])

    def greet(pipe_to, ctx_to):
        pl.semaphore_signal(barrier, inc=1, device_id=(pipe_to, ctx_to), device_id_type=MESH)

    greet(left, ctx)

    def own_copies(g):
        cols = pl.ds(g * DH, DH)
        place = lent if g == moved else kvbuf.at[g, :, own_rows]
        return (
            pltpu.make_async_copy(k_ref.at[:, cols], place.at[0], own_sem),
            pltpu.make_async_copy(v_ref.at[:, cols], place.at[1], own_sem),
        )

    def all_own():
        blocks = kvbuf.at[:, :, own_rows]
        return pltpu.make_async_copy(blocks, blocks, own_sem)

    q_copy = pltpu.make_async_copy(q_ref.at[:, sent_cols], qbuf.at[:, sent_cols], q_sem)

    def kv_copy(g, source, target, ctx_to, slot):
        from_rows = pl.ds(pl.multiple_of((last - source) * rows, rows), rows)
        to_rows = pl.ds(pl.multiple_of((last - target) * rows, rows), rows)
        return pltpu.make_async_remote_copy(
            src_ref=kvbuf.at[g, :, from_rows],
            dst_ref=kvbuf.at[g, :, to_rows],
            send_sem=kv_send,
            recv_sem=kv_recv.at[g, slot],
            device_id=(pipe, ctx_to),
            device_id_type=MESH,
        )

    def wait_block(g, d):
        kv_copy(g, 0, d, sibling, d // 2).wait_recv()

    def relays(d):
        fits = core == 0 if d == 0 else ctx >= d
        return fits & (core == 1) if d == last else fits

    sends = jnp.int32(0)
    for d in range(0, window, 2):
        sends = sends + jnp.where(relays(d), 1, 0)
        if d > 0:
            sends = sends + jnp.where(ctx + d < n_ctx, 1, 0)

    def to_right(source, target, at):
        return pltpu.make_async_remote_copy(
            src_ref=source,
            dst_ref=target,
            send_sem=o_send if at == 1 else z_send,
            recv_sem=z_recv.at[at],
            device_id=(right, ctx),
            device_id_type=MESH,
        )

    def moved_kv():
        return to_right(lent, kvbuf.at[moved, :, own_rows], 0)

    def moved_bias():
        return to_right(bias.at[0], bias.at[1], 0)

    lent_rows = kvbuf.at[0, 0, pl.ds(0, 2 * rows + 2 * bias.shape[1])]

    def moved_q():
        return to_right(q_ref.at[:, moved_cols], qbuf.at[:, moved_cols], 1)

    def moved_low_q():
        return to_right(q_ref.at[low, moved_cols], qbuf.at[low, moved_cols], 1)

    def out_copy(cols):
        return pltpu.make_async_remote_copy(
            src_ref=obuf.at[:, cols],
            dst_ref=out_ref.at[:, cols],
            send_sem=o_send,
            recv_sem=o_recv,
            device_id=(right, ctx),
            device_id_type=MESH,
        )

    def out_local(cols):
        return pltpu.make_async_copy(obuf.at[:, cols], out_ref.at[:, cols], o_recv)

    def half_local(cols):
        return pltpu.make_async_copy(obuf.at[low, cols], out_ref.at[low, cols], o_recv)

    qtop_copy = pltpu.make_async_copy(q_ref.at[pl.ds(0, TOP), moved_cols], qtop, t_sem)

    def half_copy(cols):
        return pltpu.make_async_remote_copy(
            src_ref=obuf.at[low, cols],
            dst_ref=out_ref.at[low, cols],
            send_sem=o_send,
            recv_sem=o_recv,
            device_id=(right, ctx),
            device_id_type=MESH,
        )

    def to_top(source, target, send_sem, recv_sem):
        return pltpu.make_async_remote_copy(
            src_ref=source,
            dst_ref=target,
            send_sem=send_sem,
            recv_sem=recv_sem,
            device_id=(right, ctx),
            device_id_type=MESH,
        )

    def packed_copy(g):
        tiles = pl.ds(g * group_steps, group_steps)
        return to_top(packed.at[tiles], tiles_in.at[tiles], q_sem, y_recv.at[g])

    def facts_copy(g):
        lines = pl.ds(0, 16)
        return to_top(facts.at[g, lines], facts_in.at[g, lines], doc_sem, y_recv.at[g])

    def vtop_copy():
        sent = pl.ds(0, moved)
        return to_top(
            kvbuf.at[sent, 1, pl.ds(last * rows, TOP)], vtop.at[sent], own_sem, y_recv.at[0]
        )

    def top_copy(g):
        cols = pl.ds(pl.multiple_of(g * group_cols, group_cols), group_cols)
        return pltpu.make_async_copy(top.at[:, cols], out_ref.at[pl.ds(0, TOP), cols], t_sem)

    def piece(ref):
        return ref.at[pl.ds(0, SPREAD_ROWS), pl.ds(SPREAD_STEP * step_cols, step_cols)]

    def rest_copy():
        lower = pl.ds(SPREAD_ROWS, rows - SPREAD_ROWS)
        cols = pl.ds(SPREAD_STEP * step_cols, step_cols)
        return to_top(obuf.at[lower, cols], out_ref.at[lower, cols], o_send, o_recv)

    def to_helper(helper, slot):
        return pltpu.make_async_remote_copy(
            src_ref=piece(obuf),
            dst_ref=spread.at[slot],
            send_sem=o_send,
            recv_sem=h_recv.at[slot],
            device_id=(pipe, helper),
            device_id_type=MESH,
        )

    def from_helper(helped, slot):
        return pltpu.make_async_remote_copy(
            src_ref=spread.at[slot],
            dst_ref=piece(out_ref),
            send_sem=h_send.at[slot],
            recv_sem=o_recv,
            device_id=(right, helped),
            device_id_type=MESH,
        )

    row = lax.broadcasted_iota(jnp.int32, (TOP, TOP), 0)
    lane = lax.broadcasted_iota(jnp.int32, (TOP, TOP), 1)

    def pack(step):
        first, second = weights[0], weights[1]
        packed[step] = jnp.where(row >= lane, first, second.T).astype(packed.dtype)
        diagonal = jnp.sum(jnp.where(row == lane, second, 0.0), axis=1, keepdims=True)
        at = 3 * lax.rem(step, group_steps)
        known = jnp.where(lane == at, sums[0], tile[...])
        known = jnp.where(lane == at + 1, sums[1], known)
        tile[...] = jnp.where(lane == at + 2, diagonal, known)

    def pack_moved(k):
        for at in range(STEP_HEADS):
            cols = pl.ds(pl.multiple_of(k * step_cols + at * DH, DH), DH)
            scores = lax.dot_general(
                qtop[:, cols],
                lent[0, :TOP, :],
                (((1,), (1,)), ((), ())),
                preferred_element_type=jnp.float32,
            )
            scores = jnp.where(row >= lane, scores, -HIDDEN)
            row_top = jnp.max(scores, axis=1, keepdims=True)
            seen = jnp.exp2((scores - row_top) * factor)
            weights[at] = seen
            sums[at] = jnp.broadcast_to(jnp.sum(seen, axis=1, keepdims=True), (TOP, TOP))
        pack(moved * group_steps + k)

    def hand_packed(g):
        facts[g] = tile[...].T
        packed_copy(g).start()
        facts_copy(g).start()

    def unpack(g):
        known = facts_in[g].T
        for k in range(group_steps):
            pair = tiles_in[g * group_steps + k].astype(jnp.float32)
            diagonal = known[:, 3 * k + 2 : 3 * k + 3]
            first = jnp.where(row >= lane, pair, 0.0)
            second = jnp.where(row > lane, pair.T, jnp.where(row == lane, diagonal, 0.0))
            for at, part in ((0, first), (1, second)):
                product = jnp.dot(
                    part.astype(jnp.bfloat16), vtop[g], preferred_element_type=jnp.float32
                )
                start = pl.multiple_of(g * group_cols, group_cols) + (2 * k + at) * DH
                cols = pl.ds(pl.multiple_of(start, DH), DH)
                top[:, cols] = (product / known[:, 3 * k + at : 3 * k + at + 1]).astype(top.dtype)

    def send_q():
        pl.when(packs)(lambda: moved_low_q().start())
        pl.when(jnp.logical_not(packs))(lambda: moved_q().start())

    @pl.when(ends)
    def _():
        pl.semaphore_wait(barrier, 1)
        send_q()

    pl.when((core == 1) | (ctx >= 2))(lambda: greet(hall, sibling))
    met = jnp.where((core == 0) | (ctx >= 2), 1, 0)
    for d in range(2, window, 2):
        pl.when(ctx >= d)(lambda d=d: greet(hall, lax.rem(ctx + n_ctx - d, n_ctx)))
        met = met + jnp.where(ctx + d < n_ctx, 1, 0)
    for helped, helper, _ in HELPED:
        pl.when(ctx == helper)(lambda helped=helped: greet(hall, helped))
        met = met + jnp.where(ctx == helped, 1, 0)
    met = 1 + jnp.where(guides, 2 * met, met)
    doc_copy = pltpu.make_async_copy(doc_hbm, doc_ref, doc_sem)
    doc_copy.start()

    def fetch_own():
        for g in range(HK):
            for copy in own_copies(g):
                copy.start()
        q_copy.start()

    def fill_bias():
        doc_copy.wait()
        bias[0] = jnp.zeros(bias.shape[1:], jnp.float32)
        own_doc = doc_ref[0, ctx]
        for d in range(window):
            block = jnp.maximum(ctx - d, 0)
            seen = (doc_ref[0, block] == own_doc) & (ctx >= d)
            bias[0, d : d + 1, :] = jnp.full((1, DH), jnp.where(seen, 0.0, HIDDEN), jnp.float32)

    @pl.when(jnp.logical_not(ends))
    def _():
        fetch_own()
        fill_bias()

    @pl.when(jnp.logical_not(ends))
    def _():
        pl.semaphore_wait(barrier, met)
        send_q()

    pl.when(packs)(qtop_copy.start)

    @pl.when(guides)
    def _():
        pl.semaphore_signal(go_sem, inc=1, device_id=(right, ctx), device_id_type=MESH)

    @pl.when(ends)
    def _():
        fetch_own()
        fill_bias()

    all_own().wait()
    moved_kv().start()
    moved_bias().start()
    pl.when(packs)(lambda: vtop_copy().start())
    pl.when(ends)(lambda: pl.semaphore_wait(go_sem, 1))

    def start_direct(g):
        if g == moved:
            to_right(lent_rows, lent_rows, 0).wait_recv()
        for d in range(2, window, 2):
            pl.when(ctx + d < n_ctx)(lambda d=d: kv_copy(g, 0, d, lax.rem(ctx + d, n_ctx), d // 2).start())

    def pass_on(g):
        pl.when(relays(0))(lambda: kv_copy(g, 0, 1, sibling, 0).start())
        for d in range(2, window, 2):
            pl.when(ctx >= d)(functools.partial(wait_block, g, d))
            pl.when(relays(d))(lambda d=d: kv_copy(g, d, d + turn, sibling, 0).start())

    def end_gather(g):
        for d in range(1, window, 2):
            fits = (ctx >= d) & (ctx < d + 2) if d + 2 < window else ctx >= d

            @pl.when(fits)
            def _(d=d):
                blocks = kvbuf.at[g, :, pl.ds(0, (d + 1) // 2 * rows)]
                pltpu.make_async_copy(blocks, blocks, kv_recv.at[g, 0]).wait()

    start_direct(0)

    @pl.when(packs)
    def _():
        qbuf[:TOP, moved_cols] = jnp.zeros((TOP, group_cols), qbuf.dtype)

    for d in range(1, window):

        @pl.when(ctx < d)
        def _():
            place = pl.ds((last - d) * rows, rows)
            for g in range(HK):
                for which in range(2):
                    kvbuf[g, which, place, :] = jnp.zeros((rows, DH), kvbuf.dtype)

    pass_on(0)
    start_direct(1)
    q_copy.wait()

    @pl.loop(0, steps)
    def _(step):
        g = step // group_steps

        @pl.when(lax.rem(step, group_steps) == 0)
        def _():
            pl.when((g == moved) & packs)(lambda: moved_low_q().wait_recv())
            pl.when((g == moved) & jnp.logical_not(packs))(lambda: moved_q().wait_recv())
            end_gather(g)

        @pl.when(step == 3)
        def _():
            pass_on(1)
            start_direct(2)

        @pl.when(step == 7)
        def _():
            pass_on(2)
            start_direct(3)

        @pl.when(step == 11)
        def _():
            pass_on(3)

        which = jnp.where(g == moved, 1, 0)
        causal = lax.broadcasted_iota(jnp.int32, (rows, rows), 0) >= lax.broadcasted_iota(
            jnp.int32, (rows, rows), 1
        )
        for at in range(STEP_HEADS):
            cols = pl.ds(pl.multiple_of(step * step_cols + at * DH, DH), DH)
            query = qbuf[:, cols]
            scores = []
            top = None
            for d in range(window):
                place = pl.ds((last - d) * rows, rows)
                part = lax.dot_general(
                    query,
                    kvbuf[g, 0, place, :],
                    (((1,), (1,)), ((), ())),
                    preferred_element_type=jnp.float32,
                )
                if d == 0:
                    part = jnp.where(causal, part, -HIDDEN)
                scores.append(part)
                lanes = part[:, :DH]
                for c in range(1, rows // DH):
                    lanes = jnp.maximum(lanes, part[:, c * DH : (c + 1) * DH])
                if d > 0:
                    lanes = lanes - bias[which, d : d + 1, :]
                top = lanes if top is None else jnp.maximum(top, lanes)
            row_top = jnp.broadcast_to(jnp.max(top, axis=1, keepdims=True), (rows, DH))
            total = None
            acc = None
            for d in range(window):
                place = pl.ds((last - d) * rows, rows)
                offset = row_top
                if d > 0:
                    offset = row_top + bias[which, d : d + 1, :]
                rounded = []
                for c in range(rows // DH):
                    lanes = jnp.exp2((scores[d][:, c * DH : (c + 1) * DH] - offset) * factor)
                    total = lanes if total is None else total + lanes
                    if d == 0 and c == 0:
                        weights[at] = lanes[:TOP]
                    rounded.append(lanes.astype(jnp.bfloat16))
                product = jnp.dot(
                    jnp.concatenate(rounded, axis=1),
                    kvbuf[g, 1, place, :],
                    preferred_element_type=jnp.float32,
                )
                acc = product if acc is None else acc + product
            row_total = jnp.sum(total, axis=1, keepdims=True)
            sums[at] = jnp.broadcast_to(row_total[:TOP], (TOP, TOP))
            obuf[:, cols] = (acc / row_total).astype(obuf.dtype)

        done = pl.ds(pl.multiple_of(step * step_cols, step_cols), step_cols)

        later = lax.rem(step, 2) == 1
        pair = pl.ds(pl.multiple_of((step - lax.rem(step, 2)) * step_cols, 2 * step_cols), 2 * step_cols)

        @pl.when((step < group_steps) & jnp.logical_not(packs | (spreads & (step == SPREAD_STEP))))
        def _():
            out_copy(done).start()

        @pl.when((step >= group_steps) & (g < moved) & later & jnp.logical_not(packs))
        def _():
            out_copy(pair).start()

        @pl.when((g < moved) & packs)
        def _():
            pack(step)
            pl.when(step < group_steps)(lambda: half_copy(done).start())
            pl.when((step >= group_steps) & later)(lambda: half_copy(pair).start())

            @pl.when(lax.rem(step, group_steps) == group_steps - 1)
            def _():
                hand_packed(g)

            @pl.when(step == group_steps - 1)
            def _():
                qtop_copy.wait()

                @pl.loop(0, group_steps)
                def _(k):
                    pack_moved(k)

                hand_packed(moved)

        @pl.when(spreads & (step == SPREAD_STEP))
        def _():
            for helped, helper, slot in HELPED:
                pl.when(ctx == helped)(lambda to=(helper, slot): to_helper(*to).start())
            rest_copy().start()

        for helped, helper, slot in HELPED:

            @pl.when((ctx == helper) & (step == SPREAD_LATER))
            def _(helped=helped, helper=helper, slot=slot):
                to_helper(helper, slot).wait_recv()
                from_helper(helped, slot).start()

        pl.when((g == moved) & packs)(lambda: half_local(done).start())
        pl.when((g == moved) & jnp.logical_not(packs))(lambda: out_local(done).start())

    to_right(lent_rows, lent_rows, 0).wait_send()

    for count in range(1, window + 1):

        @pl.when(sends == count)
        def _(count=count):
            blocks = kvbuf.at[:, :, pl.ds(0, count * rows)]
            pltpu.make_async_copy(blocks, blocks, kv_send).wait()

    for helped, helper, slot in HELPED:
        pl.when(ctx == helper)(lambda by=(helped, slot): from_helper(*by).wait_send())

    @pl.when(packs)
    def _():
        vtop[moved] = kvbuf[moved, 1, pl.ds(last * rows, TOP), :]
        lines = group_steps * TOP + 32

        @pl.loop(0, HK)
        def _(g):
            for first, count in ((True, lines + moved * TOP), (False, lines)):

                @pl.when((g == 0) == first)
                def _(count=count):
                    arrived = kvbuf.at[0, 0, pl.ds(0, count)]
                    pltpu.make_async_copy(arrived, arrived, y_recv.at[g]).wait()

            unpack(g)
            top_copy(g).start()

        pltpu.make_async_copy(top, out_ref.at[pl.ds(0, TOP)], t_sem).wait()

    @pl.when(packs)
    def _():
        vtop_copy().wait_send()
        to_top(packed, tiles_in, q_sem, y_recv.at[0]).wait_send()
        sent = facts.at[:, pl.ds(0, 16)]
        to_top(sent, sent, doc_sem, y_recv.at[0]).wait_send()

    whole = pl.ds(0, HQ * DH)
    lower = pl.ds(0, HQ * DH * (rows - TOP) // rows)
    pl.when(packs)(lambda: out_copy(lower).wait_send())
    pl.when(jnp.logical_not(packs))(lambda: out_copy(whole).wait_send())
    pl.when(packs)(lambda: out_copy(lower).wait_recv())
    pl.when(jnp.logical_not(packs))(lambda: out_copy(whole).wait_recv())


def shards(n_pipe, n_ctx, queries, keys, values, doc_ids):
    rows = queries.shape[1]
    window = n_ctx // 2 + 1
    bias_rows = (window + 7) // 8 * 8
    dma = pltpu.SemaphoreType.DMA
    anywhere = pl.BlockSpec(memory_space=pl.ANY)
    handed = pl.pallas_call(
        functools.partial(kernel, n_pipe, n_ctx, window, rows),
        out_shape=jax.ShapeDtypeStruct((rows, HQ * DH), jnp.bfloat16),
        in_specs=[pl.BlockSpec(memory_space=pltpu.HBM)] * 4,
        out_specs=anywhere,
        scratch_shapes=[
            pltpu.VMEM((rows, HQ * DH), jnp.bfloat16),
            pltpu.VMEM((HK, 2, window * rows, DH), jnp.bfloat16),
            pltpu.VMEM((rows, HQ * DH), jnp.bfloat16),
            pltpu.VMEM((2, bias_rows, DH), jnp.float32),
            pltpu.SMEM(doc_ids.shape, jnp.int32),
            pltpu.VMEM((2, SPREAD_ROWS, STEP_HEADS * DH), jnp.bfloat16),
            pltpu.VMEM((2, rows, DH), jnp.bfloat16),
            pltpu.VMEM((STEP_HEADS, TOP, TOP), jnp.float32),
            pltpu.VMEM((STEP_HEADS, TOP, TOP), jnp.float32),
            pltpu.VMEM((TOP, TOP), jnp.float32),
            pltpu.VMEM((HQ // STEP_HEADS, TOP, TOP), jnp.bfloat16),
            pltpu.VMEM((HK, TOP, TOP), jnp.float32),
            pltpu.VMEM((HQ // STEP_HEADS, TOP, TOP), jnp.bfloat16),
            pltpu.VMEM((HK, TOP, TOP), jnp.float32),
            pltpu.VMEM((HK, TOP, DH), jnp.bfloat16),
            pltpu.VMEM((TOP, PER_GROUP * DH), jnp.bfloat16),
            pltpu.VMEM((TOP, HQ * DH), jnp.bfloat16),
            dma,
            dma,
            dma,
            dma,
            dma((HK, 1 + (window - 1) // 2)),
            dma,
            dma((2,)),
            dma,
            dma,
            dma((2,)),
            dma((2,)),
            dma((HK,)),
            dma,
            pltpu.SemaphoreType.REGULAR,
        ],
        compiler_params=pltpu.CompilerParams(
            collective_id=0, has_side_effects=True, vmem_limit_bytes=48 * 1024 * 1024
        ),
        name="relay_attention",
    )(*(pltpu.with_memory_space_constraint(x, pltpu.HBM) for x in (doc_ids, queries[0], keys[0], values[0])))
    return handed[None]


def solution(mesh):
    placed = (
        P("pipe", "ctx", None),
        P("pipe", "ctx", None),
        P("pipe", "ctx", None),
        P("pipe", None),
    )
    return jax.shard_map(
        functools.partial(shards, mesh.shape["pipe"], mesh.shape["ctx"]),
        mesh=mesh,
        in_specs=placed,
        out_specs=P("pipe", "ctx", None),
        check_vma=False,
    )
```

```python
import functools
import math

import jax
import jax.numpy as jnp
from jax import lax
from jax.experimental import pallas as pl
from jax.experimental.pallas import tpu as pltpu
from jax.sharding import PartitionSpec as P

HQ = 32
HK = 4
DH = 128
PER_GROUP = HQ // HK
STEP_HEADS = 2
SPREAD_STEP = 2
SPREAD_LATER = 13
HELPED = ((2, 0, 0), (4, 0, 1), (6, 1, 0))
SPREAD_ROWS = 224
TOP = 128
HIDDEN = 1e30
MESH = pl.DeviceIdType.MESH


def kernel(
    n_pipe,
    n_ctx,
    window,
    rows,
    doc_hbm,
    q_ref,
    k_ref,
    v_ref,
    out_ref,
    qbuf,
    kvbuf,
    obuf,
    bias,
    doc_ref,
    spread,
    lent,
    weights,
    sums,
    tile,
    packed,
    facts,
    tiles_in,
    facts_in,
    vtop,
    qtop,
    top,
    doc_sem,
    q_sem,
    own_sem,
    kv_send,
    kv_recv,
    z_send,
    z_recv,
    o_send,
    o_recv,
    h_send,
    h_recv,
    y_recv,
    t_sem,
    go_sem,
):
    pipe = lax.axis_index("pipe")
    ctx = lax.axis_index("ctx")
    right = lax.rem(pipe + 1, n_pipe)
    left = lax.rem(pipe + n_pipe - 1, n_pipe)
    moved = HK - 1
    group_cols = PER_GROUP * DH
    step_cols = STEP_HEADS * DH
    steps = HQ // STEP_HEADS
    group_steps = PER_GROUP // STEP_HEADS
    last = window - 1
    factor = math.log2(math.e) / math.sqrt(DH)
    own_rows = pl.ds(last * rows, rows)
    low = pl.ds(TOP, rows - TOP)
    sent_cols = pl.ds(0, moved * group_cols)
    moved_cols = pl.ds(moved * group_cols, group_cols)

    core = lax.rem(ctx, 2)
    turn = 1 - 2 * core
    sibling = ctx + turn
    barrier = pltpu.get_barrier_semaphore()
    ends = pipe == n_pipe - 1
    guides = pipe == n_pipe - 2
    hall = jnp.where(ends, left, pipe)
    packs = ctx == 0
    spreads = functools.reduce(jnp.logical_or, [ctx == helped for helped, _, _ in HELPED])

    def greet(pipe_to, ctx_to):
        pl.semaphore_signal(barrier, inc=1, device_id=(pipe_to, ctx_to), device_id_type=MESH)

    greet(left, ctx)

    def own_copies(g):
        cols = pl.ds(g * DH, DH)
        place = lent if g == moved else kvbuf.at[g, :, own_rows]
        return (
            pltpu.make_async_copy(k_ref.at[:, cols], place.at[0], own_sem),
            pltpu.make_async_copy(v_ref.at[:, cols], place.at[1], own_sem),
        )

    def all_own():
        blocks = kvbuf.at[:, :, own_rows]
        return pltpu.make_async_copy(blocks, blocks, own_sem)

    q_copy = pltpu.make_async_copy(q_ref.at[:, sent_cols], qbuf.at[:, sent_cols], q_sem)

    def kv_copy(g, source, target, ctx_to, slot):
        from_rows = pl.ds(pl.multiple_of((last - source) * rows, rows), rows)
        to_rows = pl.ds(pl.multiple_of((last - target) * rows, rows), rows)
        return pltpu.make_async_remote_copy(
            src_ref=kvbuf.at[g, :, from_rows],
            dst_ref=kvbuf.at[g, :, to_rows],
            send_sem=kv_send,
            recv_sem=kv_recv.at[g, slot],
            device_id=(pipe, ctx_to),
            device_id_type=MESH,
        )

    def wait_block(g, d):
        kv_copy(g, 0, d, sibling, d // 2).wait_recv()

    def relays(d):
        fits = core == 0 if d == 0 else ctx >= d
        return fits & (core == 1) if d == last else fits

    sends = jnp.int32(0)
    for d in range(0, window, 2):
        sends = sends + jnp.where(relays(d), 1, 0)
        if d > 0:
            sends = sends + jnp.where(ctx + d < n_ctx, 1, 0)

    def to_right(source, target, at):
        return pltpu.make_async_remote_copy(
            src_ref=source,
            dst_ref=target,
            send_sem=o_send if at == 1 else z_send,
            recv_sem=z_recv.at[at],
            device_id=(right, ctx),
            device_id_type=MESH,
        )

    def moved_kv():
        return to_right(lent, kvbuf.at[moved, :, own_rows], 0)

    def moved_bias():
        return to_right(bias.at[0], bias.at[1], 0)

    lent_rows = kvbuf.at[0, 0, pl.ds(0, 2 * rows + 2 * bias.shape[1])]

    def moved_q():
        return to_right(q_ref.at[:, moved_cols], qbuf.at[:, moved_cols], 1)

    def moved_low_q():
        return to_right(q_ref.at[low, moved_cols], qbuf.at[low, moved_cols], 1)

    def out_copy(cols):
        return pltpu.make_async_remote_copy(
            src_ref=obuf.at[:, cols],
            dst_ref=out_ref.at[:, cols],
            send_sem=o_send,
            recv_sem=o_recv,
            device_id=(right, ctx),
            device_id_type=MESH,
        )

    def out_local(cols):
        return pltpu.make_async_copy(obuf.at[:, cols], out_ref.at[:, cols], o_recv)

    def half_local(cols):
        return pltpu.make_async_copy(obuf.at[low, cols], out_ref.at[low, cols], o_recv)

    qtop_copy = pltpu.make_async_copy(q_ref.at[pl.ds(0, TOP), moved_cols], qtop, t_sem)

    def half_copy(cols):
        return pltpu.make_async_remote_copy(
            src_ref=obuf.at[low, cols],
            dst_ref=out_ref.at[low, cols],
            send_sem=o_send,
            recv_sem=o_recv,
            device_id=(right, ctx),
            device_id_type=MESH,
        )

    def to_top(source, target, send_sem, recv_sem):
        return pltpu.make_async_remote_copy(
            src_ref=source,
            dst_ref=target,
            send_sem=send_sem,
            recv_sem=recv_sem,
            device_id=(right, ctx),
            device_id_type=MESH,
        )

    def packed_copy(g):
        tiles = pl.ds(g * group_steps, group_steps)
        return to_top(packed.at[tiles], tiles_in.at[tiles], q_sem, y_recv.at[g])

    def facts_copy(g):
        lines = pl.ds(0, 16)
        return to_top(facts.at[g, lines], facts_in.at[g, lines], doc_sem, y_recv.at[g])

    def vtop_copy():
        sent = pl.ds(0, moved)
        return to_top(
            kvbuf.at[sent, 1, pl.ds(last * rows, TOP)], vtop.at[sent], own_sem, y_recv.at[0]
        )

    def top_copy(g):
        cols = pl.ds(pl.multiple_of(g * group_cols, group_cols), group_cols)
        return pltpu.make_async_copy(top.at[:, cols], out_ref.at[pl.ds(0, TOP), cols], t_sem)

    def piece(ref):
        return ref.at[pl.ds(0, SPREAD_ROWS), pl.ds(SPREAD_STEP * step_cols, step_cols)]

    def rest_copy():
        lower = pl.ds(SPREAD_ROWS, rows - SPREAD_ROWS)
        cols = pl.ds(SPREAD_STEP * step_cols, step_cols)
        return to_top(obuf.at[lower, cols], out_ref.at[lower, cols], o_send, o_recv)

    def to_helper(helper, slot):
        return pltpu.make_async_remote_copy(
            src_ref=piece(obuf),
            dst_ref=spread.at[slot],
            send_sem=o_send,
            recv_sem=h_recv.at[slot],
            device_id=(pipe, helper),
            device_id_type=MESH,
        )

    def from_helper(helped, slot):
        return pltpu.make_async_remote_copy(
            src_ref=spread.at[slot],
            dst_ref=piece(out_ref),
            send_sem=h_send.at[slot],
            recv_sem=o_recv,
            device_id=(right, helped),
            device_id_type=MESH,
        )

    row = lax.broadcasted_iota(jnp.int32, (TOP, TOP), 0)
    lane = lax.broadcasted_iota(jnp.int32, (TOP, TOP), 1)

    def pack(step):
        first, second = weights[0], weights[1]
        packed[step] = jnp.where(row >= lane, first, second.T).astype(packed.dtype)
        diagonal = jnp.sum(jnp.where(row == lane, second, 0.0), axis=1, keepdims=True)
        at = 3 * lax.rem(step, group_steps)
        known = jnp.where(lane == at, sums[0], tile[...])
        known = jnp.where(lane == at + 1, sums[1], known)
        tile[...] = jnp.where(lane == at + 2, diagonal, known)

    def pack_moved(k):
        for at in range(STEP_HEADS):
            cols = pl.ds(pl.multiple_of(k * step_cols + at * DH, DH), DH)
            scores = lax.dot_general(
                qtop[:, cols],
                lent[0, :TOP, :],
                (((1,), (1,)), ((), ())),
                preferred_element_type=jnp.float32,
            )
            scores = jnp.where(row >= lane, scores, -HIDDEN)
            row_top = jnp.max(scores, axis=1, keepdims=True)
            seen = jnp.exp2((scores - row_top) * factor)
            weights[at] = seen
            sums[at] = jnp.broadcast_to(jnp.sum(seen, axis=1, keepdims=True), (TOP, TOP))
        pack(moved * group_steps + k)

    def hand_packed(g):
        facts[g] = tile[...].T
        packed_copy(g).start()
        facts_copy(g).start()

    def unpack(g):
        known = facts_in[g].T
        for k in range(group_steps):
            pair = tiles_in[g * group_steps + k].astype(jnp.float32)
            diagonal = known[:, 3 * k + 2 : 3 * k + 3]
            first = jnp.where(row >= lane, pair, 0.0)
            second = jnp.where(row > lane, pair.T, jnp.where(row == lane, diagonal, 0.0))
            for at, part in ((0, first), (1, second)):
                product = jnp.dot(
                    part.astype(jnp.bfloat16), vtop[g], preferred_element_type=jnp.float32
                )
                start = pl.multiple_of(g * group_cols, group_cols) + (2 * k + at) * DH
                cols = pl.ds(pl.multiple_of(start, DH), DH)
                top[:, cols] = (product / known[:, 3 * k + at : 3 * k + at + 1]).astype(top.dtype)

    def send_q():
        pl.when(packs)(lambda: moved_low_q().start())
        pl.when(jnp.logical_not(packs))(lambda: moved_q().start())

    @pl.when(ends)
    def _():
        pl.semaphore_wait(barrier, 1)
        send_q()

    pl.when((core == 1) | (ctx >= 2))(lambda: greet(hall, sibling))
    met = jnp.where((core == 0) | (ctx >= 2), 1, 0)
    for d in range(2, window, 2):
        pl.when(ctx >= d)(lambda d=d: greet(hall, lax.rem(ctx + n_ctx - d, n_ctx)))
        met = met + jnp.where(ctx + d < n_ctx, 1, 0)
    for helped, helper, _ in HELPED:
        pl.when(ctx == helper)(lambda helped=helped: greet(hall, helped))
        met = met + jnp.where(ctx == helped, 1, 0)
    met = 1 + jnp.where(guides, 2 * met, met)
    doc_copy = pltpu.make_async_copy(doc_hbm, doc_ref, doc_sem)
    doc_copy.start()

    def fetch_own():
        for g in range(HK):
            for copy in own_copies(g):
                copy.start()
        q_copy.start()

    def fill_bias():
        doc_copy.wait()
        bias[0] = jnp.zeros(bias.shape[1:], jnp.float32)
        own_doc = doc_ref[0, ctx]
        for d in range(window):
            block = jnp.maximum(ctx - d, 0)
            seen = (doc_ref[0, block] == own_doc) & (ctx >= d)
            bias[0, d : d + 1, :] = jnp.full((1, DH), jnp.where(seen, 0.0, HIDDEN), jnp.float32)

    @pl.when(jnp.logical_not(ends))
    def _():
        fetch_own()
        fill_bias()

    @pl.when(jnp.logical_not(ends))
    def _():
        pl.semaphore_wait(barrier, met)
        send_q()

    pl.when(packs)(qtop_copy.start)

    @pl.when(guides)
    def _():
        pl.semaphore_signal(go_sem, inc=1, device_id=(right, ctx), device_id_type=MESH)

    @pl.when(ends)
    def _():
        fetch_own()
        fill_bias()

    all_own().wait()
    moved_kv().start()
    moved_bias().start()
    pl.when(packs)(lambda: vtop_copy().start())
    pl.when(ends)(lambda: pl.semaphore_wait(go_sem, 1))

    def start_direct(g):
        if g == moved:
            to_right(lent_rows, lent_rows, 0).wait_recv()
        for d in range(2, window, 2):
            pl.when(ctx + d < n_ctx)(lambda d=d: kv_copy(g, 0, d, lax.rem(ctx + d, n_ctx), d // 2).start())

    def pass_on(g):
        pl.when(relays(0))(lambda: kv_copy(g, 0, 1, sibling, 0).start())
        for d in range(2, window, 2):
            pl.when(ctx >= d)(functools.partial(wait_block, g, d))
            pl.when(relays(d))(lambda d=d: kv_copy(g, d, d + turn, sibling, 0).start())

    def end_gather(g):
        for d in range(1, window, 2):
            fits = (ctx >= d) & (ctx < d + 2) if d + 2 < window else ctx >= d

            @pl.when(fits)
            def _(d=d):
                blocks = kvbuf.at[g, :, pl.ds(0, (d + 1) // 2 * rows)]
                pltpu.make_async_copy(blocks, blocks, kv_recv.at[g, 0]).wait()

    start_direct(0)

    @pl.when(packs)
    def _():
        qbuf[:TOP, moved_cols] = jnp.zeros((TOP, group_cols), qbuf.dtype)

    for d in range(1, window):

        @pl.when(ctx < d)
        def _():
            place = pl.ds((last - d) * rows, rows)
            for g in range(HK):
                for which in range(2):
                    kvbuf[g, which, place, :] = jnp.zeros((rows, DH), kvbuf.dtype)

    pass_on(0)
    start_direct(1)
    q_copy.wait()

    @pl.loop(0, steps)
    def _(step):
        g = step // group_steps

        @pl.when(lax.rem(step, group_steps) == 0)
        def _():
            pl.when((g == moved) & packs)(lambda: moved_low_q().wait_recv())
            pl.when((g == moved) & jnp.logical_not(packs))(lambda: moved_q().wait_recv())
            end_gather(g)

        @pl.when(step == 3)
        def _():
            pass_on(1)
            start_direct(2)

        @pl.when(step == 7)
        def _():
            pass_on(2)
            start_direct(3)

        @pl.when(step == 11)
        def _():
            pass_on(3)

        which = jnp.where(g == moved, 1, 0)
        causal = lax.broadcasted_iota(jnp.int32, (rows, rows), 0) >= lax.broadcasted_iota(
            jnp.int32, (rows, rows), 1
        )
        for at in range(STEP_HEADS):
            cols = pl.ds(pl.multiple_of(step * step_cols + at * DH, DH), DH)
            query = qbuf[:, cols]
            scores = []
            top = None
            for d in range(window):
                place = pl.ds((last - d) * rows, rows)
                part = lax.dot_general(
                    query,
                    kvbuf[g, 0, place, :],
                    (((1,), (1,)), ((), ())),
                    preferred_element_type=jnp.float32,
                )
                if d == 0:
                    part = jnp.where(causal, part, -HIDDEN)
                scores.append(part)
                lanes = part[:, :DH]
                for c in range(1, rows // DH):
                    lanes = jnp.maximum(lanes, part[:, c * DH : (c + 1) * DH])
                if d > 0:
                    lanes = lanes - bias[which, d : d + 1, :]
                top = lanes if top is None else jnp.maximum(top, lanes)
            row_top = jnp.broadcast_to(jnp.max(top, axis=1, keepdims=True), (rows, DH))
            total = None
            acc = None
            for d in range(window):
                place = pl.ds((last - d) * rows, rows)
                offset = row_top
                if d > 0:
                    offset = row_top + bias[which, d : d + 1, :]
                rounded = []
                for c in range(rows // DH):
                    lanes = jnp.exp2((scores[d][:, c * DH : (c + 1) * DH] - offset) * factor)
                    total = lanes if total is None else total + lanes
                    if d == 0 and c == 0:
                        weights[at] = lanes[:TOP]
                    rounded.append(lanes.astype(jnp.bfloat16))
                product = jnp.dot(
                    jnp.concatenate(rounded, axis=1),
                    kvbuf[g, 1, place, :],
                    preferred_element_type=jnp.float32,
                )
                acc = product if acc is None else acc + product
            row_total = jnp.sum(total, axis=1, keepdims=True)
            sums[at] = jnp.broadcast_to(row_total[:TOP], (TOP, TOP))
            obuf[:, cols] = (acc / row_total).astype(obuf.dtype)

        done = pl.ds(pl.multiple_of(step * step_cols, step_cols), step_cols)

        later = lax.rem(step, 2) == 1
        pair = pl.ds(pl.multiple_of((step - lax.rem(step, 2)) * step_cols, 2 * step_cols), 2 * step_cols)

        @pl.when((step < group_steps) & jnp.logical_not(packs | (spreads & (step == SPREAD_STEP))))
        def _():
            out_copy(done).start()

        @pl.when((step >= group_steps) & (g < moved) & later & jnp.logical_not(packs))
        def _():
            out_copy(pair).start()

        @pl.when((g < moved) & packs)
        def _():
            pack(step)
            pl.when(step < group_steps)(lambda: half_copy(done).start())
            pl.when((step >= group_steps) & later)(lambda: half_copy(pair).start())

            @pl.when(lax.rem(step, group_steps) == group_steps - 1)
            def _():
                hand_packed(g)

            @pl.when(step == group_steps - 1)
            def _():
                qtop_copy.wait()

                @pl.loop(0, group_steps)
                def _(k):
                    pack_moved(k)

                hand_packed(moved)

        @pl.when(spreads & (step == SPREAD_STEP))
        def _():
            for helped, helper, slot in HELPED:
                pl.when(ctx == helped)(lambda to=(helper, slot): to_helper(*to).start())
            rest_copy().start()

        for helped, helper, slot in HELPED:

            @pl.when((ctx == helper) & (step == SPREAD_LATER))
            def _(helped=helped, helper=helper, slot=slot):
                to_helper(helper, slot).wait_recv()
                from_helper(helped, slot).start()

        pl.when((g == moved) & packs)(lambda: half_local(done).start())
        pl.when((g == moved) & jnp.logical_not(packs))(lambda: out_local(done).start())

    to_right(lent_rows, lent_rows, 0).wait_send()

    for count in range(1, window + 1):

        @pl.when(sends == count)
        def _(count=count):
            blocks = kvbuf.at[:, :, pl.ds(0, count * rows)]
            pltpu.make_async_copy(blocks, blocks, kv_send).wait()

    for helped, helper, slot in HELPED:
        pl.when(ctx == helper)(lambda by=(helped, slot): from_helper(*by).wait_send())

    @pl.when(packs)
    def _():
        vtop[moved] = kvbuf[moved, 1, pl.ds(last * rows, TOP), :]
        lines = group_steps * TOP + 32

        @pl.loop(0, HK)
        def _(g):
            for first, count in ((True, lines + moved * TOP), (False, lines)):

                @pl.when((g == 0) == first)
                def _(count=count):
                    arrived = kvbuf.at[0, 0, pl.ds(0, count)]
                    pltpu.make_async_copy(arrived, arrived, y_recv.at[g]).wait()

            unpack(g)
            top_copy(g).start()

        pltpu.make_async_copy(top, out_ref.at[pl.ds(0, TOP)], t_sem).wait()

    @pl.when(packs)
    def _():
        vtop_copy().wait_send()
        to_top(packed, tiles_in, q_sem, y_recv.at[0]).wait_send()
        sent = facts.at[:, pl.ds(0, 16)]
        to_top(sent, sent, doc_sem, y_recv.at[0]).wait_send()

    whole = pl.ds(0, HQ * DH)
    lower = pl.ds(0, HQ * DH * (rows - TOP) // rows)
    pl.when(packs)(lambda: out_copy(lower).wait_send())
    pl.when(jnp.logical_not(packs))(lambda: out_copy(whole).wait_send())
    pl.when(packs)(lambda: out_copy(lower).wait_recv())
    pl.when(jnp.logical_not(packs))(lambda: out_copy(whole).wait_recv())


def shards(n_pipe, n_ctx, queries, keys, values, doc_ids):
    rows = queries.shape[1]
    window = n_ctx // 2 + 1
    bias_rows = (window + 7) // 8 * 8
    dma = pltpu.SemaphoreType.DMA
    anywhere = pl.BlockSpec(memory_space=pl.ANY)
    handed = pl.pallas_call(
        functools.partial(kernel, n_pipe, n_ctx, window, rows),
        out_shape=jax.ShapeDtypeStruct((rows, HQ * DH), jnp.bfloat16),
        in_specs=[pl.BlockSpec(memory_space=pltpu.HBM)] * 4,
        out_specs=anywhere,
        scratch_shapes=[
            pltpu.VMEM((rows, HQ * DH), jnp.bfloat16),
            pltpu.VMEM((HK, 2, window * rows, DH), jnp.bfloat16),
            pltpu.VMEM((rows, HQ * DH), jnp.bfloat16),
            pltpu.VMEM((2, bias_rows, DH), jnp.float32),
            pltpu.SMEM(doc_ids.shape, jnp.int32),
            pltpu.VMEM((2, SPREAD_ROWS, STEP_HEADS * DH), jnp.bfloat16),
            pltpu.VMEM((2, rows, DH), jnp.bfloat16),
            pltpu.VMEM((STEP_HEADS, TOP, TOP), jnp.float32),
            pltpu.VMEM((STEP_HEADS, TOP, TOP), jnp.float32),
            pltpu.VMEM((TOP, TOP), jnp.float32),
            pltpu.VMEM((HQ // STEP_HEADS, TOP, TOP), jnp.bfloat16),
            pltpu.VMEM((HK, TOP, TOP), jnp.float32),
            pltpu.VMEM((HQ // STEP_HEADS, TOP, TOP), jnp.bfloat16),
            pltpu.VMEM((HK, TOP, TOP), jnp.float32),
            pltpu.VMEM((HK, TOP, DH), jnp.bfloat16),
            pltpu.VMEM((TOP, PER_GROUP * DH), jnp.bfloat16),
            pltpu.VMEM((TOP, HQ * DH), jnp.bfloat16),
            dma,
            dma,
            dma,
            dma,
            dma((HK, 1 + (window - 1) // 2)),
            dma,
            dma((2,)),
            dma,
            dma,
            dma((2,)),
            dma((2,)),
            dma((HK,)),
            dma,
            pltpu.SemaphoreType.REGULAR,
        ],
        compiler_params=pltpu.CompilerParams(
            collective_id=0, has_side_effects=True, vmem_limit_bytes=48 * 1024 * 1024
        ),
        name="relay_attention",
    )(*(pltpu.with_memory_space_constraint(x, pltpu.HBM) for x in (doc_ids, queries[0], keys[0], values[0])))
    return handed[None]


def solution(mesh):
    placed = (
        P("pipe", "ctx", None),
        P("pipe", "ctx", None),
        P("pipe", "ctx", None),
        P("pipe", None),
    )
    return jax.shard_map(
        functools.partial(shards, mesh.shape["pipe"], mesh.shape["ctx"]),
        mesh=mesh,
        in_specs=placed,
        out_specs=P("pipe", "ctx", None),
        check_vma=False,
    )
```
